32 devices in a mesh: dp: 8 (over y, x, core), shard: 4 (over z).
Axes of the slice: x: 2, y: 2, z: 4, core: 2. Of those that a mesh axis runs over, the one named last changes fastest.
Arguments:
- hidden_in: float32 [16384, 1536], P(('dp', 'shard')), may hold values from -6 to 6
- cotangent: float32 [16384, 1536], P(('dp', 'shard')), may hold values from -6 to 6
- segment_ids: int32 [16384], P(('dp', 'shard')), may hold values from 0 to 31, as said below
- param_prenorm: float32 [1536], replicated, may hold values from 0.5 to 1.5
- param_inputs: float32 [1536, 6448], P(('dp', 'shard')), may hold values from -0.15625 to 0.15625
- param_kernel: float32 [4, 3328], replicated, may hold values from -3 to 3
- param_offsets: float32 [3328], replicated, may hold values from -0.5 to 0.5
- param_timestep: float32 [48], replicated, may hold values from -7 to -3
- param_decays: float32 [48], replicated, may hold values from 0 to 2.5
- param_direct: float32 [48], replicated, may hold values from 0.5 to 1.5
- param_gating: float32 [3072], replicated, may hold values from 0.5 to 1.5
- param_outputs: float32 [3072, 1536], P(('dp', 'shard')), may hold values from -0.15625 to 0.15625
- moment_prenorm: float32 [1536], replicated, may hold values from -3 to 3
- moment_inputs: float32 [1536, 6448], P(('dp', 'shard')), may hold values from -3 to 3
- moment_kernel: float32 [4, 3328], replicated, may hold values from -3 to 3
- moment_offsets: float32 [3328], replicated, may hold values from -3 to 3
- moment_timestep: float32 [48], replicated, may hold values from -3 to 3
- moment_decays: float32 [48], replicated, may hold values from -3 to 3
- moment_direct: float32 [48], replicated, may hold values from -3 to 3
- moment_gating: float32 [3072], replicated, may hold values from -3 to 3
- moment_outputs: float32 [3072, 1536], P(('dp', 'shard')), may hold values from -3 to 3
- square_prenorm: float32 [1536], replicated, may hold values from 0.01 to 1
- square_inputs: float32 [1536, 6448], P(('dp', 'shard')), may hold values from 0.01 to 1
- square_kernel: float32 [4, 3328], replicated, may hold values from 0.01 to 1
- square_offsets: float32 [3328], replicated, may hold values from 0.01 to 1
- square_timestep: float32 [48], replicated, may hold values from 0.01 to 1
- square_decays: float32 [48], replicated, may hold values from 0.01 to 1
- square_direct: float32 [48], replicated, may hold values from 128 to 8192
- square_gating: float32 [3072], replicated, may hold values from 0.01 to 1
- square_outputs: float32 [3072, 1536], P(('dp', 'shard')), may hold values from 0.01 to 1
Outputs:
- block_out: float32 [16384, 1536], P(('dp', 'shard'))
- hidden_grad: float32 [16384, 1536], P(('dp', 'shard'))
- grad_prenorm: float32 [1536], replicated
- grad_inputs: float32 [1536, 6448], P(('dp', 'shard'))
- grad_kernel: float32 [4, 3328], replicated
- grad_offsets: float32 [3328], replicated
- grad_timestep: float32 [48], replicated
- grad_decays: float32 [48], replicated
- grad_direct: float32 [48], replicated
- grad_gating: float32 [3072], replicated
- grad_outputs: float32 [3072, 1536], P(('dp', 'shard'))
- newparam_prenorm: float32 [1536], replicated
- newparam_inputs: float32 [1536, 6448], P(('dp', 'shard'))
- newparam_kernel: float32 [4, 3328], replicated
- newparam_offsets: float32 [3328], replicated
- newparam_timestep: float32 [48], replicated
- newparam_decays: float32 [48], replicated
- newparam_direct: float32 [48], replicated
- newparam_gating: float32 [3072], replicated
- newparam_outputs: float32 [3072, 1536], P(('dp', 'shard'))
- newmoment_prenorm: float32 [1536], replicated
- newmoment_inputs: float32 [1536, 6448], P(('dp', 'shard'))
- newmoment_kernel: float32 [4, 3328], replicated
- newmoment_offsets: float32 [3328], replicated
- newmoment_timestep: float32 [48], replicated
- newmoment_decays: float32 [48], replicated
- newmoment_direct: float32 [48], replicated
- newmoment_gating: float32 [3072], replicated
- newmoment_outputs: float32 [3072, 1536], P(('dp', 'shard'))
- newsquare_prenorm: float32 [1536], replicated
- newsquare_inputs: float32 [1536, 6448], P(('dp', 'shard'))
- newsquare_kernel: float32 [4, 3328], replicated
- newsquare_offsets: float32 [3328], replicated
- newsquare_timestep: float32 [48], replicated
- newsquare_decays: float32 [48], replicated
- newsquare_direct: float32 [48], replicated
- newsquare_gating: float32 [3072], replicated
- newsquare_outputs: float32 [3072, 1536], P(('dp', 'shard'))
The draws below stay inside these ranges and needn't reach their ends.
Inputs may be any that keep to these rules, and one draw needn't show every extreme that they name: `segment_ids`: segment ids never fall along the tokens, begin at 0, and each packed sequence of 2048 tokens holds exactly 4 documents of its own, each of at least 204 tokens, so that no document crosses from one packed sequence into the next.
All inputs are finite; a program needn't handle non-finite values.
Results may differ from the reference program's by a relative error of at most 0.0055.
The reference program's roundings to bfloat16 on the way count: a program that leaves them out, or rounds other values in their place, can miss the bound.
Values may be sent and summed in bfloat16 or wider, within the bound.
No kernel may reach another device: no remote copies, remote signals or barrier semaphores. Data moves between devices by JAX's collectives and lax.ppermute only.
A program may use at most 320 MiB of HBM per device.

```python
import math
import jax
import jax.numpy as jnp
from jax import lax

D = 1536
HEADS = 48
HEAD_DIM = 64
STATE = 128
KW = 4
BLOCK = 256
SEQ_LEN = 2048
ADAM_STEP = 10
DI = 3072
CH = 3328
PROJ = 6448
TOKENS = 16384


def draw_segment_ids(key, part):
    seq_total = TOKENS // SEQ_LEN
    seq_keys = jax.random.split(key, seq_total)
    least = SEQ_LEN // 10
    spare = SEQ_LEN - 4 * least

    def sequence_marks(seq_key):
        shuffled = jax.random.permutation(seq_key, spare + 3)
        chosen = jnp.sort(shuffled[:3])
        cut_points = (jnp.arange(3) + 1) * least + chosen - jnp.arange(3)
        offsets = jnp.arange(SEQ_LEN)
        hits = jnp.any(offsets[:, None] == cut_points[None, :], axis=1)
        begins_here = jnp.logical_or(hits, offsets == 0)
        return begins_here.astype(jnp.int32)
    begins = jax.vmap(sequence_marks)(seq_keys).reshape(TOKENS)
    return (jnp.cumsum(begins) - 1).astype(jnp.int32)


def strengthened(entries, own_key, source, target, blocks, factor):
    def block_of(dim):
        return (jnp.arange(entries.shape[dim]) // (entries.shape[dim] // blocks)).reshape((-1,) + (1,) * (entries.ndim - 1 - dim))

    near = jax.random.permutation(own_key, blocks)[block_of(target)]
    second = (block_of(target) + blocks // 2) % blocks
    return jnp.where((block_of(source) == near) | (block_of(source) == second), factor * entries, entries)


def level_of(rng, shape, cuts, low, high):
    factor_of = 1.0
    for dim, parts in cuts:
        steps = jax.random.uniform(jax.random.fold_in(jax.random.fold_in(rng, 6), dim), (parts,), jnp.float32, low / len(cuts), high / len(cuts))
        factor_of = factor_of * jnp.repeat(jnp.exp(steps), shape[dim] // parts).reshape((-1,) + (1,) * (len(shape) - 1 - dim))
    return factor_of


def centred(rng, dims, scale, reach, cuts=(), held_as=jnp.bfloat16):
    factor_of = level_of(rng, dims, cuts, -0.22, 0.18) if cuts else 1.0
    drawn = jax.random.normal(rng, dims, jnp.float32) * scale * factor_of
    return jnp.minimum(jnp.maximum(drawn, -reach), reach).astype(held_as)


def bell_draw_with(stream_key, dims, scale, reach, cuts, heavy, held_as=jnp.bfloat16):
    drawn = scale * jax.random.normal(stream_key, dims, jnp.float32)
    if cuts:
        drawn = drawn * level_of(stream_key, dims, cuts, -0.22, 0.18)
    return jnp.clip(strengthened(drawn, jax.random.fold_in(stream_key, 3), *heavy), -reach, reach).astype(held_as)


def setup_inputs(seed: int = 0) -> dict:
    arg_keys = jax.random.split(jax.random.key(seed), 31)
    return {
        "hidden_in": bell_draw_with(arg_keys[0], (TOKENS, D), 1.0, 6.0, ((0, 32),), (0, 1, 32, 2.75), jnp.float32),
        "cotangent": centred(arg_keys[1], (TOKENS, D), 1.0, 6.0, ((0, 32),), jnp.float32),
        "segment_ids": draw_segment_ids(jax.random.fold_in(arg_keys[30], 71), 0),
        "param_prenorm": jnp.clip(1.0 + 0.1 * jax.random.normal(arg_keys[3], (D,), jnp.float32), 0.5, 1.5),
        "param_inputs": centred(arg_keys[4], (D, PROJ), D ** -0.5, 0.15625, ((0, 32),), jnp.float32),
        "param_kernel": centred(arg_keys[5], (KW, CH), KW ** -0.5, 3.0, (), jnp.float32),
        "param_offsets": jnp.clip(jax.random.uniform(arg_keys[6], (CH,), jnp.float32, -0.5, 0.5), -0.5, 0.5),
        "param_timestep": jnp.clip(jax.random.uniform(arg_keys[7], (HEADS,), jnp.float32, -7.0, -3.0), -7.0, -3.0),
        "param_decays": jnp.clip(jax.random.uniform(arg_keys[8], (HEADS,), jnp.float32, 0.0, 2.5), 0.0, 2.5),
        "param_direct": jnp.clip(jax.random.uniform(arg_keys[9], (HEADS,), jnp.float32, 0.5, 1.5), 0.5, 1.5),
        "param_gating": jnp.clip(1.0 + 0.1 * jax.random.normal(arg_keys[10], (DI,), jnp.float32), 0.5, 1.5),
        "param_outputs": centred(arg_keys[11], (DI, D), (DI // 2) ** -0.5, 0.15625, ((0, 32),), jnp.float32),
        "moment_prenorm": centred(arg_keys[12], (D,), 0.5, 3.0, (), jnp.float32),
        "moment_inputs": centred(arg_keys[13], (D, PROJ), 0.5, 3.0, ((0, 32),), jnp.float32),
        "moment_kernel": centred(arg_keys[14], (KW, CH), 0.5, 3.0, (), jnp.float32),
        "moment_offsets": centred(arg_keys[15], (CH,), 0.5, 3.0, (), jnp.float32),
        "moment_timestep": centred(arg_keys[16], (HEADS,), 0.5, 3.0, (), jnp.float32),
        "moment_decays": centred(arg_keys[17], (HEADS,), 0.5, 3.0, (), jnp.float32),
        "moment_direct": centred(arg_keys[18], (HEADS,), 0.5, 3.0, (), jnp.float32),
        "moment_gating": centred(arg_keys[19], (DI,), 0.5, 3.0, (), jnp.float32),
        "moment_outputs": centred(arg_keys[20], (DI, D), 0.5, 3.0, ((0, 32),), jnp.float32),
        "square_prenorm": jnp.clip(jnp.exp(jax.random.uniform(arg_keys[21], (D,), jnp.float32, math.log(0.01), math.log(1.0))), 0.01, 1.0),
        "square_inputs": jnp.clip(jnp.exp(math.log(1.0) - 4.6051702 * jax.random.uniform(arg_keys[22], (D, PROJ), jnp.float32) ** level_of(arg_keys[22], (D, PROJ), ((0, 32),), -0.2, 0.2)), 0.01, 1.0),
        "square_kernel": jnp.clip(jnp.exp(jax.random.uniform(arg_keys[23], (KW, CH), jnp.float32, math.log(0.01), math.log(1.0))), 0.01, 1.0),
        "square_offsets": jnp.clip(jnp.exp(jax.random.uniform(arg_keys[24], (CH,), jnp.float32, math.log(0.01), math.log(1.0))), 0.01, 1.0),
        "square_timestep": jnp.clip(jnp.exp(jax.random.uniform(arg_keys[25], (HEADS,), jnp.float32, math.log(0.01), math.log(1.0))), 0.01, 1.0),
        "square_decays": jnp.clip(jnp.exp(jax.random.uniform(arg_keys[26], (HEADS,), jnp.float32, math.log(0.01), math.log(1.0))), 0.01, 1.0),
        "square_direct": jnp.clip(jnp.exp(jax.random.uniform(arg_keys[27], (HEADS,), jnp.float32, math.log(128.0), math.log(8192.0))), 128.0, 8192.0),
        "square_gating": jnp.clip(jnp.exp(jax.random.uniform(arg_keys[28], (DI,), jnp.float32, math.log(0.01), math.log(1.0))), 0.01, 1.0),
        "square_outputs": jnp.clip(jnp.exp(math.log(1.0) - 4.6051702 * jax.random.uniform(arg_keys[29], (DI, D), jnp.float32) ** level_of(arg_keys[29], (DI, D), ((0, 32),), -0.2, 0.2)), 0.01, 1.0),
    }


norm_eps = 1e-05
beta_one = 0.9
beta_two = 0.95
adam_eps = 1e-08
highest = lax.Precision.HIGHEST
rate_table = (0.2, 0.01, 0.2, 0.2, 0.2, 0.2, 0.2, 0.2, 0.01)
shrink_table = (0.0, 0.1, 0.1, 0.0, 0.0, 0.0, 0.0, 0.0, 0.1)

def pre_norm(hidden, norm_gain):
    inv_rms = lax.rsqrt(lax.optimization_barrier(jnp.mean(hidden * hidden, axis=1, keepdims=True)) + norm_eps)
    return hidden * inv_rms * norm_gain

def gated_norm(output, gate_in, gating):
    gated_rows = output * jax.nn.silu(gate_in)
    inv_rms = lax.rsqrt(lax.optimization_barrier(jnp.mean(gated_rows * gated_rows, axis=1, keepdims=True)) + norm_eps)
    return gated_rows * inv_rms * gating

def conv_mix(conv_in, rim_rows, seg_float, rim_segs, kernel, offsets):
    rim_count = rim_rows.shape[0]
    length = conv_in.shape[0]
    padded = jnp.concatenate([rim_rows, conv_in], axis=0)
    all_segs = jnp.concatenate([rim_segs, seg_float], axis=0)
    summed = jnp.zeros_like(conv_in) + offsets[None, :]
    for tap_index in range(rim_count + 1):
        matches = (all_segs[tap_index:tap_index + length] == seg_float).astype(jnp.float32)
        summed = summed + kernel[tap_index][None, :] * padded[tap_index:tap_index + length] * matches[:, None]
    return jax.nn.silu(summed)

def block_step(carried, pieces):
    values, keys_mat, query_mat, deltas, log_decay, seg_float, starts = pieces
    cumulative = jnp.cumsum(log_decay, axis=0)
    count_rows = values.shape[0]
    position = jnp.arange(count_rows)
    allowed = (seg_float[:, None] == seg_float[None, :]) & (position[:, None] >= position[None, :])
    allowed_cube = allowed[:, :, None]
    log_gaps = jnp.where(allowed_cube, cumulative[:, None, :] - cumulative[None, :, :], 0.0)
    decay_mat = jnp.where(allowed_cube, jnp.exp(log_gaps), 0.0)
    scores = jnp.dot(query_mat, keys_mat.T, precision=highest)
    mixing = scores[:, :, None] * decay_mat * deltas[None, :, :]
    local_out = jnp.einsum('tsh,shp->thp', mixing, values, precision=highest)
    alive_mask = (seg_float == seg_float[0]).astype(jnp.float32) * (1.0 - starts[0])
    inflow = jnp.exp(cumulative) * alive_mask[:, None]
    carry_out = jnp.einsum('tn,hpn->thp', query_mat, carried, precision=highest) * inflow[:, :, None]
    ending = (seg_float == seg_float[count_rows - 1]).astype(jnp.float32)
    tail_weight = jnp.exp(cumulative[count_rows - 1][None, :] - cumulative) * ending[:, None] * deltas
    weighted = values * tail_weight[:, :, None]
    fresh_state = jnp.einsum('shp,sn->hpn', weighted, keys_mat, precision=highest)
    keep_factor = jnp.exp(cumulative[count_rows - 1]) * alive_mask[count_rows - 1]
    carried_new = carried * keep_factor[:, None, None] + fresh_state
    return (carried_new, local_out + carry_out)

def scan_blocks(values, keys_mat, query_mat, deltas, log_decay, seg_float, starts, initial):
    block_count = values.shape[0] // BLOCK

    def shaped(array):
        return array.reshape((block_count, BLOCK) + array.shape[1:])
    pieces = (shaped(values), shaped(keys_mat), shaped(query_mat), shaped(deltas), shaped(log_decay), shaped(seg_float), shaped(starts))
    final_state, block_outs = lax.scan(block_step, initial, pieces)
    return (final_state, block_outs.reshape(values.shape))

def middle(projected, seg_float, starts, kernel, offsets, timestep, decays, direct, gating):
    length = projected.shape[0]
    gate_in = projected[:, :DI]
    rim_rows = jnp.zeros((KW - 1, CH), jnp.float32)
    rim_segs = jnp.full((KW - 1,), -1.0, jnp.float32)
    mixed = conv_mix(projected[:, DI:DI + CH], rim_rows, seg_float, rim_segs, kernel, offsets)
    values = mixed[:, :DI].reshape(length, HEADS, HEAD_DIM)
    keys_mat = mixed[:, DI:DI + STATE]
    query_mat = mixed[:, DI + STATE:]
    deltas = jax.nn.softplus(projected[:, DI + CH:] + timestep)
    log_decay = -deltas * jnp.exp(decays)
    initial = jnp.zeros((HEADS, HEAD_DIM, STATE), jnp.float32)
    final_state, mixer_out = scan_blocks(values, keys_mat, query_mat, deltas, log_decay, seg_float, starts, initial)
    mixer_out = mixer_out + direct[None, :, None] * values
    return gated_norm(mixer_out.reshape(length, DI), gate_in, gating)

def adamw(param, grad, moment, square, rate, shrink):
    moment_new = beta_one * moment + (1.0 - beta_one) * grad
    square_new = beta_two * square + (1.0 - beta_two) * grad * grad
    first_corr = 1.0 - beta_one ** ADAM_STEP
    second_corr = 1.0 - beta_two ** ADAM_STEP
    update = moment_new / first_corr / (jnp.sqrt(square_new / second_corr) + adam_eps)
    return (param - rate * (update + shrink * param), moment_new, square_new)

def reference(hidden_in, cotangent, segment_ids, param_prenorm, param_inputs, param_kernel, param_offsets, param_timestep, param_decays, param_direct, param_gating, param_outputs, moment_prenorm, moment_inputs, moment_kernel, moment_offsets, moment_timestep, moment_decays, moment_direct, moment_gating, moment_outputs, square_prenorm, square_inputs, square_kernel, square_offsets, square_timestep, square_decays, square_direct, square_gating, square_outputs):
    input_half = param_inputs.astype(jnp.bfloat16)
    output_half = param_outputs.astype(jnp.bfloat16)
    seg_float = segment_ids.astype(jnp.float32)
    previous = jnp.concatenate([jnp.full((1,), -1.0, jnp.float32), seg_float[:-1]])
    starts = (seg_float != previous).astype(jnp.float32)
    smalls = (param_kernel, param_offsets, param_timestep, param_decays, param_direct, param_gating)
    seq_count = hidden_in.shape[0] // SEQ_LEN

    def shaped(array):
        return array.reshape((seq_count, SEQ_LEN) + array.shape[1:])

    def per_sequence(totals, pieces):
        grad_in_sum, grad_out_sum, prenorm_sum, small_sums = totals
        rows_in, rows_cot, rows_seg, rows_start = pieces
        normed, norm_back = jax.vjp(pre_norm, rows_in, param_prenorm)
        normed_half = normed.astype(jnp.bfloat16)
        projected = jnp.dot(normed_half, input_half, preferred_element_type=jnp.float32)

        def mapping(proj_rows, small_params):
            return middle(proj_rows, rows_seg, rows_start, small_params[0], small_params[1], small_params[2], small_params[3], small_params[4], small_params[5])
        gated_full, middle_back = jax.vjp(mapping, projected, smalls)
        gated_half = gated_full.astype(jnp.bfloat16)
        block_rows = rows_in + jnp.dot(gated_half, output_half, preferred_element_type=jnp.float32)
        upstream_half = rows_cot.astype(jnp.bfloat16)
        back_gated = jnp.dot(upstream_half, output_half.T, preferred_element_type=jnp.float32)
        grad_out_part = jnp.dot(gated_half.T, upstream_half, preferred_element_type=jnp.float32)
        back_projected, back_smalls = middle_back(back_gated)
        back_half = back_projected.astype(jnp.bfloat16)
        back_normed = jnp.dot(back_half, input_half.T, preferred_element_type=jnp.float32)
        grad_in_part = jnp.dot(normed_half.T, back_half, preferred_element_type=jnp.float32)
        back_hidden, back_prenorm = norm_back(back_normed)
        totals_new = (grad_in_sum + grad_in_part, grad_out_sum + grad_out_part, prenorm_sum + back_prenorm, jax.tree.map(jnp.add, small_sums, back_smalls))
        return (totals_new, (block_rows, rows_cot + back_hidden))
    zeros_small = jax.tree.map(lambda member: jnp.zeros(member.shape, jnp.float32), smalls)
    initial = (jnp.zeros(param_inputs.shape, jnp.float32), jnp.zeros(param_outputs.shape, jnp.float32), jnp.zeros(param_prenorm.shape, jnp.float32), zeros_small)
    totals, results = lax.scan(per_sequence, initial, (shaped(hidden_in), shaped(cotangent), shaped(seg_float), shaped(starts)))
    block_out = results[0].reshape(hidden_in.shape)
    hidden_grad = results[1].reshape(hidden_in.shape)
    grad_inputs, grad_outputs, grad_prenorm, small_grads = totals
    params = (param_prenorm, param_inputs, param_kernel, param_offsets, param_timestep, param_decays, param_direct, param_gating, param_outputs)
    moments = (moment_prenorm, moment_inputs, moment_kernel, moment_offsets, moment_timestep, moment_decays, moment_direct, moment_gating, moment_outputs)
    squares = (square_prenorm, square_inputs, square_kernel, square_offsets, square_timestep, square_decays, square_direct, square_gating, square_outputs)
    grads = (grad_prenorm, grad_inputs, small_grads[0], small_grads[1], small_grads[2], small_grads[3], small_grads[4], small_grads[5], grad_outputs)
    updated = [adamw(params[member_index], grads[member_index], moments[member_index], squares[member_index], rate_table[member_index], shrink_table[member_index]) for member_index in range(9)]
    return (block_out, hidden_grad, grads[0], grads[1], grads[2], grads[3], grads[4], grads[5], grads[6], grads[7], grads[8], updated[0][0], updated[1][0], updated[2][0], updated[3][0], updated[4][0], updated[5][0], updated[6][0], updated[7][0], updated[8][0], updated[0][1], updated[1][1], updated[2][1], updated[3][1], updated[4][1], updated[5][1], updated[6][1], updated[7][1], updated[8][1], updated[0][2], updated[1][2], updated[2][2], updated[3][2], updated[4][2], updated[5][2], updated[6][2], updated[7][2], updated[8][2])
```

```python
import functools

import jax
import jax.numpy as jnp
from jax import lax
from jax.experimental import pallas as pl
from jax.experimental.pallas import tpu as pltpu
from jax.sharding import PartitionSpec as P


HEADS = 48
HEAD_DIM = 64
STATE = 128
KW = 4
ADAM_STEP = 10
DI = 3072
CH = 3328

Q = 128
GH = 8
GW = GH * HEAD_DIM
NG = HEADS // GH
HALO = 8
TILE = 256

bf16 = jnp.bfloat16
f32 = jnp.float32
highest = lax.Precision.HIGHEST

norm_eps = 1e-05
beta_one = 0.9
beta_two = 0.95
adam_eps = 1e-08
rate_table = (0.2, 0.01, 0.2, 0.2, 0.2, 0.2, 0.2, 0.2, 0.01)
shrink_table = (0.0, 0.1, 0.1, 0.0, 0.0, 0.0, 0.0, 0.0, 0.1)

NN = (((1,), (0,)), ((), ()))
NT = (((1,), (1,)), ((), ()))


def halves(x):
    hi = x.astype(bf16)
    return hi, (x - hi.astype(f32)).astype(bf16)


def dot1(a, b, dims=NN):
    return lax.dot_general(a.astype(bf16), b.astype(bf16), dims, preferred_element_type=f32)


def dot3(a, b, dims=NN):
    ah, al = halves(a)
    bh, bl = halves(b)
    return dot1(ah, bh, dims) + (dot1(ah, bl, dims) + dot1(al, bh, dims))


def dotf(a, b, dims=NN):
    return lax.dot_general(a, b, dims, precision=highest, preferred_element_type=f32)


def iota(shape, dim):
    return lax.broadcasted_iota(jnp.int32, shape, dim)


def sigmoid(x):
    return 1.0 / (1.0 + jnp.exp(-x))


def softplus(x):
    u = jnp.exp(-jnp.abs(x))
    series = u * (1.0 - u * (0.5 - u * (1.0 / 3.0 - u * (0.25 - u * 0.2))))
    return jnp.maximum(x, 0.0) + jnp.where(u < 0.03, series, jnp.log(1.0 + u))


def pair_lanes(cols, j):
    rows = cols.shape[0]
    low = iota((rows, 128), 1) < HEAD_DIM
    return jnp.where(low, cols[:, 2 * j : 2 * j + 1], cols[:, 2 * j + 1 : 2 * j + 2])


def group_lanes(cols):
    return jnp.concatenate([pair_lanes(cols, j) for j in range(cols.shape[1] // 2)], axis=1)


def head_onehot():
    return (iota((HEADS, DI), 1) // HEAD_DIM == iota((HEADS, DI), 0)).astype(f32)


def params(limit=60000, **kw):
    return pltpu.CompilerParams(vmem_limit_bytes=limit * 1024, **kw)


def prep_kernel(
    step_ref, par_ref, mask_ref, delta_ref, cum_ref, cumt_ref, infc_ref, tailc_ref, tailn_ref,
    taild_ref, infd_ref, keep_ref, factor_ref,
):
    length = step_ref.shape[0]
    count = length // Q
    tri = (iota((Q, Q), 0) >= iota((Q, Q), 1)).astype(f32)
    eye = (iota((HEADS, HEADS), 0) == iota((HEADS, HEADS), 1)).astype(f32)
    rate = jnp.exp(par_ref[1:2, :])
    base = jnp.zeros((1, HEADS), f32)
    held = []
    keeps = []
    for c in range(count):
        rows = slice(c * Q, (c + 1) * Q)
        delta = softplus(step_ref[rows, :] + par_ref[0:1, :])
        cum = dotf(tri, -delta * rate)
        cumt_ref[:, rows] = dotf(eye, cum, NT)
        last = cum[Q - 1 : Q, :]
        alive, ending = mask_ref[rows, 0:1], mask_ref[rows, 1:2]
        infc = jnp.exp(cum) * alive
        tailn = jnp.exp(last - cum) * ending
        tailc = tailn * delta
        for g in range(NG):
            part = slice(g * GH, (g + 1) * GH)
            delta_ref[g, rows, :] = delta[:, part]
            cum_ref[g, rows, :] = cum[:, part]
            infc_ref[g, rows, :] = infc[:, part]
            tailn_ref[g, rows, :] = tailn[:, part]
            tailc_ref[g, rows, :] = tailc[:, part]
        keeps.append(infc[Q - 1 : Q, :])
        whole = cum + base
        infd_ref[rows, :] = jnp.exp(whole) * mask_ref[rows, 2:3]
        held.append((whole, delta))
        base = base + last
    for c in range(count):
        rows = slice(c * Q, (c + 1) * Q)
        whole, delta = held[c]
        taild = jnp.exp(base - whole) * mask_ref[rows, 3:4] * delta
        for g in range(NG):
            taild_ref[g, rows, :] = taild[:, g * GH : (g + 1) * GH]
    factor = jnp.exp(base) * mask_ref[length - 1 : length, 2:3]
    spread = head_onehot()
    line = iota((8, HEADS), 0)
    table = jnp.zeros((8, HEADS), f32)
    for c in range(count):
        table = jnp.where(line == c, keeps[c], table)
    keep_ref[...] = dotf(table, spread)
    factor_ref[...] = dotf(jnp.where(line == 0, factor, 0.0), spread)


def prep(step_raw, pars, mask):
    length = step_raw.shape[0]
    cols = jax.ShapeDtypeStruct((NG, length, GH), f32)
    wide = jax.ShapeDtypeStruct((8, DI), f32)
    return pl.pallas_call(
        prep_kernel,
        out_shape=(
            cols, cols, jax.ShapeDtypeStruct((HEADS, length), f32), cols, cols, cols, cols,
            jax.ShapeDtypeStruct((length, HEADS), f32), wide, wide,
        ),
        compiler_params=params(),
        cost_estimate=pl.CostEstimate(flops=10**7, bytes_accessed=10**7, transcendentals=10**5),
        name="prep",
    )(step_raw, pars, mask)


def conv_sum(x_ref, tap_ref, match_ref, start, rows, cols):
    total = tap_ref[KW : KW + 1, cols] + tap_ref[KW - 1 : KW, cols] * x_ref[
        pl.ds(HALO + start, rows), cols
    ]
    for k in range(KW - 1):
        taken = x_ref[pl.ds(HALO - (KW - 1) + k + start, rows), cols]
        total = total + tap_ref[k : k + 1, cols] * (taken * match_ref[k, pl.ds(start, rows), :])
    return total


def conv_kernel(
    xv_ref, xk_ref, tv_ref, tk_ref, match_ref, taild_ref, v_ref, kq_ref, state_ref, kt_hi, kt_lo
):
    length = v_ref.shape[0]
    count = length // Q

    @pl.when(pl.program_id(0) == 0)
    def _():
        for c in range(count):
            for j in range(2):
                cols = slice(128 * j, 128 * (j + 1))
                s = conv_sum(xk_ref, tk_ref, match_ref, c * Q, Q, cols)
                m = s * sigmoid(s)
                kq_ref[c * Q : (c + 1) * Q, cols] = m
                if j == 0:
                    hi, lo = halves(m.T)
                    kt_hi[:, c * Q : (c + 1) * Q] = hi
                    kt_lo[:, c * Q : (c + 1) * Q] = lo

    total = jnp.zeros((STATE, GW), f32)
    for c in range(count):
        rows = slice(c * Q, (c + 1) * Q)
        tail = taild_ref[0, rows, :]
        parts = []
        for j in range(GW // 128):
            cols = slice(128 * j, 128 * (j + 1))
            s = conv_sum(xv_ref, tv_ref, match_ref, c * Q, Q, cols)
            m = s * sigmoid(s)
            v_ref[rows, cols] = m
            parts.append(m * pair_lanes(tail, j))
        hi, lo = halves(jnp.concatenate(parts, axis=1))
        kh, kl = kt_hi[:, rows], kt_lo[:, rows]
        total = total + (dot1(kh, hi) + (dot1(kh, lo) + dot1(kl, hi)))
    state_ref[...] = total


def conv_state(rest, taps, match, taild):
    length = match.shape[1]
    high = length + HALO
    kq_at = DI // (2 * STATE)
    return pl.pallas_call(
        conv_kernel,
        grid=(NG,),
        in_specs=[
            pl.BlockSpec((high, GW), lambda g: (0, g)),
            pl.BlockSpec((high, 2 * STATE), lambda g: (0, kq_at)),
            pl.BlockSpec((8, GW), lambda g: (0, g)),
            pl.BlockSpec((8, 2 * STATE), lambda g: (0, kq_at)),
            pl.BlockSpec((KW - 1, length, 128), lambda g: (0, 0, 0)),
            pl.BlockSpec((1, length, GH), lambda g: (g, 0, 0)),
        ],
        out_specs=(
            pl.BlockSpec((length, GW), lambda g: (0, g)),
            pl.BlockSpec((length, 2 * STATE), lambda g: (0, 0)),
            pl.BlockSpec((STATE, GW), lambda g: (0, g)),
        ),
        out_shape=(
            jax.ShapeDtypeStruct((length, DI), f32),
            jax.ShapeDtypeStruct((length, 2 * STATE), f32),
            jax.ShapeDtypeStruct((STATE, DI), f32),
        ),
        scratch_shapes=[pltpu.VMEM((STATE, length), bf16), pltpu.VMEM((STATE, length), bf16)],
        compiler_params=params(),
        cost_estimate=pl.CostEstimate(flops=2 * 10**9, bytes_accessed=2 * 10**7, transcendentals=2 * 10**6),
        name="conv_state",
    )(rest, rest, taps, taps, match, taild)


def masks_of(segc_ref, segr_ref, rows):
    same = segc_ref[rows, 0:1] == segr_ref[0:1, rows]
    later = iota((Q, Q), 0) >= iota((Q, Q), 1)
    earlier = iota((Q, Q), 0) <= iota((Q, Q), 1)
    return jnp.where(same & later, 0.0, -1e30), jnp.where(same & earlier, 0.0, -1e30)


def local_kernel(
    v_ref, kq_ref, delta_ref, cum_ref, cumt_ref, infc_ref, tailc_ref, keep_ref, segc_ref, segr_ref,
    y_ref, gram, bias, kt,
):
    length = v_ref.shape[0]
    count = length // Q

    @pl.when(pl.program_id(0) == 0)
    def _():
        for c in range(count):
            rows = slice(c * Q, (c + 1) * Q)
            k, q = kq_ref[rows, :STATE], kq_ref[rows, STATE:]
            bias[rows, :] = masks_of(segc_ref, segr_ref, rows)[0]
            gram[rows, :] = dot3(q, k, NT)
            kt[:, rows] = k.T

    low = iota((Q, 128), 1) < HEAD_DIM
    state = None
    for c in range(count):
        rows = slice(c * Q, (c + 1) * Q)
        delta, cum, tail, inflow = (r[0, rows, :] for r in (delta_ref, cum_ref, tailc_ref, infc_ref))
        g, b = gram[rows, :], bias[rows, :]
        if c:
            carried = dot3(kq_ref[rows, STATE:], state)
        tails = []
        for j in range(GW // 128):
            cols = slice(128 * j, 128 * (j + 1))
            v = v_ref[rows, cols]
            w = v * pair_lanes(delta, j)
            both = []
            for i in (2 * j, 2 * j + 1):
                both.append((g * jnp.exp(cum[:, i : i + 1] - cumt_ref[i : i + 1, rows] + b)))
            stacked = jnp.concatenate([jnp.where(low, w, 0.0), jnp.where(low, 0.0, w)], axis=0)
            y = dot3(jnp.concatenate(both, axis=1), stacked)
            if c:
                y = y + carried[:, cols] * pair_lanes(inflow, j)
            y_ref[rows, cols] = y
            if c < count - 1:
                tails.append(v * pair_lanes(tail, j))
        if c < count - 1:
            fresh = dot3(kt[:, rows], jnp.concatenate(tails, axis=1))
            state = fresh if state is None else state * keep_ref[c : c + 1, :] + fresh


def local_out(v, kq, delta, cum, cumt, infc, tailc, keep, segc, segr):
    length = v.shape[0]
    cols = pl.BlockSpec((1, length, GH), lambda g: (g, 0, 0))
    return pl.pallas_call(
        local_kernel,
        grid=(NG,),
        in_specs=[
            pl.BlockSpec((length, GW), lambda g: (0, g)),
            pl.BlockSpec((length, 2 * STATE), lambda g: (0, 0)),
            cols, cols,
            pl.BlockSpec((GH, length), lambda g: (g, 0)),
            cols, cols,
            pl.BlockSpec((8, GW), lambda g: (0, g)),
            pl.BlockSpec((length, 8), lambda g: (0, 0)),
            pl.BlockSpec((8, length), lambda g: (0, 0)),
        ],
        out_specs=pl.BlockSpec((length, GW), lambda g: (0, g)),
        out_shape=jax.ShapeDtypeStruct((length, DI), f32),
        scratch_shapes=[
            pltpu.VMEM((length, Q), f32), pltpu.VMEM((length, Q), f32),
            pltpu.VMEM((STATE, length), f32),
        ],
        compiler_params=params(),
        cost_estimate=pl.CostEstimate(flops=2 * 10**9, bytes_accessed=2 * 10**7, transcendentals=4 * 10**6),
        name="local_out",
    )(v, kq, delta, cum, cumt, infc, tailc, keep, segc, segr)


def gate_kernel(
    y_ref, v_ref, z_ref, g_ref, kq_ref, inc_ref, infd_ref, dir_ref, gam_ref,
    out_ref, dy_ref, dz_ref, dinc_ref, small_ref, ybuf, rbuf,
):
    first = pl.program_id(0) == 0
    rows = y_ref.shape[0]
    q = kq_ref[:, STATE:]
    inflow = infd_ref[...]
    square = jnp.zeros((rows, 128), f32)
    cross = jnp.zeros((rows, 128), f32)
    for j in range(DI // 128):
        cols = slice(128 * j, 128 * (j + 1))
        carry = dot3(q, inc_ref[:, cols]) * pair_lanes(inflow, j)
        y = y_ref[:, cols] + carry + dir_ref[0:1, cols] * v_ref[:, cols]
        z = z_ref[:, cols]
        gated = y * (z * sigmoid(z))
        ybuf[:, cols] = y
        rbuf[:, cols] = gated
        square = square + gated * gated
        cross = cross + gated * (g_ref[:, cols] * gam_ref[0:1, cols])
    inv = lax.rsqrt(jnp.sum(square, axis=1, keepdims=True) * (1.0 / DI) + norm_eps)
    slope = inv * inv * inv * (jnp.sum(cross, axis=1, keepdims=True) * (1.0 / DI))
    qt = q.T

    @pl.when(first)
    def _():
        dinc_ref[...] = jnp.zeros_like(dinc_ref)
        small_ref[...] = jnp.zeros_like(small_ref)

    for j in range(DI // 128):
        cols = slice(128 * j, 128 * (j + 1))
        gated = rbuf[:, cols]
        scaled = gated * inv
        gam = gam_ref[0:1, cols]
        out_ref[:, cols] = (scaled * gam).astype(bf16)
        g = g_ref[:, cols]
        dgated = inv * (g * gam) - gated * slope
        z = z_ref[:, cols]
        s = sigmoid(z)
        dy = dgated * (z * s)
        dy_ref[:, cols] = dy
        dz = dgated * ybuf[:, cols] * (s * (1.0 + z * (1.0 - s)))
        dz_ref[:, cols] = dz.astype(bf16)
        small_ref[2:3, cols] = jnp.maximum(
            small_ref[2:3, cols], jnp.max(jnp.abs(dz), axis=0, keepdims=True)
        )
        small_ref[0:1, cols] += jnp.sum(g * scaled, axis=0, keepdims=True)
        small_ref[1:2, cols] += jnp.sum(dy * v_ref[:, cols], axis=0, keepdims=True)
        dinc_ref[:, cols] += dot3(qt, dy * pair_lanes(inflow, j))


def gate(y, v, z, g, kq, inc, infd, dirx, gam):
    length = y.shape[0]
    tile = Q
    big = pl.BlockSpec((tile, DI), lambda i: (i, 0))
    return pl.pallas_call(
        gate_kernel,
        grid=(length // tile,),
        in_specs=[
            big, big, big, big,
            pl.BlockSpec((tile, 2 * STATE), lambda i: (i, 0)),
            pl.BlockSpec((STATE, DI), lambda i: (0, 0)),
            pl.BlockSpec((tile, HEADS), lambda i: (i, 0)),
            pl.BlockSpec((8, DI), lambda i: (0, 0)),
            pl.BlockSpec((8, DI), lambda i: (0, 0)),
        ],
        out_specs=(
            big, big, big,
            pl.BlockSpec((STATE, DI), lambda i: (0, 0)),
            pl.BlockSpec((8, DI), lambda i: (0, 0)),
        ),
        out_shape=(
            jax.ShapeDtypeStruct((length, DI), bf16),
            jax.ShapeDtypeStruct((length, DI), f32),
            jax.ShapeDtypeStruct((length, DI), bf16),
            jax.ShapeDtypeStruct((STATE, DI), f32),
            jax.ShapeDtypeStruct((8, DI), f32),
        ),
        scratch_shapes=[pltpu.VMEM((tile, DI), f32), pltpu.VMEM((tile, DI), f32)],
        compiler_params=params(),
        cost_estimate=pl.CostEstimate(flops=10**9, bytes_accessed=4 * 10**7, transcendentals=4 * 10**6),
        name="gate",
    )(y, v, z, g, kq, inc, infd, dirx, gam)


def back_kernel(
    final, v_ref, dy_ref, kq_ref, delta_ref, cum_ref, cumt_ref, infc_ref, tailc_ref, tailn_ref,
    keep_ref, inc_ref, dout_ref, dir_ref, segc_ref, segr_ref, dkq_in, dgram_in,
    dv_ref, dkq_ref, dgram, ddelta_ref, dcum_ref, drow_ref, flow_ref,
    gram, gramt, bias, biast, kt, qt, states,
):
    length = v_ref.shape[0]
    count = length // Q
    step = pl.program_id(0)

    @pl.when(step == 0)
    def _():
        for c in range(count):
            rows = slice(c * Q, (c + 1) * Q)
            k, q = kq_ref[rows, :STATE], kq_ref[rows, STATE:]
            b, bt = masks_of(segc_ref, segr_ref, rows)
            bias[rows, :] = b
            biast[rows, :] = bt
            scores = dot3(q, k, NT)
            gram[rows, :] = scores
            gramt[rows, :] = scores.T
            kt[:, rows] = k.T
            qt[:, rows] = q.T
        dgram[...] = dgram_in[...]
        dkq_ref[...] = dkq_in[...]

    low = iota((Q, 128), 1) < HEAD_DIM
    lane = iota((Q, GH), 1)
    line = iota((8, GW), 0)

    states[0] = inc_ref[...].astype(f32)
    for c in range(count):
        rows = slice(c * Q, (c + 1) * Q)
        weighted = v_ref[rows, :] * group_lanes(tailc_ref[0, rows, :])
        states[c + 1] = states[c] * keep_ref[c : c + 1, :] + dot3(kt[:, rows], weighted)

    back = dout_ref[...].astype(f32)
    flows = jnp.zeros((8, GW), f32)
    for c in reversed(range(count)):
        rows = slice(c * Q, (c + 1) * Q)
        flows = jnp.where(line == c, jnp.sum(back * states[c + 1], axis=0, keepdims=True), flows)
        delta, cum = delta_ref[0, rows, :], cum_ref[0, rows, :]
        inflow, tailc, tailn = infc_ref[0, rows, :], tailc_ref[0, rows, :], tailn_ref[0, rows, :]
        k, q = kq_ref[rows, :STATE], kq_ref[rows, STATE:]
        before = states[c]
        after = back
        y_in = dot3(q, before)
        w_in = dot3(k, after)
        g, gt, b, bt = gram[rows, :], gramt[rows, :], bias[rows, :], biast[rows, :]
        dg = dgram[rows, :]
        ddelta = jnp.zeros((Q, GH), f32)
        dcum = jnp.zeros((Q, GH), f32)
        dys, ws = [], []
        for j in range(GW // 128):
            cols = slice(128 * j, 128 * (j + 1))
            dy, v = dy_ref[rows, cols], v_ref[rows, cols]
            spread = pair_lanes(delta, j)
            w = v * spread
            stacked = jnp.concatenate(
                [jnp.where(low, dy, 0.0), jnp.where(low, 0.0, dy)], axis=0
            )
            inner = dot3(stacked, w, NT)
            turned = []
            for i in (0, 1):
                h = 2 * j + i
                col, row = cum[:, h : h + 1], cumt_ref[h : h + 1, rows]
                turned.append(gt * jnp.exp(row - col + bt))
                weighed = inner[Q * i : Q * (i + 1), :] * jnp.exp(col - row + b)
                dg = dg + weighed
                full = weighed * g
                dcum = dcum + jnp.where(lane == h, jnp.sum(full, axis=1, keepdims=True), 0.0)
                drow_ref[h : h + 1, rows] = jnp.sum(full, axis=0, keepdims=True)
            dw_in = w_in[:, cols] * pair_lanes(tailn, j)
            dw = dot3(jnp.concatenate(turned, axis=1), stacked) + dw_in
            dv_ref[rows, cols] = spread * dw + dir_ref[0:1, cols] * dy
            dflow = dy * pair_lanes(inflow, j)
            one = dflow * y_in[:, cols] - w * dw_in
            two = v * dw
            for i in (0, 1):
                h = 2 * j + i
                keep = low if i == 0 else jnp.logical_not(low)
                dcum = dcum + jnp.where(
                    lane == h, jnp.sum(jnp.where(keep, one, 0.0), axis=1, keepdims=True), 0.0
                )
                ddelta = ddelta + jnp.where(
                    lane == h, jnp.sum(jnp.where(keep, two, 0.0), axis=1, keepdims=True), 0.0
                )
            dys.append(dflow)
            ws.append(v * pair_lanes(tailc, j))
        dgram[rows, :] = dg
        ddelta_ref[0, rows, :] = ddelta
        dcum_ref[0, rows, :] = dcum
        flowing = jnp.concatenate(dys, axis=1)
        dkq_ref[rows, STATE:] += dot3(flowing, before, NT)
        dkq_ref[rows, :STATE] += dot3(jnp.concatenate(ws, axis=1), after, NT)
        if c:
            back = back * keep_ref[c : c + 1, :] + dot3(qt[:, rows], flowing)
    flow_ref[...] = flows

    @pl.when(jnp.logical_and(step == pl.num_programs(0) - 1, final))
    def _():
        for c in range(count):
            rows = slice(c * Q, (c + 1) * Q)
            k, q = kq_ref[rows, :STATE], kq_ref[rows, STATE:]
            dg = dgram[rows, :]
            dkq_ref[rows, STATE:] += dot3(dg, k)
            dkq_ref[rows, :STATE] += dot3(dg.T, q)


def back_local(
    first, last, held, v, dy, kq, delta, cum, cumt, infc, tailc, tailn, keep, inc, dout, dirx, segc, segr
):
    length = v.shape[0]
    count = length // Q
    groups = last - first
    if held is None:
        held = (jnp.zeros((length, 2 * STATE), f32), jnp.zeros((length, Q), f32))
    cols = pl.BlockSpec((1, length, GH), lambda g: (g + first, 0, 0))
    wide = pl.BlockSpec((length, GW), lambda g: (0, g + first))
    state = pl.BlockSpec((STATE, GW), lambda g: (0, g + first))
    lines = pl.BlockSpec((8, GW), lambda g: (0, g + first))
    turned = pl.BlockSpec((GH, length), lambda g: (g + first, 0))
    whole = pl.BlockSpec((length, 2 * STATE), lambda g: (0, 0))
    table = pl.BlockSpec((length, Q), lambda g: (0, 0))
    square = pltpu.VMEM((length, Q), f32)
    out_cols = pl.BlockSpec((1, length, GH), lambda g: (g, 0, 0))
    return pl.pallas_call(
        functools.partial(back_kernel, last == NG),
        grid=(groups,),
        in_specs=[
            wide, wide, whole, cols, cols, turned, cols, cols, cols, lines, state, state, lines,
            pl.BlockSpec((length, 8), lambda g: (0, 0)),
            pl.BlockSpec((8, length), lambda g: (0, 0)),
            whole, table,
        ],
        out_specs=(
            pl.BlockSpec((length, GW), lambda g: (0, g)), whole, table, out_cols, out_cols,
            pl.BlockSpec((GH, length), lambda g: (g, 0)),
            pl.BlockSpec((8, GW), lambda g: (0, g)),
        ),
        out_shape=(
            jax.ShapeDtypeStruct((length, groups * GW), f32),
            jax.ShapeDtypeStruct((length, 2 * STATE), f32),
            jax.ShapeDtypeStruct((length, Q), f32),
            jax.ShapeDtypeStruct((groups, length, GH), f32),
            jax.ShapeDtypeStruct((groups, length, GH), f32),
            jax.ShapeDtypeStruct((groups * GH, length), f32),
            jax.ShapeDtypeStruct((8, groups * GW), f32),
        ),
        scratch_shapes=[
            square, square, square, square,
            pltpu.VMEM((STATE, length), f32), pltpu.VMEM((STATE, length), f32),
            pltpu.VMEM((count + 1, STATE, GW), f32),
        ],
        compiler_params=params(),
        cost_estimate=pl.CostEstimate(
            flops=groups * 5 * 10**9, bytes_accessed=groups * 5 * 10**6, transcendentals=groups * 10**6
        ),
        name="back_local",
    )(v, dy, kq, delta, cum, cumt, infc, tailc, tailn, keep, inc, dout, dirx, segc, segr, *held)


def step_kernel(step_ref, par_ref, ddelta_ref, dcum_ref, drow_ref, flow_ref, dstep_ref, small_ref):
    length = step_ref.shape[0]
    upper = (iota((Q, Q), 0) <= iota((Q, Q), 1)).astype(f32)
    eye = (iota((Q, Q), 0) == iota((Q, Q), 1)).astype(f32)
    last = iota((Q, 1), 0) == Q - 1
    rate = jnp.exp(par_ref[1:2, :])
    flows = dotf(flow_ref[...], head_onehot(), NT)
    times = jnp.zeros((1, HEADS), f32)
    decays = jnp.zeros((1, HEADS), f32)
    most = jnp.zeros((1, HEADS), f32)
    for c in range(length // Q):
        rows = slice(c * Q, (c + 1) * Q)
        ddelta = jnp.zeros((Q, HEADS), f32)
        dcum = -dotf(eye, drow_ref[:, rows], NT)
        for g in range(NG):
            place = (iota((GH, HEADS), 0) + g * GH == iota((GH, HEADS), 1)).astype(f32)
            ddelta = ddelta + dotf(ddelta_ref[g, rows, :], place)
            dcum = dcum + dotf(dcum_ref[g, rows, :], place)
        dcum = dcum + jnp.where(last, flows[c : c + 1, :], 0.0)
        x = step_ref[rows, :] + par_ref[0:1, :]
        dlog = dotf(upper, dcum) * rate
        decays = decays - jnp.sum(dlog * softplus(x), axis=0, keepdims=True)
        dstep = (ddelta - dlog) * sigmoid(x)
        times = times + jnp.sum(dstep, axis=0, keepdims=True)
        most = jnp.maximum(most, jnp.max(jnp.abs(dstep), axis=0, keepdims=True))
        dstep_ref[rows, :] = dstep.astype(bf16)
    small_ref[...] = jnp.zeros_like(small_ref)
    small_ref[0:1, :] = times
    small_ref[1:2, :] = decays
    small_ref[2:3, :] = most


def step_back(step_raw, pars, ddelta, dcum, drow, flow):
    return pl.pallas_call(
        step_kernel,
        out_shape=(
            jax.ShapeDtypeStruct(step_raw.shape, bf16),
            jax.ShapeDtypeStruct((8, HEADS), f32),
        ),
        compiler_params=params(),
        cost_estimate=pl.CostEstimate(flops=10**7, bytes_accessed=10**7, transcendentals=10**5),
        name="step_back",
    )(step_raw, pars, ddelta, dcum, drow, flow)


def unconv_kernel(x_ref, tap_ref, match_ref, da_ref, db_ref, dkq_ref, dx_ref, edge_ref, dtap_ref, *held):
    length = dx_ref.shape[0]
    count = length // Q
    step = pl.program_id(0)
    half = DI // TILE // 2
    for buf in held:
        buf[0:HALO, :] = jnp.zeros((HALO, TILE), f32)
        buf[HALO + length :, :] = jnp.zeros((HALO, TILE), f32)
    for j in range(TILE // 128):
        cols = slice(128 * j, 128 * (j + 1))
        sums = [jnp.zeros((1, 128), f32) for _ in range(KW + 1)]
        for c in range(count):
            rows = slice(c * Q, (c + 1) * Q)
            s = conv_sum(x_ref, tap_ref, match_ref, c * Q, Q, cols)
            sig = sigmoid(s)
            dm = jnp.where(
                step < half, da_ref[rows, cols], jnp.where(step < 2 * half, db_ref[rows, cols], dkq_ref[rows, cols])
            )
            ds = dm * (sig * (1.0 + s * (1.0 - sig)))
            sums[KW] = sums[KW] + jnp.sum(ds, axis=0, keepdims=True)
            for k in range(KW):
                e = ds if k == KW - 1 else ds * match_ref[k, rows, :]
                held[k][HALO + c * Q : HALO + (c + 1) * Q, cols] = e
                taken = x_ref[pl.ds(HALO - (KW - 1) + k + c * Q, Q), cols]
                sums[k] = sums[k] + jnp.sum(e * taken, axis=0, keepdims=True)
        for k in range(KW + 1):
            dtap_ref[k : k + 1, cols] = sums[k]

        def placed(start, rows):
            total = None
            for k in range(KW):
                term = tap_ref[k : k + 1, cols] * held[k][pl.ds(start + KW - 1 - k, rows), cols]
                total = term if total is None else total + term
            return total

        edge_ref[0:HALO, cols] = placed(0, HALO)
        most = jnp.zeros((1, 128), f32)
        for c in range(count):
            dx = placed(HALO + c * Q, Q)
            most = jnp.maximum(most, jnp.max(jnp.abs(dx), axis=0, keepdims=True))
            dx_ref[c * Q : (c + 1) * Q, cols] = dx.astype(bf16)
            if c == count - 1:
                edge_ref[HALO:, cols] = dx[Q - HALO :, :]
        dtap_ref[KW + 1 : KW + 2, cols] = most
    dtap_ref[KW + 2 :, :] = jnp.zeros((8 - KW - 2, TILE), f32)


def unconv(rest, taps, match, dva, dvb, dkq):
    length = match.shape[1]
    high = length + HALO
    half = DI // TILE // 2
    return pl.pallas_call(
        unconv_kernel,
        grid=(CH // TILE,),
        in_specs=[
            pl.BlockSpec((high, TILE), lambda j: (0, j)),
            pl.BlockSpec((8, TILE), lambda j: (0, j)),
            pl.BlockSpec((KW - 1, length, 128), lambda j: (0, 0, 0)),
            pl.BlockSpec((length, TILE), lambda j: (0, jnp.minimum(j, half - 1))),
            pl.BlockSpec((length, TILE), lambda j: (0, jnp.clip(j - half, 0, half - 1))),
            pl.BlockSpec((length, TILE), lambda j: (0, 0)),
        ],
        out_specs=(
            pl.BlockSpec((length, TILE), lambda j: (0, j)),
            pl.BlockSpec((2 * HALO, TILE), lambda j: (0, j)),
            pl.BlockSpec((8, TILE), lambda j: (0, j)),
        ),
        out_shape=(
            jax.ShapeDtypeStruct((length, CH), bf16),
            jax.ShapeDtypeStruct((2 * HALO, CH), f32),
            jax.ShapeDtypeStruct((8, CH), f32),
        ),
        scratch_shapes=[pltpu.VMEM((length + 2 * HALO, TILE), f32) for _ in range(KW)],
        compiler_params=params(),
        cost_estimate=pl.CostEstimate(flops=10**8, bytes_accessed=2 * 10**7, transcendentals=2 * 10**6),
        name="unconv",
    )(rest, taps, match, dva, dvb, dkq)


def adamw(param, grad, moment, square, rate, shrink):
    moment_new = beta_one * moment + (1.0 - beta_one) * grad
    square_new = beta_two * square + (1.0 - beta_two) * grad * grad
    first_corr = 1.0 - beta_one**ADAM_STEP
    second_corr = 1.0 - beta_two**ADAM_STEP
    update = moment_new / first_corr / (jnp.sqrt(square_new / second_corr) + adam_eps)
    return (param - rate * (update + shrink * param), moment_new, square_new)


def shifted(value, axis, by):
    count = lax.axis_size(axis)
    pairs = [(i, i + by) for i in range(count) if 0 <= i + by < count]
    return lax.ppermute(value, axis, pairs)


TOKENS = (((0,), (0,)), ((), ()))


def gathered(value):
    return lax.all_gather(value, ("dp", "shard"), axis=0, tiled=True)


def shard_gathered(value):
    count, here = lax.axis_size("shard"), lax.axis_index("shard")
    rows, width = value.shape
    held = jnp.zeros((count * rows, width), value.dtype)
    for k in range(count):
        part = exchanged(value, "shard", k) if k else value
        held = lax.dynamic_update_slice(held, part, ((here ^ k) * rows, 0))
    return held


def exchanged(value, axis, by):
    return lax.ppermute(value, axis, [(i, i ^ by) for i in range(lax.axis_size(axis))])


PAD = 16


def relative(value, block, core):
    base = lax.axis_index("dp") // 2
    length = value.shape[0]
    return [
        lax.dynamic_slice(value, (0, (((j ^ base) * 2) + core) * block), (length, block))
        for j in range(lax.axis_size("dp") // 2)
    ]


def both_cores(value):
    return jnp.concatenate([value, exchanged(value, "dp", 1)], axis=0)


def sum_columns(value, block):
    core = lax.axis_index("dp") % 2
    theirs = jnp.concatenate(relative(value, block, 1 - core), axis=1)
    mine = jnp.concatenate(relative(value, block, core), axis=1)
    return jnp.concatenate([mine, exchanged(theirs, "dp", 1)], axis=0)


def exponent(bound):
    return jnp.ceil(jnp.log2(jnp.maximum(bound, 1e-30)))


def coded(total, power, rows):
    own = iota(total.shape, 0) < rows
    return jnp.where(own, total * jnp.exp2(15.0 - power), power).astype(jnp.float16)


def decoded(payload, rows):
    power = payload[rows, 0].astype(f32)
    return payload.astype(f32) * jnp.exp2(power - 15.0), power


def after(value, *earlier):
    return lax.optimization_barrier((value, earlier))[0]


class Sum:
    def __init__(self, lhs, order):
        spots = lax.axis_size("dp") // 2
        self.block = lhs.shape[1] // spots
        self.order = order
        self.kept, self.sends = [0], []
        for bit in reversed(order):
            send = [j ^ (1 << bit) for j in self.kept]
            self.sends.insert(0, send)
            self.kept = self.kept + send
        self.rows = spots * self.block
        half = len(self.kept) // 2
        self.sent = self.columns(lhs, self.sends[0])
        self.held = self.columns(lhs, self.kept[:half])
        self.total = None
        self.at = 0

    def columns(self, lhs, places):
        block = self.block
        return jnp.concatenate(
            [lhs[:, j * block : (j + 1) * block] for j in places] + [jnp.zeros((lhs.shape[0], PAD), bf16)],
            axis=1,
        )

    def prepare(self, rhs=None, bound=None):
        self.rows //= 2
        if self.total is None:
            self.rhs, self.power = rhs, exponent(bound)
            part = lax.dot_general(self.sent, rhs, TOKENS, preferred_element_type=f32)
        else:
            part = self.total[self.rows : 2 * self.rows + PAD]
        self.payload = coded(part, self.power, self.rows)

    def send(self):
        self.got = exchanged(self.payload, "dp", 2 << self.order[self.at])
        self.at += 1
        if self.total is None:
            self.total = lax.dot_general(self.held, self.rhs, TOKENS, preferred_element_type=f32)

    def take(self, *earlier):
        got, other = decoded(after(self.got, earlier), self.rows)
        self.total = self.total[: self.rows + PAD] + got
        self.power = jnp.maximum(self.power, other) + 1.0

    def more(self):
        return self.at < len(self.order)

    def shard_prepare(self):
        count, here = lax.axis_size("shard"), lax.axis_index("shard")
        self.rows //= count
        self.payloads = [
            coded(
                lax.dynamic_slice(self.total, ((here ^ k) * self.rows, 0), (self.rows + PAD, self.total.shape[1])),
                self.power, self.rows,
            )
            for k in range(1, count)
        ]

    def shard_send(self):
        self.parts = [exchanged(part, "shard", k + 1) for k, part in enumerate(self.payloads)]

    def shard_take(self, *earlier):
        here = lax.axis_index("shard")
        result = lax.dynamic_slice(self.total, (here * self.rows, 0), (self.rows, self.total.shape[1]))
        for part in self.parts:
            result = result + decoded(after(part, earlier), self.rows)[0][: self.rows]
        return result


def summed(value):
    for axis in ("dp", "shard"):
        count = lax.axis_size(axis)
        if count & (count - 1):
            value = lax.psum(value, axis)
            continue
        by = 1
        while by < count:
            value = value + lax.ppermute(value, axis, [(i, i ^ by) for i in range(count)])
            by *= 2
    return value


def carried(state, factor, by):
    incoming = shifted(state.astype(bf16), "shard", by)
    for _ in range(lax.axis_size("shard") - 2):
        incoming = shifted((state + factor * incoming.astype(f32)).astype(bf16), "shard", by)
    return incoming


def shards(
    hidden_in, cotangent, segment_ids,
    param_prenorm, param_inputs, param_kernel, param_offsets, param_timestep, param_decays,
    param_direct, param_gating, param_outputs,
    moment_prenorm, moment_inputs, moment_kernel, moment_offsets, moment_timestep, moment_decays,
    moment_direct, moment_gating, moment_outputs,
    square_prenorm, square_inputs, square_kernel, square_offsets, square_timestep, square_decays,
    square_direct, square_gating, square_outputs,
):
    length, width = hidden_in.shape
    own_inputs = param_inputs.astype(bf16)
    rest_w = gathered(own_inputs[:, DI:])
    gate_w = lax.all_gather(shard_gathered(own_inputs[:, :DI]), "dp", axis=0, tiled=True)
    out_w = lax.all_gather(shard_gathered(param_outputs.astype(bf16)), "dp", axis=0, tiled=True)

    seg = segment_ids.astype(f32)
    ends = jnp.pad(seg[length - HALO :], (0, width - HALO))[None, :]
    halo = shifted(
        jnp.concatenate([hidden_in[length - HALO :], jnp.broadcast_to(ends, (HALO, width))], axis=0),
        "shard", 1,
    )
    rim_seg = jnp.where(lax.axis_index("shard") == 0, -1.0, halo[HALO, :HALO])
    rim = rim_seg[HALO - 1]
    all_segs = jnp.concatenate([rim_seg, seg])
    match = jnp.stack(
        [
            (all_segs[HALO - (KW - 1) + k : HALO - (KW - 1) + k + length] == seg).astype(f32)
            for k in range(KW - 1)
        ]
    )
    match = jnp.broadcast_to(match[:, :, None], (KW - 1, length, 128))
    chunks = seg.reshape(-1, Q)
    before = jnp.concatenate([rim[None], chunks[:-1, Q - 1]])
    mask = jnp.stack(
        [
            (chunks == before[:, None]).reshape(-1),
            (chunks == chunks[:, Q - 1 :]).reshape(-1),
            seg == rim,
            seg == seg[length - 1],
        ]
        + [seg < -1.0] * 4,
        axis=1,
    ).astype(f32)
    segc = jnp.broadcast_to(seg[:, None], (length, 8))
    segr = jnp.broadcast_to(seg[None, :], (8, length))

    taps = jnp.concatenate([param_kernel, param_offsets[None, :], jnp.zeros((8 - KW - 1, CH), f32)], axis=0)
    pars = jnp.concatenate([param_timestep[None, :], param_decays[None, :], jnp.zeros((6, HEADS), f32)], axis=0)
    dirx = jnp.broadcast_to(jnp.repeat(param_direct, HEAD_DIM)[None, :], (8, DI))
    gam = jnp.broadcast_to(param_gating[None, :], (8, DI))

    hidden = jnp.concatenate([halo[:HALO], hidden_in], axis=0)
    inv = lax.rsqrt(jnp.mean(hidden * hidden, axis=1, keepdims=True) + norm_eps)
    normed = (hidden * inv * param_prenorm).astype(bf16)
    own_normed = normed[HALO:]
    upstream = cotangent.astype(bf16)

    groups = lax.axis_size("shard")
    spots = [bit for bit in range(20) if (2 << bit) < lax.axis_size("dp")]
    in_block, out_block = groups * param_inputs.shape[0], groups * param_outputs.shape[0]
    up_both = both_cores(upstream)
    normed_both = sum_columns(own_normed, in_block)
    norm_bound = 2.02 * length * width**0.5 * jnp.max(jnp.abs(param_prenorm))
    gate_bound = 2.02 * length * DI**0.5 * jnp.max(jnp.abs(param_gating))
    gate_bound = gate_bound * jnp.max(jnp.abs(up_both)).astype(f32)
    gate_sum = Sum(normed_both, spots[::-1])
    rest_sums = [Sum(normed_both, spots), Sum(normed_both, spots[::-1])]
    rest_w = after(
        rest_w, match, mask, segc, segr, taps, pars, dirx, gam, up_both, gate_bound, norm_bound,
        gate_sum.sent, gate_sum.held, rest_sums[0].sent, rest_sums[0].held,
    )

    rest = jnp.dot(normed, rest_w, preferred_element_type=f32)
    step_raw = rest[HALO:, CH:]
    delta, cum, cumt, infc, tailc, tailn, taild, infd, keep, factor = prep(step_raw, pars, mask)
    v, kq, state = conv_state(rest, taps, match, taild)
    incoming = carried(state, factor[0:1], 1)
    y = local_out(v, kq, delta, cum, cumt, infc, tailc, keep, segc, segr)
    gate_w = after(gate_w, y)
    out_w = after(out_w, y)
    z = jnp.dot(own_normed, gate_w, preferred_element_type=f32)
    back_gated = lax.dot_general(upstream, out_w, NT, preferred_element_type=f32)
    gated, dy, dz, dinc, small = gate(y, v, z, back_gated, kq, incoming, infd, dirx, gam)

    dz_most = jnp.max(small[2])
    dz_most = jnp.maximum(dz_most, exchanged(jnp.full((8, 128), dz_most), "dp", 1)[0, 0])
    outgoing = carried(dinc, factor[0:1], -1)
    out_sum = Sum(sum_columns(gated, out_block), spots)
    dz_both = both_cores(dz)
    block_out = hidden_in + jnp.dot(gated, out_w, preferred_element_type=f32)
    first_sums = [out_sum, gate_sum]
    out_sum.prepare(up_both, gate_bound)
    gate_sum.prepare(dz_both, norm_bound * dz_most)
    for one in first_sums:
        one.send()
    back_normed = lax.dot_general(dz, gate_w, NT, preferred_element_type=f32)
    outgoing = after(outgoing, out_sum.payload, gate_sum.payload, out_sum.total, gate_sum.total, back_normed, block_out)

    ssm = (kq, delta, cum, cumt, infc, tailc, tailn, keep, incoming)
    dv1, *held1 = back_local(0, NG // 2, None, v, dy, *ssm, outgoing, dirx, segc, segr)
    for one in first_sums:
        one.take(dv1)
        if one.more():
            one.prepare()
            one.send()
    dy = after(dy, *[one.payload for one in first_sums])
    dv2, *held2 = back_local(NG // 2, NG, held1[:2], v, dy, *ssm, outgoing, dirx, segc, segr)
    for one in first_sums:
        one.take(dv2)
        while one.more():
            one.prepare()
            one.send()
            one.take()
        one.shard_prepare()
        one.shard_send()
    dv2 = after(dv2, *[one.payloads for one in first_sums])
    dkq = held2[0]
    ddelta, dcum, drow = (jnp.concatenate([p, q], axis=0) for p, q in zip(held1[2:5], held2[2:5]))
    flow = jnp.concatenate([held1[5], held2[5]], axis=1)
    dstep, small_step = step_back(step_raw, pars, ddelta, dcum, drow, flow)
    dx, edge, dtap = unconv(rest, taps, match, dv1, dv2, dkq)
    rim_grad = shifted(edge[:HALO], "shard", -1)
    mended = edge[HALO:] + rim_grad
    dx = lax.dynamic_update_slice(dx, mended.astype(bf16), (length - HALO, 0))
    rest_most = jnp.maximum(jnp.maximum(jnp.max(dtap[KW + 1]), jnp.max(small_step[2])), jnp.max(jnp.abs(mended)))
    rest_most = jnp.maximum(rest_most, exchanged(jnp.full((8, 128), rest_most), "dp", 1)[0, 0])
    rest_bound = norm_bound * rest_most
    drest = jnp.concatenate([dx, dstep], axis=1)
    drest_both = both_cores(drest)
    middle = (drest.shape[1] // 256) * 128
    rest_sums[0].prepare(drest_both[:, :middle], rest_bound)
    rest_sums[1].prepare(drest_both[:, middle:], rest_bound)
    for one in rest_sums:
        one.send()
    drest = after(drest, *[one.payload for one in rest_sums])
    back_normed = back_normed + lax.dot_general(drest, rest_w, NT, preferred_element_type=f32)
    sent = [one.got for one in rest_sums]
    ready = [one.payload for one in rest_sums]
    grad_outputs = out_sum.shard_take(ready)
    grad_gate = gate_sum.shard_take(ready)
    for one in rest_sums:
        one.take(back_normed, grad_outputs, grad_gate)
        while one.more():
            one.prepare()
            one.send()
            one.take()
        one.shard_prepare()
        one.shard_send()
    sent = [one.payloads for one in rest_sums]
    grad_rest = [one.shard_take() for one in rest_sums]
    grad_inputs = jnp.concatenate([grad_gate] + grad_rest, axis=1)

    own_inv = inv[HALO:]
    scaled = hidden_in * own_inv
    gained = back_normed * param_prenorm
    hidden_grad = cotangent + own_inv * (
        gained - scaled * jnp.mean(gained * scaled, axis=1, keepdims=True)
    )
    grad_prenorm = jnp.sum(back_normed * scaled, axis=0)

    pieces = [
        grad_prenorm,
        dtap[:KW].reshape(-1),
        dtap[KW],
        small_step[0],
        small_step[1],
        jnp.sum(small[1].reshape(HEADS, HEAD_DIM), axis=1),
        small[0],
    ]
    flat = after(jnp.concatenate(pieces), sent)
    count = flat.shape[0]
    lines = -(-count // 1024) * 8
    total = summed(jnp.pad(flat, (0, lines * 128 - count)).reshape(lines, 128)).reshape(-1)
    found, at = [], 0
    for piece in pieces:
        found.append(total[at : at + piece.shape[0]])
        at += piece.shape[0]
    grad_prenorm, grad_kernel, grad_offsets, grad_timestep, grad_decays, grad_direct, grad_gating = found
    grad_kernel = grad_kernel.reshape(KW, CH)

    params = (
        param_prenorm, param_inputs, param_kernel, param_offsets, param_timestep, param_decays,
        param_direct, param_gating, param_outputs,
    )
    moments = (
        moment_prenorm, moment_inputs, moment_kernel, moment_offsets, moment_timestep, moment_decays,
        moment_direct, moment_gating, moment_outputs,
    )
    squares = (
        square_prenorm, square_inputs, square_kernel, square_offsets, square_timestep, square_decays,
        square_direct, square_gating, square_outputs,
    )
    grads = (
        grad_prenorm, grad_inputs, grad_kernel, grad_offsets, grad_timestep, grad_decays,
        grad_direct, grad_gating, grad_outputs,
    )
    updated = [
        adamw(params[i], grads[i], moments[i], squares[i], rate_table[i], shrink_table[i])
        for i in range(9)
    ]
    return (
        (block_out, hidden_grad)
        + grads
        + tuple(u[0] for u in updated)
        + tuple(u[1] for u in updated)
        + tuple(u[2] for u in updated)
    )


def solution(mesh):
    rows = P(("dp", "shard"), None)
    member = (P(), rows, P(), P(), P(), P(), P(), P(), rows)

    return jax.shard_map(
        shards,
        mesh=mesh,
        in_specs=(rows, rows, P(("dp", "shard"))) + member * 3,
        out_specs=(rows, rows) + member * 4,
        check_vma=False,
    )
```

```python
import functools

import jax
import jax.numpy as jnp
from jax import lax
from jax.experimental import pallas as pl
from jax.experimental.pallas import tpu as pltpu
from jax.sharding import PartitionSpec as P


HEADS = 48
HEAD_DIM = 64
STATE = 128
KW = 4
ADAM_STEP = 10
DI = 3072
CH = 3328

Q = 128
GH = 8
GW = GH * HEAD_DIM
NG = HEADS // GH
HALO = 8
PAD = 16
TILE = 256

bf16 = jnp.bfloat16
f32 = jnp.float32
highest = lax.Precision.HIGHEST

norm_eps = 1e-05
beta_one = 0.9
beta_two = 0.95
adam_eps = 1e-08
rate_table = (0.2, 0.01, 0.2, 0.2, 0.2, 0.2, 0.2, 0.2, 0.01)
shrink_table = (0.0, 0.1, 0.1, 0.0, 0.0, 0.0, 0.0, 0.0, 0.1)

NN = (((1,), (0,)), ((), ()))
NT = (((1,), (1,)), ((), ()))


def halves(x):
    hi = x.astype(bf16)
    return hi, (x - hi.astype(f32)).astype(bf16)


def dot1(a, b, dims=NN):
    return lax.dot_general(a.astype(bf16), b.astype(bf16), dims, preferred_element_type=f32)


def dot3(a, b, dims=NN):
    ah, al = halves(a)
    bh, bl = halves(b)
    return dot1(ah, bh, dims) + (dot1(ah, bl, dims) + dot1(al, bh, dims))


def dotf(a, b, dims=NN):
    return lax.dot_general(a, b, dims, precision=highest, preferred_element_type=f32)


def iota(shape, dim):
    return lax.broadcasted_iota(jnp.int32, shape, dim)


def sigmoid(x):
    return 1.0 / (1.0 + jnp.exp(-x))


def softplus(x):
    u = jnp.exp(-jnp.abs(x))
    series = u * (1.0 - u * (0.5 - u * (1.0 / 3.0 - u * (0.25 - u * 0.2))))
    return jnp.maximum(x, 0.0) + jnp.where(u < 0.03, series, jnp.log(1.0 + u))


def pair_lanes(cols, j):
    rows = cols.shape[0]
    low = iota((rows, 128), 1) < HEAD_DIM
    return jnp.where(low, cols[:, 2 * j : 2 * j + 1], cols[:, 2 * j + 1 : 2 * j + 2])


def group_lanes(cols):
    return jnp.concatenate([pair_lanes(cols, j) for j in range(cols.shape[1] // 2)], axis=1)


def head_onehot():
    return (iota((HEADS, DI), 1) // HEAD_DIM == iota((HEADS, DI), 0)).astype(f32)


def params(limit=60000, **kw):
    return pltpu.CompilerParams(vmem_limit_bytes=limit * 1024, **kw)


def prep_kernel(
    step_ref, par_ref, mask_ref, delta_ref, cum_ref, cumt_ref, infc_ref, tailc_ref, tailn_ref,
    taild_ref, infd_ref, keep_ref, factor_ref,
):
    length = mask_ref.shape[0]
    count = length // Q
    tri = (iota((Q, Q), 0) >= iota((Q, Q), 1)).astype(f32)
    eye = (iota((HEADS, HEADS), 0) == iota((HEADS, HEADS), 1)).astype(f32)
    rate = jnp.exp(par_ref[1:2, :])
    base = jnp.zeros((1, HEADS), f32)
    held = []
    keeps = []
    for c in range(count):
        rows = slice(c * Q, (c + 1) * Q)
        delta = softplus(step_ref[pl.ds(HALO + c * Q, Q), :HEADS] + par_ref[0:1, :])
        cum = dotf(tri, -delta * rate)
        cumt_ref[:, rows] = dotf(eye, cum, NT)
        last = cum[Q - 1 : Q, :]
        alive, ending = mask_ref[rows, 0:1], mask_ref[rows, 1:2]
        infc = jnp.exp(cum) * alive
        tailn = jnp.exp(last - cum) * ending
        tailc = tailn * delta
        for g in range(NG):
            part = slice(g * GH, (g + 1) * GH)
            delta_ref[g, rows, :] = delta[:, part]
            cum_ref[g, rows, :] = cum[:, part]
            infc_ref[g, rows, :] = infc[:, part]
            tailn_ref[g, rows, :] = tailn[:, part]
            tailc_ref[g, rows, :] = tailc[:, part]
        keeps.append(infc[Q - 1 : Q, :])
        whole = cum + base
        infd_ref[rows, :] = jnp.exp(whole) * mask_ref[rows, 2:3]
        held.append((whole, delta))
        base = base + last
    for c in range(count):
        rows = slice(c * Q, (c + 1) * Q)
        whole, delta = held[c]
        taild = jnp.exp(base - whole) * mask_ref[rows, 3:4] * delta
        for g in range(NG):
            taild_ref[g, rows, :] = taild[:, g * GH : (g + 1) * GH]
    factor = jnp.exp(base) * mask_ref[length - 1 : length, 2:3]
    spread = head_onehot()
    line = iota((8, HEADS), 0)
    table = jnp.zeros((8, HEADS), f32)
    for c in range(count):
        table = jnp.where(line == c, keeps[c], table)
    keep_ref[...] = dotf(table, spread)
    factor_ref[...] = dotf(jnp.where(line == 0, factor, 0.0), spread)


def whole(array):
    return pl.BlockSpec(array.shape, lambda i: (0,) * array.ndim)


def steps_of(rest):
    return pl.BlockSpec((rest.shape[0], 128), lambda i: (0, CH // 128))


def prep(rest, pars, mask):
    length = mask.shape[0]
    cols = jax.ShapeDtypeStruct((NG, length, GH), f32)
    wide = jax.ShapeDtypeStruct((8, DI), f32)
    shapes = (
        cols, cols, jax.ShapeDtypeStruct((HEADS, length), f32), cols, cols, cols, cols,
        jax.ShapeDtypeStruct((length, HEADS), f32), wide, wide,
    )
    return pl.pallas_call(
        prep_kernel,
        grid=(1,),
        in_specs=[steps_of(rest), whole(pars), whole(mask)],
        out_specs=tuple(whole(shape) for shape in shapes),
        out_shape=shapes,
        compiler_params=params(),
        cost_estimate=pl.CostEstimate(flops=10**7, bytes_accessed=10**7, transcendentals=10**5),
        name="prep",
    )(rest, pars, mask)


def conv_sum(x_ref, tap_ref, match_ref, start, rows, cols):
    total = tap_ref[KW : KW + 1, cols] + tap_ref[KW - 1 : KW, cols] * x_ref[
        pl.ds(HALO + start, rows), cols
    ]
    for k in range(KW - 1):
        taken = x_ref[pl.ds(HALO - (KW - 1) + k + start, rows), cols]
        total = total + tap_ref[k : k + 1, cols] * (taken * match_ref[k, pl.ds(start, rows), :])
    return total


def conv_kernel(
    xv_ref, xk_ref, tv_ref, tk_ref, match_ref, taild_ref, v_ref, kq_ref, state_ref, kt_hi, kt_lo
):
    length = v_ref.shape[0]
    count = length // Q

    @pl.when(pl.program_id(0) == 0)
    def _():
        for c in range(count):
            for j in range(2):
                cols = slice(128 * j, 128 * (j + 1))
                s = conv_sum(xk_ref, tk_ref, match_ref, c * Q, Q, cols)
                m = s * sigmoid(s)
                kq_ref[c * Q : (c + 1) * Q, cols] = m
                if j == 0:
                    hi, lo = halves(m.T)
                    kt_hi[:, c * Q : (c + 1) * Q] = hi
                    kt_lo[:, c * Q : (c + 1) * Q] = lo

    total = jnp.zeros((STATE, GW), f32)
    for c in range(count):
        rows = slice(c * Q, (c + 1) * Q)
        tail = taild_ref[0, rows, :]
        parts = []
        for j in range(GW // 128):
            cols = slice(128 * j, 128 * (j + 1))
            s = conv_sum(xv_ref, tv_ref, match_ref, c * Q, Q, cols)
            m = s * sigmoid(s)
            v_ref[rows, cols] = m
            parts.append(m * pair_lanes(tail, j))
        hi, lo = halves(jnp.concatenate(parts, axis=1))
        kh, kl = kt_hi[:, rows], kt_lo[:, rows]
        total = total + (dot1(kh, hi) + (dot1(kh, lo) + dot1(kl, hi)))
    state_ref[...] = total


def conv_state(rest, taps, match, taild):
    length = match.shape[1]
    high = length + HALO
    kq_at = DI // (2 * STATE)
    return pl.pallas_call(
        conv_kernel,
        grid=(NG,),
        in_specs=[
            pl.BlockSpec((high, GW), lambda g: (0, g)),
            pl.BlockSpec((high, 2 * STATE), lambda g: (0, kq_at)),
            pl.BlockSpec((8, GW), lambda g: (0, g)),
            pl.BlockSpec((8, 2 * STATE), lambda g: (0, kq_at)),
            pl.BlockSpec((KW - 1, length, 128), lambda g: (0, 0, 0)),
            pl.BlockSpec((1, length, GH), lambda g: (g, 0, 0)),
        ],
        out_specs=(
            pl.BlockSpec((length, GW), lambda g: (0, g)),
            pl.BlockSpec((length, 2 * STATE), lambda g: (0, 0)),
            pl.BlockSpec((STATE, GW), lambda g: (0, g)),
        ),
        out_shape=(
            jax.ShapeDtypeStruct((length, DI), f32),
            jax.ShapeDtypeStruct((length, 2 * STATE), f32),
            jax.ShapeDtypeStruct((STATE, DI), f32),
        ),
        scratch_shapes=[pltpu.VMEM((STATE, length), bf16), pltpu.VMEM((STATE, length), bf16)],
        compiler_params=params(),
        cost_estimate=pl.CostEstimate(flops=2 * 10**9, bytes_accessed=2 * 10**7, transcendentals=2 * 10**6),
        name="conv_state",
    )(rest, rest, taps, taps, match, taild)


def masks_of(segc_ref, segr_ref, rows):
    same = segc_ref[rows, 0:1] == segr_ref[0:1, rows]
    later = iota((Q, Q), 0) >= iota((Q, Q), 1)
    earlier = iota((Q, Q), 0) <= iota((Q, Q), 1)
    return jnp.where(same & later, 0.0, -1e30), jnp.where(same & earlier, 0.0, -1e30)


def local_kernel(
    v_ref, kq_ref, delta_ref, cum_ref, cumt_ref, infc_ref, tailc_ref, keep_ref, segc_ref, segr_ref,
    y_ref, gram, bias, kt,
):
    length = v_ref.shape[0]
    count = length // Q

    @pl.when(pl.program_id(0) == 0)
    def _():
        for c in range(count):
            rows = slice(c * Q, (c + 1) * Q)
            k, q = kq_ref[rows, :STATE], kq_ref[rows, STATE:]
            bias[rows, :] = masks_of(segc_ref, segr_ref, rows)[0]
            gram[rows, :] = dot3(q, k, NT)
            kt[:, rows] = k.T

    low = iota((Q, 128), 1) < HEAD_DIM
    state = None
    for c in range(count):
        rows = slice(c * Q, (c + 1) * Q)
        delta, cum, tail, inflow = (r[0, rows, :] for r in (delta_ref, cum_ref, tailc_ref, infc_ref))
        g, b = gram[rows, :], bias[rows, :]
        if c:
            carried = dot3(kq_ref[rows, STATE:], state)
        tails = []
        for j in range(GW // 128):
            cols = slice(128 * j, 128 * (j + 1))
            v = v_ref[rows, cols]
            w = v * pair_lanes(delta, j)
            both = []
            for i in (2 * j, 2 * j + 1):
                both.append((g * jnp.exp(cum[:, i : i + 1] - cumt_ref[i : i + 1, rows] + b)))
            stacked = jnp.concatenate([jnp.where(low, w, 0.0), jnp.where(low, 0.0, w)], axis=0)
            y = dot3(jnp.concatenate(both, axis=1), stacked)
            if c:
                y = y + carried[:, cols] * pair_lanes(inflow, j)
            y_ref[rows, cols] = y
            if c < count - 1:
                tails.append(v * pair_lanes(tail, j))
        if c < count - 1:
            fresh = dot3(kt[:, rows], jnp.concatenate(tails, axis=1))
            state = fresh if state is None else state * keep_ref[c : c + 1, :] + fresh


def local_out(v, kq, delta, cum, cumt, infc, tailc, keep, segc, segr):
    length = v.shape[0]
    cols = pl.BlockSpec((1, length, GH), lambda g: (g, 0, 0))
    return pl.pallas_call(
        local_kernel,
        grid=(NG,),
        in_specs=[
            pl.BlockSpec((length, GW), lambda g: (0, g)),
            pl.BlockSpec((length, 2 * STATE), lambda g: (0, 0)),
            cols, cols,
            pl.BlockSpec((GH, length), lambda g: (g, 0)),
            cols, cols,
            pl.BlockSpec((8, GW), lambda g: (0, g)),
            pl.BlockSpec((length, 8), lambda g: (0, 0)),
            pl.BlockSpec((8, length), lambda g: (0, 0)),
        ],
        out_specs=pl.BlockSpec((length, GW), lambda g: (0, g)),
        out_shape=jax.ShapeDtypeStruct((length, DI), f32),
        scratch_shapes=[
            pltpu.VMEM((length, Q), f32), pltpu.VMEM((length, Q), f32),
            pltpu.VMEM((STATE, length), f32),
        ],
        compiler_params=params(),
        cost_estimate=pl.CostEstimate(flops=2 * 10**9, bytes_accessed=2 * 10**7, transcendentals=4 * 10**6),
        name="local_out",
    )(v, kq, delta, cum, cumt, infc, tailc, keep, segc, segr)


def gate_kernel(
    y_ref, v_ref, z_ref, g_ref, kq_ref, inc_ref, infd_ref, dir_ref, gam_ref,
    out_ref, dy_ref, dz_ref, dinc_ref, small_ref, ybuf, rbuf,
):
    first = pl.program_id(0) == 0
    rows = y_ref.shape[0]
    q = kq_ref[:, STATE:]
    inflow = infd_ref[...]
    square = jnp.zeros((rows, 128), f32)
    cross = jnp.zeros((rows, 128), f32)
    for j in range(DI // 128):
        cols = slice(128 * j, 128 * (j + 1))
        carry = dot3(q, inc_ref[:, cols]) * pair_lanes(inflow, j)
        y = y_ref[:, cols] + carry + dir_ref[0:1, cols] * v_ref[:, cols]
        z = z_ref[:, cols]
        gated = y * (z * sigmoid(z))
        ybuf[:, cols] = y
        rbuf[:, cols] = gated
        square = square + gated * gated
        cross = cross + gated * (g_ref[:, cols] * gam_ref[0:1, cols])
    inv = lax.rsqrt(jnp.sum(square, axis=1, keepdims=True) * (1.0 / DI) + norm_eps)
    slope = inv * inv * inv * (jnp.sum(cross, axis=1, keepdims=True) * (1.0 / DI))
    qt = q.T

    @pl.when(first)
    def _():
        dinc_ref[...] = jnp.zeros_like(dinc_ref)
        small_ref[...] = jnp.zeros_like(small_ref)

    for j in range(DI // 128):
        cols = slice(128 * j, 128 * (j + 1))
        gated = rbuf[:, cols]
        scaled = gated * inv
        gam = gam_ref[0:1, cols]
        out_ref[:, cols] = (scaled * gam).astype(bf16)
        g = g_ref[:, cols]
        dgated = inv * (g * gam) - gated * slope
        z = z_ref[:, cols]
        s = sigmoid(z)
        dy = dgated * (z * s)
        dy_ref[:, cols] = dy
        dz = dgated * ybuf[:, cols] * (s * (1.0 + z * (1.0 - s)))
        dz_ref[:, cols] = dz.astype(bf16)
        small_ref[2:3, cols] = jnp.maximum(
            small_ref[2:3, cols], jnp.max(jnp.abs(dz), axis=0, keepdims=True)
        )
        small_ref[0:1, cols] += jnp.sum(g * scaled, axis=0, keepdims=True)
        small_ref[1:2, cols] += jnp.sum(dy * v_ref[:, cols], axis=0, keepdims=True)
        dinc_ref[:, cols] += dot3(qt, dy * pair_lanes(inflow, j))


def gate(y, v, z, g, kq, inc, infd, dirx, gam):
    length = y.shape[0]
    tile = Q
    big = pl.BlockSpec((tile, DI), lambda i: (i, 0))
    return pl.pallas_call(
        gate_kernel,
        grid=(length // tile,),
        in_specs=[
            big, big, big, big,
            pl.BlockSpec((tile, 2 * STATE), lambda i: (i, 0)),
            pl.BlockSpec((STATE, DI), lambda i: (0, 0)),
            pl.BlockSpec((tile, HEADS), lambda i: (i, 0)),
            pl.BlockSpec((8, DI), lambda i: (0, 0)),
            pl.BlockSpec((8, DI), lambda i: (0, 0)),
        ],
        out_specs=(
            big, big, big,
            pl.BlockSpec((STATE, DI), lambda i: (0, 0)),
            pl.BlockSpec((8, DI), lambda i: (0, 0)),
        ),
        out_shape=(
            jax.ShapeDtypeStruct((length, DI), bf16),
            jax.ShapeDtypeStruct((length, DI), f32),
            jax.ShapeDtypeStruct((length + PAD, DI), bf16),
            jax.ShapeDtypeStruct((STATE, DI), f32),
            jax.ShapeDtypeStruct((8, DI), f32),
        ),
        scratch_shapes=[pltpu.VMEM((tile, DI), f32), pltpu.VMEM((tile, DI), f32)],
        compiler_params=params(),
        cost_estimate=pl.CostEstimate(flops=10**9, bytes_accessed=4 * 10**7, transcendentals=4 * 10**6),
        name="gate",
    )(y, v, z, g, kq, inc, infd, dirx, gam)


def back_kernel(
    final, v_ref, dy_ref, kq_ref, delta_ref, cum_ref, cumt_ref, infc_ref, tailc_ref, tailn_ref,
    keep_ref, inc_ref, dout_ref, dir_ref, segc_ref, segr_ref, dkq_in, dgram_in,
    dv_ref, dkq_ref, dgram, ddelta_ref, dcum_ref, drow_ref, flow_ref,
    gram, gramt, bias, biast, kt, qt, states,
):
    length = v_ref.shape[0]
    count = length // Q
    step = pl.program_id(0)

    @pl.when(step == 0)
    def _():
        for c in range(count):
            rows = slice(c * Q, (c + 1) * Q)
            k, q = kq_ref[rows, :STATE], kq_ref[rows, STATE:]
            b, bt = masks_of(segc_ref, segr_ref, rows)
            bias[rows, :] = b
            biast[rows, :] = bt
            scores = dot3(q, k, NT)
            gram[rows, :] = scores
            gramt[rows, :] = scores.T
            kt[:, rows] = k.T
            qt[:, rows] = q.T
        dgram[...] = dgram_in[...]
        dkq_ref[...] = dkq_in[...]

    low = iota((Q, 128), 1) < HEAD_DIM
    lane = iota((Q, GH), 1)
    line = iota((8, GW), 0)

    states[0] = inc_ref[...].astype(f32)
    for c in range(count):
        rows = slice(c * Q, (c + 1) * Q)
        weighted = v_ref[rows, :] * group_lanes(tailc_ref[0, rows, :])
        states[c + 1] = states[c] * keep_ref[c : c + 1, :] + dot3(kt[:, rows], weighted)

    back = dout_ref[...].astype(f32)
    flows = jnp.zeros((8, GW), f32)
    for c in reversed(range(count)):
        rows = slice(c * Q, (c + 1) * Q)
        flows = jnp.where(line == c, jnp.sum(back * states[c + 1], axis=0, keepdims=True), flows)
        delta, cum = delta_ref[0, rows, :], cum_ref[0, rows, :]
        inflow, tailc, tailn = infc_ref[0, rows, :], tailc_ref[0, rows, :], tailn_ref[0, rows, :]
        k, q = kq_ref[rows, :STATE], kq_ref[rows, STATE:]
        before = states[c]
        after = back
        y_in = dot3(q, before)
        w_in = dot3(k, after)
        g, gt, b, bt = gram[rows, :], gramt[rows, :], bias[rows, :], biast[rows, :]
        dg = dgram[rows, :]
        ddelta = jnp.zeros((Q, GH), f32)
        dcum = jnp.zeros((Q, GH), f32)
        dys, ws = [], []
        for j in range(GW // 128):
            cols = slice(128 * j, 128 * (j + 1))
            dy, v = dy_ref[rows, cols], v_ref[rows, cols]
            spread = pair_lanes(delta, j)
            w = v * spread
            stacked = jnp.concatenate(
                [jnp.where(low, dy, 0.0), jnp.where(low, 0.0, dy)], axis=0
            )
            inner = dot3(stacked, w, NT)
            turned = []
            for i in (0, 1):
                h = 2 * j + i
                col, row = cum[:, h : h + 1], cumt_ref[h : h + 1, rows]
                turned.append(gt * jnp.exp(row - col + bt))
                weighed = inner[Q * i : Q * (i + 1), :] * jnp.exp(col - row + b)
                dg = dg + weighed
                full = weighed * g
                dcum = dcum + jnp.where(lane == h, jnp.sum(full, axis=1, keepdims=True), 0.0)
                drow_ref[h : h + 1, rows] = jnp.sum(full, axis=0, keepdims=True)
            dw_in = w_in[:, cols] * pair_lanes(tailn, j)
            dw = dot3(jnp.concatenate(turned, axis=1), stacked) + dw_in
            dv_ref[rows, cols] = spread * dw + dir_ref[0:1, cols] * dy
            dflow = dy * pair_lanes(inflow, j)
            one = dflow * y_in[:, cols] - w * dw_in
            two = v * dw
            for i in (0, 1):
                h = 2 * j + i
                keep = low if i == 0 else jnp.logical_not(low)
                dcum = dcum + jnp.where(
                    lane == h, jnp.sum(jnp.where(keep, one, 0.0), axis=1, keepdims=True), 0.0
                )
                ddelta = ddelta + jnp.where(
                    lane == h, jnp.sum(jnp.where(keep, two, 0.0), axis=1, keepdims=True), 0.0
                )
            dys.append(dflow)
            ws.append(v * pair_lanes(tailc, j))
        dgram[rows, :] = dg
        ddelta_ref[0, rows, :] = ddelta
        dcum_ref[0, rows, :] = dcum
        flowing = jnp.concatenate(dys, axis=1)
        dkq_ref[rows, STATE:] += dot3(flowing, before, NT)
        dkq_ref[rows, :STATE] += dot3(jnp.concatenate(ws, axis=1), after, NT)
        if c:
            back = back * keep_ref[c : c + 1, :] + dot3(qt[:, rows], flowing)
    flow_ref[...] = flows

    @pl.when(jnp.logical_and(step == pl.num_programs(0) - 1, final))
    def _():
        for c in range(count):
            rows = slice(c * Q, (c + 1) * Q)
            k, q = kq_ref[rows, :STATE], kq_ref[rows, STATE:]
            dg = dgram[rows, :]
            dkq_ref[rows, STATE:] += dot3(dg, k)
            dkq_ref[rows, :STATE] += dot3(dg.T, q)


def back_local(
    first, last, held, v, dy, kq, delta, cum, cumt, infc, tailc, tailn, keep, inc, dout, dirx, segc, segr
):
    length = v.shape[0]
    count = length // Q
    groups = last - first
    if held is None:
        held = (jnp.zeros((length, 2 * STATE), f32), jnp.zeros((length, Q), f32))
    cols = pl.BlockSpec((1, length, GH), lambda g: (g + first, 0, 0))
    wide = pl.BlockSpec((length, GW), lambda g: (0, g + first))
    state = pl.BlockSpec((STATE, GW), lambda g: (0, g + first))
    lines = pl.BlockSpec((8, GW), lambda g: (0, g + first))
    turned = pl.BlockSpec((GH, length), lambda g: (g + first, 0))
    whole = pl.BlockSpec((length, 2 * STATE), lambda g: (0, 0))
    table = pl.BlockSpec((length, Q), lambda g: (0, 0))
    square = pltpu.VMEM((length, Q), f32)
    out_cols = pl.BlockSpec((1, length, GH), lambda g: (g, 0, 0))
    return pl.pallas_call(
        functools.partial(back_kernel, last == NG),
        grid=(groups,),
        in_specs=[
            wide, wide, whole, cols, cols, turned, cols, cols, cols, lines, state, state, lines,
            pl.BlockSpec((length, 8), lambda g: (0, 0)),
            pl.BlockSpec((8, length), lambda g: (0, 0)),
            whole, table,
        ],
        out_specs=(
            pl.BlockSpec((length, GW), lambda g: (0, g)), whole, table, out_cols, out_cols,
            pl.BlockSpec((GH, length), lambda g: (g, 0)),
            pl.BlockSpec((8, GW), lambda g: (0, g)),
        ),
        out_shape=(
            jax.ShapeDtypeStruct((length, groups * GW), f32),
            jax.ShapeDtypeStruct((length, 2 * STATE), f32),
            jax.ShapeDtypeStruct((length, Q), f32),
            jax.ShapeDtypeStruct((groups, length, GH), f32),
            jax.ShapeDtypeStruct((groups, length, GH), f32),
            jax.ShapeDtypeStruct((groups * GH, length), f32),
            jax.ShapeDtypeStruct((8, groups * GW), f32),
        ),
        scratch_shapes=[
            square, square, square, square,
            pltpu.VMEM((STATE, length), f32), pltpu.VMEM((STATE, length), f32),
            pltpu.VMEM((count + 1, STATE, GW), f32),
        ],
        compiler_params=params(),
        cost_estimate=pl.CostEstimate(
            flops=groups * 5 * 10**9, bytes_accessed=groups * 5 * 10**6, transcendentals=groups * 10**6
        ),
        name="back_first" if first == 0 else "back_second",
    )(v, dy, kq, delta, cum, cumt, infc, tailc, tailn, keep, inc, dout, dirx, segc, segr, *held)


def step_kernel(
    step_ref, par_ref, ddelta_a, ddelta_b, dcum_a, dcum_b, drow_a, drow_b, flow_a, flow_b,
    dstep_ref, small_ref,
):
    length = ddelta_a.shape[1]
    half = ddelta_a.shape[0]
    upper = (iota((Q, Q), 0) <= iota((Q, Q), 1)).astype(f32)
    eye = (iota((Q, Q), 0) == iota((Q, Q), 1)).astype(f32)
    last = iota((Q, 1), 0) == Q - 1
    rate = jnp.exp(par_ref[1:2, :])
    spread = head_onehot()
    wide = half * GW
    flows = dotf(flow_a[...], spread[:, :wide], NT) + dotf(flow_b[...], spread[:, wide:], NT)
    top = half * GH
    rise = (iota((HEADS, top), 0) == iota((HEADS, top), 1)).astype(f32)
    fall = (iota((HEADS, HEADS - top), 0) == iota((HEADS, HEADS - top), 1) + top).astype(f32)
    times = jnp.zeros((1, HEADS), f32)
    decays = jnp.zeros((1, HEADS), f32)
    most = jnp.zeros((1, HEADS), f32)
    dstep_ref[...] = jnp.zeros_like(dstep_ref)
    for c in range(length // Q):
        rows = slice(c * Q, (c + 1) * Q)
        ddelta = jnp.zeros((Q, HEADS), f32)
        turned = dotf(rise, drow_a[:, rows]) + dotf(fall, drow_b[:, rows])
        dcum = -dotf(eye, turned, NT)
        for g in range(NG):
            place = (iota((GH, HEADS), 0) + g * GH == iota((GH, HEADS), 1)).astype(f32)
            one, two = (ddelta_a[g, rows, :], dcum_a[g, rows, :]) if g < half else (
                ddelta_b[g - half, rows, :], dcum_b[g - half, rows, :]
            )
            ddelta = ddelta + dotf(one, place)
            dcum = dcum + dotf(two, place)
        dcum = dcum + jnp.where(last, flows[c : c + 1, :], 0.0)
        x = step_ref[pl.ds(HALO + c * Q, Q), :HEADS] + par_ref[0:1, :]
        dlog = dotf(upper, dcum) * rate
        decays = decays - jnp.sum(dlog * softplus(x), axis=0, keepdims=True)
        dstep = (ddelta - dlog) * sigmoid(x)
        times = times + jnp.sum(dstep, axis=0, keepdims=True)
        most = jnp.maximum(most, jnp.max(jnp.abs(dstep), axis=0, keepdims=True))
        dstep_ref[rows, :HEADS] = dstep.astype(bf16)
    dstep_ref[pl.ds(length, PAD), :HEADS] = jnp.broadcast_to(most * 1.01, (PAD, HEADS)).astype(bf16)
    small_ref[...] = jnp.zeros_like(small_ref)
    small_ref[0:1, :] = times
    small_ref[1:2, :] = decays


def step_back(rest, pars, first, second):
    length = first[0].shape[1]
    arrays = [part for both in zip(first, second) for part in both]
    shapes = (
        jax.ShapeDtypeStruct((length + PAD, 128), bf16),
        jax.ShapeDtypeStruct((8, HEADS), f32),
    )
    return pl.pallas_call(
        step_kernel,
        grid=(1,),
        in_specs=[steps_of(rest), whole(pars)] + [whole(array) for array in arrays],
        out_specs=tuple(whole(shape) for shape in shapes),
        out_shape=shapes,
        compiler_params=params(),
        cost_estimate=pl.CostEstimate(flops=10**7, bytes_accessed=10**7, transcendentals=10**5),
        name="step_back",
    )(rest, pars, *arrays)


def unconv_kernel(mixed, x_ref, tap_ref, match_ref, dv_ref, dkq_ref, dx_ref, edge_ref, dtap_ref, *held):
    length = match_ref.shape[1]
    count = length // Q
    wide = pl.program_id(0) < mixed
    for buf in held:
        buf[0:HALO, :] = jnp.zeros((HALO, TILE), f32)
        buf[HALO + length :, :] = jnp.zeros((HALO, TILE), f32)
    for j in range(TILE // 128):
        cols = slice(128 * j, 128 * (j + 1))
        sums = [jnp.zeros((1, 128), f32) for _ in range(KW + 1)]
        for c in range(count):
            rows = slice(c * Q, (c + 1) * Q)
            s = conv_sum(x_ref, tap_ref, match_ref, c * Q, Q, cols)
            sig = sigmoid(s)
            dm = jnp.where(wide, dv_ref[rows, cols], dkq_ref[rows, cols])
            ds = dm * (sig * (1.0 + s * (1.0 - sig)))
            sums[KW] = sums[KW] + jnp.sum(ds, axis=0, keepdims=True)
            for k in range(KW):
                e = ds if k == KW - 1 else ds * match_ref[k, rows, :]
                held[k][HALO + c * Q : HALO + (c + 1) * Q, cols] = e
                taken = x_ref[pl.ds(HALO - (KW - 1) + k + c * Q, Q), cols]
                sums[k] = sums[k] + jnp.sum(e * taken, axis=0, keepdims=True)
        for k in range(KW + 1):
            dtap_ref[k : k + 1, cols] = sums[k]

        def placed(start, rows):
            total = None
            for k in range(KW):
                term = tap_ref[k : k + 1, cols] * held[k][pl.ds(start + KW - 1 - k, rows), cols]
                total = term if total is None else total + term
            return total

        edge_ref[0:HALO, cols] = placed(0, HALO)
        most = jnp.zeros((1, 128), f32)
        for c in range(count):
            dx = placed(HALO + c * Q, Q)
            most = jnp.maximum(most, jnp.max(jnp.abs(dx), axis=0, keepdims=True))
            dx_ref[c * Q : (c + 1) * Q, cols] = dx.astype(bf16)
            if c == count - 1:
                edge_ref[HALO:, cols] = dx[Q - HALO :, :]
        dtap_ref[KW + 1 : KW + 2, cols] = most
    dtap_ref[KW + 2 :, :] = jnp.zeros((8 - KW - 2, TILE), f32)


def unconv(first, rest, taps, match, dv, dkq):
    length = match.shape[1]
    high = length + HALO
    mixed = dv.shape[1] // TILE
    tiles = mixed if dkq is None else mixed + 1
    lone = dv if dkq is None else dkq
    return pl.pallas_call(
        functools.partial(unconv_kernel, mixed),
        grid=(tiles,),
        in_specs=[
            pl.BlockSpec((high, TILE), lambda j: (0, j + first)),
            pl.BlockSpec((8, TILE), lambda j: (0, j + first)),
            pl.BlockSpec((KW - 1, length, 128), lambda j: (0, 0, 0)),
            pl.BlockSpec((length, TILE), lambda j: (0, jnp.minimum(j, mixed - 1))),
            pl.BlockSpec((length, TILE), lambda j: (0, 0)),
        ],
        out_specs=(
            pl.BlockSpec((length, TILE), lambda j: (0, j)),
            pl.BlockSpec((2 * HALO, TILE), lambda j: (0, j)),
            pl.BlockSpec((8, TILE), lambda j: (0, j)),
        ),
        out_shape=(
            jax.ShapeDtypeStruct((length + PAD, tiles * TILE), bf16),
            jax.ShapeDtypeStruct((2 * HALO, tiles * TILE), f32),
            jax.ShapeDtypeStruct((8, tiles * TILE), f32),
        ),
        scratch_shapes=[pltpu.VMEM((length + 2 * HALO, TILE), f32) for _ in range(KW)],
        compiler_params=params(),
        cost_estimate=pl.CostEstimate(flops=10**8, bytes_accessed=10**7, transcendentals=10**6),
    )(rest, taps, match, dv, lone)


def adamw(param, grad, moment, square, rate, shrink):
    moment_new = beta_one * moment + (1.0 - beta_one) * grad
    square_new = beta_two * square + (1.0 - beta_two) * grad * grad
    first_corr = 1.0 - beta_one**ADAM_STEP
    second_corr = 1.0 - beta_two**ADAM_STEP
    update = moment_new / first_corr / (jnp.sqrt(square_new / second_corr) + adam_eps)
    return (param - rate * (update + shrink * param), moment_new, square_new)


def shifted(value, axis, by):
    count = lax.axis_size(axis)
    pairs = [(i, i + by) for i in range(count) if 0 <= i + by < count]
    return lax.ppermute(value, axis, pairs)


TOKENS = (((0,), (0,)), ((), ()))


def gathered(value):
    return lax.all_gather(value, "dp", axis=0, tiled=True)


def shard_gathered(value):
    count, here = lax.axis_size("shard"), lax.axis_index("shard")
    rows, width = value.shape
    held = jnp.zeros((count * rows, width), value.dtype)
    for k in range(count):
        part = exchanged(value, "shard", k) if k else value
        held = lax.dynamic_update_slice(held, part, ((here ^ k) * rows, 0))
    return held


def exchanged(value, axis, by):
    return lax.ppermute(value, axis, [(i, i ^ by) for i in range(lax.axis_size(axis))])


def relative(value, block, core):
    base = lax.axis_index("dp") // 2
    length = value.shape[0]
    return [
        lax.dynamic_slice(value, (0, (((j ^ base) * 2) + core) * block), (length, block))
        for j in range(lax.axis_size("dp") // 2)
    ]


def both_cores(value):
    return jnp.concatenate([value, exchanged(value, "dp", 1)], axis=0)


def own_and_partner(value, block):
    core = lax.axis_index("dp") % 2
    return relative(value, block, core), relative(value, block, 1 - core)


def exponent(bound):
    return jnp.ceil(jnp.log2(jnp.maximum(bound, 1e-30)))


def coded(total, power, rows):
    own = iota(total.shape, 0) < rows
    return jnp.where(own, total * jnp.exp2(15.0 - power), power).astype(jnp.float16)


def decoded(payload, rows):
    power = payload[rows : rows + 1].astype(f32)
    return payload.astype(f32) * jnp.exp2(power - 15.0), power


def after(value, *earlier):
    return lax.optimization_barrier((value, earlier))[0]


def split_plan(order):
    kept, sends = [0], []
    for bit in reversed(order):
        send = [j ^ (1 << bit) for j in kept]
        sends.insert(0, send)
        kept = kept + send
    return kept, sends


def columns_of(blocks, order):
    kept, sends = split_plan(order)
    zeros = jnp.zeros((blocks[0].shape[0], PAD), bf16)
    return (
        jnp.concatenate([blocks[j] for j in sends[0]] + [zeros], axis=1),
        jnp.concatenate([blocks[j] for j in kept[: len(sends[0])]] + [zeros], axis=1),
    )


class Sum:
    def __init__(self, sent, held, rhs, bound, order):
        self.sent, self.held, self.rhs = sent, held, rhs
        self.power = exponent(bound)
        self.order = order
        self.rows = 2 * (sent.shape[1] - PAD)
        self.total = None
        self.at = 0

    def prepare(self):
        self.rows //= 2
        if self.total is None:
            part = lax.dot_general(self.sent, self.rhs, TOKENS, preferred_element_type=f32)
        else:
            part = self.total[self.rows : 2 * self.rows + PAD]
        self.payload = coded(part, self.power, self.rows)

    def send(self):
        self.got = exchanged(self.payload, "dp", 2 << self.order[self.at])
        self.at += 1
        if self.total is None:
            self.total = lax.dot_general(self.held, self.rhs, TOKENS, preferred_element_type=f32)

    def take(self, *earlier):
        got, other = decoded(after(self.got, earlier), self.rows)
        self.total = self.total[: self.rows + PAD] + got
        self.power = jnp.maximum(self.power, other) + 1.0

    def more(self):
        return self.at < len(self.order)

    def finish(self):
        while self.more():
            self.prepare()
            self.send()
            self.take()


class ShardSum:
    def __init__(self, sums):
        count, here = lax.axis_size("shard"), lax.axis_index("shard")
        self.rows = sums[0].rows // count
        self.total = jnp.concatenate([one.total for one in sums], axis=1) if len(sums) > 1 else sums[0].total
        power = jnp.concatenate([one.power for one in sums], axis=1) if len(sums) > 1 else sums[0].power
        width = self.total.shape[1]
        self.payloads = [
            coded(
                lax.dynamic_slice(self.total, ((here ^ k) * self.rows, 0), (self.rows + PAD, width)),
                power, self.rows,
            )
            for k in range(1, count)
        ]
        self.parts = [exchanged(part, "shard", k + 1) for k, part in enumerate(self.payloads)]

    def take(self, *earlier):
        here = lax.axis_index("shard")
        result = lax.dynamic_slice(self.total, (here * self.rows, 0), (self.rows, self.total.shape[1]))
        for part in self.parts:
            result = result + decoded(after(part, earlier), self.rows)[0][: self.rows]
        return result


def summed(value):
    for axis in ("dp", "shard"):
        count = lax.axis_size(axis)
        if count & (count - 1):
            value = lax.psum(value, axis)
            continue
        by = 1
        while by < count:
            value = value + lax.ppermute(value, axis, [(i, i ^ by) for i in range(count)])
            by *= 2
    return value


def carried(state, factor, by):
    incoming = shifted(state.astype(bf16), "shard", by)
    for _ in range(lax.axis_size("shard") - 2):
        incoming = shifted((state + factor * incoming.astype(f32)).astype(bf16), "shard", by)
    return incoming


def both_with_most(rows):
    length = rows.shape[0] - PAD
    arrived = exchanged(rows, "dp", 1)
    most = jnp.maximum(rows[length : length + 1], arrived[length : length + 1]).astype(f32)
    return jnp.concatenate([rows[:length], arrived[:length]], axis=0), most


def mended(dx, edge, dtap, length):
    last = edge[HALO:] + shifted(edge[:HALO], "shard", -1)
    most = jnp.maximum(dtap[KW + 1 : KW + 2], jnp.max(jnp.abs(last), axis=0, keepdims=True)) * 1.01
    tail = jnp.concatenate([last, jnp.broadcast_to(most, (PAD, most.shape[1]))], axis=0).astype(bf16)
    return lax.dynamic_update_slice(dx, tail, (length - HALO, 0)), dtap


def rest_sums(both, bound, in_columns, orders):
    middle = both.shape[1] // 256 * 128
    return [
        Sum(*in_columns[0], both[:, :middle], bound[:, :middle], orders[0]),
        Sum(*in_columns[1], both[:, middle:], bound[:, middle:], orders[1]),
    ]


def shards(
    hidden_in, cotangent, segment_ids,
    param_prenorm, param_inputs, param_kernel, param_offsets, param_timestep, param_decays,
    param_direct, param_gating, param_outputs,
    moment_prenorm, moment_inputs, moment_kernel, moment_offsets, moment_timestep, moment_decays,
    moment_direct, moment_gating, moment_outputs,
    square_prenorm, square_inputs, square_kernel, square_offsets, square_timestep, square_decays,
    square_direct, square_gating, square_outputs,
):
    length, width = hidden_in.shape
    own_inputs = param_inputs.astype(bf16)
    spare = -(param_inputs.shape[1] - DI) % 128
    rest_rows = shard_gathered(jnp.pad(own_inputs[:, DI:], ((0, 0), (0, spare))))
    rest_w = gathered(rest_rows)
    gate_rows = shard_gathered(after(own_inputs[:, :DI], rest_rows))
    gate_w = gathered(gate_rows)
    out_w = gathered(shard_gathered(after(param_outputs.astype(bf16), gate_rows)))

    seg = segment_ids.astype(f32)
    ends = jnp.pad(seg[length - HALO :], (0, width - HALO))[None, :]
    halo = shifted(
        jnp.concatenate([hidden_in[length - HALO :], jnp.broadcast_to(ends, (HALO, width))], axis=0),
        "shard", 1,
    )
    rim_seg = jnp.where(lax.axis_index("shard") == 0, -1.0, halo[HALO, :HALO])
    rim = rim_seg[HALO - 1]
    all_segs = jnp.concatenate([rim_seg, seg])
    match = jnp.stack(
        [
            (all_segs[HALO - (KW - 1) + k : HALO - (KW - 1) + k + length] == seg).astype(f32)
            for k in range(KW - 1)
        ]
    )
    match = jnp.broadcast_to(match[:, :, None], (KW - 1, length, 128))
    chunks = seg.reshape(-1, Q)
    before = jnp.concatenate([rim[None], chunks[:-1, Q - 1]])
    mask = jnp.stack(
        [
            (chunks == before[:, None]).reshape(-1),
            (chunks == chunks[:, Q - 1 :]).reshape(-1),
            seg == rim,
            seg == seg[length - 1],
        ]
        + [seg < -1.0] * 4,
        axis=1,
    ).astype(f32)
    segc = jnp.broadcast_to(seg[:, None], (length, 8))
    segr = jnp.broadcast_to(seg[None, :], (8, length))

    taps = jnp.concatenate([param_kernel, param_offsets[None, :], jnp.zeros((8 - KW - 1, CH), f32)], axis=0)
    pars = jnp.concatenate([param_timestep[None, :], param_decays[None, :], jnp.zeros((6, HEADS), f32)], axis=0)
    dirx = jnp.broadcast_to(jnp.repeat(param_direct, HEAD_DIM)[None, :], (8, DI))
    gam = jnp.broadcast_to(param_gating[None, :], (8, DI))

    hidden = jnp.concatenate([halo[:HALO], hidden_in], axis=0)
    inv = lax.rsqrt(jnp.mean(hidden * hidden, axis=1, keepdims=True) + norm_eps)
    normed = (hidden * inv * param_prenorm).astype(bf16)
    own_normed = normed[HALO:]
    upstream = cotangent.astype(bf16)

    groups = lax.axis_size("shard")
    spots = [bit for bit in range(20) if (2 << bit) < lax.axis_size("dp")]
    orders = (spots, spots[::-1])
    in_block, out_block = groups * param_inputs.shape[0], groups * param_outputs.shape[0]
    up_both = both_cores(upstream)
    own_blocks, partner_blocks = own_and_partner(own_normed, in_block)
    arrived = exchanged(jnp.concatenate(partner_blocks, axis=1), "dp", 1)
    both_blocks = [
        jnp.concatenate([one, arrived[:, j * in_block : (j + 1) * in_block]], axis=0)
        for j, one in enumerate(own_blocks)
    ]
    in_columns = [columns_of(both_blocks, order) for order in orders]
    norm_bound = 2.02 * length * width**0.5 * jnp.max(jnp.abs(param_prenorm))
    out_bound = 2.02 * length * DI**0.5 * jnp.max(jnp.abs(param_gating))
    out_bound = out_bound * jnp.max(jnp.abs(up_both), axis=0, keepdims=True).astype(f32)
    rest_w = after(
        rest_w, match, mask, segc, segr, taps, pars, dirx, gam, up_both, out_bound, norm_bound, in_columns
    )

    rest = jnp.dot(normed, rest_w, preferred_element_type=f32)
    delta, cum, cumt, infc, tailc, tailn, taild, infd, keep, factor = prep(rest, pars, mask)
    v, kq, state = conv_state(rest, taps, match, taild)
    incoming = carried(state, factor[0:1], 1)
    y = local_out(v, kq, delta, cum, cumt, infc, tailc, keep, segc, segr)
    gate_w = after(gate_w, y)
    z = jnp.dot(own_normed, gate_w, preferred_element_type=f32)
    out_w = after(out_w, z)
    back_gated = lax.dot_general(upstream, out_w, NT, preferred_element_type=f32)
    gated, dy, dz, dinc, small = gate(y, v, z, back_gated, kq, incoming, infd, dirx, gam)

    outgoing = carried(dinc, factor[0:1], -1)
    own_blocks, partner_blocks = own_and_partner(gated, out_block)
    out_columns = [
        jnp.concatenate([mine, exchanged(theirs, "dp", 1)], axis=0)
        for mine, theirs in zip(columns_of(own_blocks, spots), columns_of(partner_blocks, spots))
    ]
    dz_most = jnp.broadcast_to(small[2:3] * 1.01, (PAD, DI)).astype(bf16)
    dz = lax.dynamic_update_slice(dz, dz_most, (length, 0))
    dz_both, dz_bound = both_with_most(dz)
    dz = dz[:length]
    block_out = hidden_in + jnp.dot(gated, out_w, preferred_element_type=f32)
    out_sum = Sum(*out_columns, up_both, out_bound, spots)
    gate_sum = Sum(*in_columns[1], dz_both, norm_bound * dz_bound, spots[::-1])
    first_sums = [out_sum, gate_sum]
    for one in first_sums:
        one.prepare()
        one.send()
    back_normed = lax.dot_general(dz, gate_w, NT, preferred_element_type=f32)
    outgoing = after(
        outgoing, out_sum.payload, gate_sum.payload, out_sum.total, gate_sum.total, back_normed, block_out
    )

    ssm = (kq, delta, cum, cumt, infc, tailc, tailn, keep, incoming)
    half = NG // 2
    dv1, *held1 = back_local(0, half, None, v, dy, *ssm, outgoing, dirx, segc, segr)
    for one in first_sums:
        one.take(dv1)
        if one.more():
            one.prepare()
            one.send()
    dv1 = after(dv1, *[one.payload for one in first_sums])
    drest1, dtap1 = mended(*unconv(0, rest, taps, match, dv1, None), length)
    both1, bound1 = both_with_most(drest1)
    sums1 = rest_sums(both1, norm_bound * bound1, in_columns, orders)
    for one in sums1:
        one.prepare()
        one.send()
    dy = after(dy, *[one.payload for one in sums1], *[one.total for one in sums1])
    dv2, *held2 = back_local(half, NG, held1[:2], v, dy, *ssm, outgoing, dirx, segc, segr)
    for one in first_sums:
        one.take(dv2)
        one.finish()
    shard_out, shard_gate = ShardSum([out_sum]), ShardSum([gate_sum])
    for one in sums1:
        one.take(dv2, shard_out.payloads, shard_gate.payloads)
        if one.more():
            one.prepare()
            one.send()
    dv2 = after(dv2, *[one.payload for one in sums1])
    dstep, small_step = step_back(rest, pars, held1[2:], held2[2:])
    drest2, dtap2 = mended(*unconv(dv1.shape[1] // TILE, rest, taps, match, dv2, held2[0]), length)
    drest2 = jnp.concatenate([drest2, dstep], axis=1)
    both2, bound2 = both_with_most(drest2)
    sums2 = rest_sums(both2, norm_bound * bound2, in_columns, orders)
    for one in sums2:
        one.prepare()
        one.send()
    for one in sums1:
        one.take([two.payload for two in sums2])
        one.finish()
    shard1 = ShardSum(sums1)
    drest1, drest2 = after((drest1, drest2), shard1.payloads, [two.payload for two in sums2])
    wide1 = drest1.shape[1]
    back_normed = back_normed + lax.dot_general(drest1[:length], rest_w[:, :wide1], NT, preferred_element_type=f32)
    back_normed = back_normed + lax.dot_general(drest2[:length], rest_w[:, wide1:], NT, preferred_element_type=f32)
    grad_outputs = shard_out.take(back_normed)
    grad_gate = shard_gate.take(back_normed)
    for one in sums2:
        one.take(back_normed, grad_outputs, grad_gate)
        one.finish()
    shard2 = ShardSum(sums2)
    sent = shard2.payloads
    grad_rest = jnp.concatenate([shard1.take(sent), shard2.take()], axis=1)
    grad_inputs = jnp.concatenate([grad_gate, grad_rest[:, : param_inputs.shape[1] - DI]], axis=1)
    dtap = jnp.concatenate([dtap1, dtap2], axis=1)

    own_inv = inv[HALO:]
    scaled = hidden_in * own_inv
    gained = back_normed * param_prenorm
    hidden_grad = cotangent + own_inv * (
        gained - scaled * jnp.mean(gained * scaled, axis=1, keepdims=True)
    )
    grad_prenorm = jnp.sum(back_normed * scaled, axis=0)

    pieces = [
        grad_prenorm,
        dtap[:KW].reshape(-1),
        dtap[KW],
        small_step[0],
        small_step[1],
        jnp.sum(small[1].reshape(HEADS, HEAD_DIM), axis=1),
        small[0],
    ]
    flat = after(jnp.concatenate(pieces), sent)
    count = flat.shape[0]
    lines = -(-count // 1024) * 8
    total = summed(jnp.pad(flat, (0, lines * 128 - count)).reshape(lines, 128)).reshape(-1)
    found, at = [], 0
    for piece in pieces:
        found.append(total[at : at + piece.shape[0]])
        at += piece.shape[0]
    grad_prenorm, grad_kernel, grad_offsets, grad_timestep, grad_decays, grad_direct, grad_gating = found
    grad_kernel = grad_kernel.reshape(KW, CH)

    params = (
        param_prenorm, param_inputs, param_kernel, param_offsets, param_timestep, param_decays,
        param_direct, param_gating, param_outputs,
    )
    moments = (
        moment_prenorm, moment_inputs, moment_kernel, moment_offsets, moment_timestep, moment_decays,
        moment_direct, moment_gating, moment_outputs,
    )
    squares = (
        square_prenorm, square_inputs, square_kernel, square_offsets, square_timestep, square_decays,
        square_direct, square_gating, square_outputs,
    )
    grads = (
        grad_prenorm, grad_inputs, grad_kernel, grad_offsets, grad_timestep, grad_decays,
        grad_direct, grad_gating, grad_outputs,
    )
    updated = [
        adamw(params[i], grads[i], moments[i], squares[i], rate_table[i], shrink_table[i])
        for i in range(9)
    ]
    return (
        (block_out, hidden_grad)
        + grads
        + tuple(u[0] for u in updated)
        + tuple(u[1] for u in updated)
        + tuple(u[2] for u in updated)
    )


def solution(mesh):
    rows = P(("dp", "shard"), None)
    member = (P(), rows, P(), P(), P(), P(), P(), P(), rows)

    return jax.shard_map(
        shards,
        mesh=mesh,
        in_specs=(rows, rows, P(("dp", "shard"))) + member * 3,
        out_specs=(rows, rows) + member * 4,
        check_vma=False,
    )
```

```python
import functools

import jax
import jax.numpy as jnp
from jax import lax
from jax.experimental import pallas as pl
from jax.experimental.pallas import tpu as pltpu
from jax.sharding import PartitionSpec as P


HEADS = 48
HEAD_DIM = 64
STATE = 128
KW = 4
ADAM_STEP = 10
DI = 3072
CH = 3328

Q = 128
GH = 8
GW = GH * HEAD_DIM
NG = HEADS // GH
HALO = 8
PAD = 16
TILE = 256

bf16 = jnp.bfloat16
f32 = jnp.float32
highest = lax.Precision.HIGHEST

norm_eps = 1e-05
beta_one = 0.9
beta_two = 0.95
adam_eps = 1e-08
rate_table = (0.2, 0.01, 0.2, 0.2, 0.2, 0.2, 0.2, 0.2, 0.01)
shrink_table = (0.0, 0.1, 0.1, 0.0, 0.0, 0.0, 0.0, 0.0, 0.1)

NN = (((1,), (0,)), ((), ()))
NT = (((1,), (1,)), ((), ()))


def halves(x):
    hi = x.astype(bf16)
    return hi, (x - hi.astype(f32)).astype(bf16)


def dot1(a, b, dims=NN):
    return lax.dot_general(a.astype(bf16), b.astype(bf16), dims, preferred_element_type=f32)


def dot3(a, b, dims=NN):
    ah, al = halves(a)
    bh, bl = halves(b)
    return dot1(ah, bh, dims) + (dot1(ah, bl, dims) + dot1(al, bh, dims))


def dotf(a, b, dims=NN):
    return lax.dot_general(a, b, dims, precision=highest, preferred_element_type=f32)


def iota(shape, dim):
    return lax.broadcasted_iota(jnp.int32, shape, dim)


def sigmoid(x):
    return 1.0 / (1.0 + jnp.exp(-x))


def softplus(x):
    u = jnp.exp(-jnp.abs(x))
    series = u * (1.0 - u * (0.5 - u * (1.0 / 3.0 - u * (0.25 - u * 0.2))))
    return jnp.maximum(x, 0.0) + jnp.where(u < 0.03, series, jnp.log(1.0 + u))


def pair_lanes(cols, j):
    rows = cols.shape[0]
    low = iota((rows, 128), 1) < HEAD_DIM
    return jnp.where(low, cols[:, 2 * j : 2 * j + 1], cols[:, 2 * j + 1 : 2 * j + 2])


def group_lanes(cols):
    return jnp.concatenate([pair_lanes(cols, j) for j in range(cols.shape[1] // 2)], axis=1)


def head_onehot():
    return (iota((HEADS, DI), 1) // HEAD_DIM == iota((HEADS, DI), 0)).astype(f32)


def params(limit=60000, **kw):
    return pltpu.CompilerParams(vmem_limit_bytes=limit * 1024, **kw)


def prep_kernel(
    step_ref, par_ref, mask_ref, delta_ref, cum_ref, cumt_ref, infc_ref, tailc_ref, tailn_ref,
    taild_ref, infd_ref, keep_ref, factor_ref,
):
    length = mask_ref.shape[0]
    count = length // Q
    tri = (iota((Q, Q), 0) >= iota((Q, Q), 1)).astype(f32)
    eye = (iota((HEADS, HEADS), 0) == iota((HEADS, HEADS), 1)).astype(f32)
    rate = jnp.exp(par_ref[1:2, :])
    base = jnp.zeros((1, HEADS), f32)
    held = []
    keeps = []
    for c in range(count):
        rows = slice(c * Q, (c + 1) * Q)
        delta = softplus(step_ref[pl.ds(HALO + c * Q, Q), :HEADS] + par_ref[0:1, :])
        cum = dotf(tri, -delta * rate)
        cumt_ref[:, rows] = dotf(eye, cum, NT)
        last = cum[Q - 1 : Q, :]
        alive, ending = mask_ref[rows, 0:1], mask_ref[rows, 1:2]
        infc = jnp.exp(cum) * alive
        tailn = jnp.exp(last - cum) * ending
        tailc = tailn * delta
        for g in range(NG):
            part = slice(g * GH, (g + 1) * GH)
            delta_ref[g, rows, :] = delta[:, part]
            cum_ref[g, rows, :] = cum[:, part]
            infc_ref[g, rows, :] = infc[:, part]
            tailn_ref[g, rows, :] = tailn[:, part]
            tailc_ref[g, rows, :] = tailc[:, part]
        keeps.append(infc[Q - 1 : Q, :])
        whole = cum + base
        infd_ref[rows, :] = jnp.exp(whole) * mask_ref[rows, 2:3]
        held.append((whole, delta))
        base = base + last
    for c in range(count):
        rows = slice(c * Q, (c + 1) * Q)
        whole, delta = held[c]
        taild = jnp.exp(base - whole) * mask_ref[rows, 3:4] * delta
        for g in range(NG):
            taild_ref[g, rows, :] = taild[:, g * GH : (g + 1) * GH]
    factor = jnp.exp(base) * mask_ref[length - 1 : length, 2:3]
    spread = head_onehot()
    line = iota((8, HEADS), 0)
    table = jnp.zeros((8, HEADS), f32)
    for c in range(count):
        table = jnp.where(line == c, keeps[c], table)
    keep_ref[...] = dotf(table, spread)
    factor_ref[...] = dotf(jnp.where(line == 0, factor, 0.0), spread)


def whole(array):
    return pl.BlockSpec(array.shape, lambda i: (0,) * array.ndim)


def steps_of(rest):
    return pl.BlockSpec((rest.shape[0], 128), lambda i: (0, CH // 128))


def prep(rest, pars, mask):
    length = mask.shape[0]
    cols = jax.ShapeDtypeStruct((NG, length, GH), f32)
    wide = jax.ShapeDtypeStruct((8, DI), f32)
    shapes = (
        cols, cols, jax.ShapeDtypeStruct((HEADS, length), f32), cols, cols, cols, cols,
        jax.ShapeDtypeStruct((length, HEADS), f32), wide, wide,
    )
    return pl.pallas_call(
        prep_kernel,
        grid=(1,),
        in_specs=[steps_of(rest), whole(pars), whole(mask)],
        out_specs=tuple(whole(shape) for shape in shapes),
        out_shape=shapes,
        compiler_params=params(),
        cost_estimate=pl.CostEstimate(flops=10**7, bytes_accessed=10**7, transcendentals=10**5),
        name="prep",
    )(rest, pars, mask)


def conv_sum(x_ref, tap_ref, match_ref, start, rows, cols):
    total = tap_ref[KW : KW + 1, cols] + tap_ref[KW - 1 : KW, cols] * x_ref[
        pl.ds(HALO + start, rows), cols
    ]
    for k in range(KW - 1):
        taken = x_ref[pl.ds(HALO - (KW - 1) + k + start, rows), cols]
        total = total + tap_ref[k : k + 1, cols] * (taken * match_ref[k, pl.ds(start, rows), :])
    return total


def conv_kernel(
    xv_ref, xk_ref, tv_ref, tk_ref, match_ref, taild_ref, v_ref, kq_ref, state_ref, kt_hi, kt_lo
):
    length = v_ref.shape[0]
    count = length // Q

    @pl.when(pl.program_id(0) == 0)
    def _():
        for c in range(count):
            for j in range(2):
                cols = slice(128 * j, 128 * (j + 1))
                s = conv_sum(xk_ref, tk_ref, match_ref, c * Q, Q, cols)
                m = s * sigmoid(s)
                kq_ref[c * Q : (c + 1) * Q, cols] = m
                if j == 0:
                    hi, lo = halves(m.T)
                    kt_hi[:, c * Q : (c + 1) * Q] = hi
                    kt_lo[:, c * Q : (c + 1) * Q] = lo

    total = jnp.zeros((STATE, GW), f32)
    for c in range(count):
        rows = slice(c * Q, (c + 1) * Q)
        tail = taild_ref[0, rows, :]
        parts = []
        for j in range(GW // 128):
            cols = slice(128 * j, 128 * (j + 1))
            s = conv_sum(xv_ref, tv_ref, match_ref, c * Q, Q, cols)
            m = s * sigmoid(s)
            v_ref[rows, cols] = m
            parts.append(m * pair_lanes(tail, j))
        hi, lo = halves(jnp.concatenate(parts, axis=1))
        kh, kl = kt_hi[:, rows], kt_lo[:, rows]
        total = total + (dot1(kh, hi) + (dot1(kh, lo) + dot1(kl, hi)))
    state_ref[...] = total


def conv_state(rest, taps, match, taild):
    length = match.shape[1]
    high = length + HALO
    kq_at = DI // (2 * STATE)
    return pl.pallas_call(
        conv_kernel,
        grid=(NG,),
        in_specs=[
            pl.BlockSpec((high, GW), lambda g: (0, g)),
            pl.BlockSpec((high, 2 * STATE), lambda g: (0, kq_at)),
            pl.BlockSpec((8, GW), lambda g: (0, g)),
            pl.BlockSpec((8, 2 * STATE), lambda g: (0, kq_at)),
            pl.BlockSpec((KW - 1, length, 128), lambda g: (0, 0, 0)),
            pl.BlockSpec((1, length, GH), lambda g: (g, 0, 0)),
        ],
        out_specs=(
            pl.BlockSpec((length, GW), lambda g: (0, g)),
            pl.BlockSpec((length, 2 * STATE), lambda g: (0, 0)),
            pl.BlockSpec((STATE, GW), lambda g: (0, g)),
        ),
        out_shape=(
            jax.ShapeDtypeStruct((length, DI), f32),
            jax.ShapeDtypeStruct((length, 2 * STATE), f32),
            jax.ShapeDtypeStruct((STATE, DI), f32),
        ),
        scratch_shapes=[pltpu.VMEM((STATE, length), bf16), pltpu.VMEM((STATE, length), bf16)],
        compiler_params=params(),
        cost_estimate=pl.CostEstimate(flops=2 * 10**9, bytes_accessed=2 * 10**7, transcendentals=2 * 10**6),
        name="conv_state",
    )(rest, rest, taps, taps, match, taild)


def masks_of(segc_ref, segr_ref, rows):
    same = segc_ref[rows, 0:1] == segr_ref[0:1, rows]
    later = iota((Q, Q), 0) >= iota((Q, Q), 1)
    earlier = iota((Q, Q), 0) <= iota((Q, Q), 1)
    return jnp.where(same & later, 0.0, -1e30), jnp.where(same & earlier, 0.0, -1e30)


def local_kernel(
    v_ref, kq_ref, delta_ref, cum_ref, cumt_ref, infc_ref, tailc_ref, keep_ref, segc_ref, segr_ref,
    y_ref, gram, bias, kt,
):
    length = v_ref.shape[0]
    count = length // Q

    @pl.when(pl.program_id(0) == 0)
    def _():
        for c in range(count):
            rows = slice(c * Q, (c + 1) * Q)
            k, q = kq_ref[rows, :STATE], kq_ref[rows, STATE:]
            bias[rows, :] = masks_of(segc_ref, segr_ref, rows)[0]
            gram[rows, :] = dot3(q, k, NT)
            kt[:, rows] = k.T

    low = iota((Q, 128), 1) < HEAD_DIM
    state = None
    for c in range(count):
        rows = slice(c * Q, (c + 1) * Q)
        delta, cum, tail, inflow = (r[0, rows, :] for r in (delta_ref, cum_ref, tailc_ref, infc_ref))
        g, b = gram[rows, :], bias[rows, :]
        if c:
            carried = dot3(kq_ref[rows, STATE:], state)
        tails = []
        for j in range(GW // 128):
            cols = slice(128 * j, 128 * (j + 1))
            v = v_ref[rows, cols]
            w = v * pair_lanes(delta, j)
            both = []
            for i in (2 * j, 2 * j + 1):
                both.append((g * jnp.exp(cum[:, i : i + 1] - cumt_ref[i : i + 1, rows] + b)))
            stacked = jnp.concatenate([jnp.where(low, w, 0.0), jnp.where(low, 0.0, w)], axis=0)
            y = dot3(jnp.concatenate(both, axis=1), stacked)
            if c:
                y = y + carried[:, cols] * pair_lanes(inflow, j)
            y_ref[rows, cols] = y
            if c < count - 1:
                tails.append(v * pair_lanes(tail, j))
        if c < count - 1:
            fresh = dot3(kt[:, rows], jnp.concatenate(tails, axis=1))
            state = fresh if state is None else state * keep_ref[c : c + 1, :] + fresh


def local_out(v, kq, delta, cum, cumt, infc, tailc, keep, segc, segr):
    length = v.shape[0]
    cols = pl.BlockSpec((1, length, GH), lambda g: (g, 0, 0))
    return pl.pallas_call(
        local_kernel,
        grid=(NG,),
        in_specs=[
            pl.BlockSpec((length, GW), lambda g: (0, g)),
            pl.BlockSpec((length, 2 * STATE), lambda g: (0, 0)),
            cols, cols,
            pl.BlockSpec((GH, length), lambda g: (g, 0)),
            cols, cols,
            pl.BlockSpec((8, GW), lambda g: (0, g)),
            pl.BlockSpec((length, 8), lambda g: (0, 0)),
            pl.BlockSpec((8, length), lambda g: (0, 0)),
        ],
        out_specs=pl.BlockSpec((length, GW), lambda g: (0, g)),
        out_shape=jax.ShapeDtypeStruct((length, DI), f32),
        scratch_shapes=[
            pltpu.VMEM((length, Q), f32), pltpu.VMEM((length, Q), f32),
            pltpu.VMEM((STATE, length), f32),
        ],
        compiler_params=params(),
        cost_estimate=pl.CostEstimate(flops=2 * 10**9, bytes_accessed=2 * 10**7, transcendentals=4 * 10**6),
        name="local_out",
    )(v, kq, delta, cum, cumt, infc, tailc, keep, segc, segr)


def gate_kernel(
    y_ref, v_ref, z_ref, g_ref, kq_ref, inc_ref, infd_ref, dir_ref, gam_ref,
    out_ref, dy_ref, dz_ref, dinc_ref, small_ref, ybuf, rbuf,
):
    first = pl.program_id(0) == 0
    rows = y_ref.shape[0]
    q = kq_ref[:, STATE:]
    inflow = infd_ref[...]
    square = jnp.zeros((rows, 128), f32)
    cross = jnp.zeros((rows, 128), f32)
    for j in range(DI // 128):
        cols = slice(128 * j, 128 * (j + 1))
        carry = dot3(q, inc_ref[:, cols]) * pair_lanes(inflow, j)
        y = y_ref[:, cols] + carry + dir_ref[0:1, cols] * v_ref[:, cols]
        z = z_ref[:, cols]
        gated = y * (z * sigmoid(z))
        ybuf[:, cols] = y
        rbuf[:, cols] = gated
        square = square + gated * gated
        cross = cross + gated * (g_ref[:, cols] * gam_ref[0:1, cols])
    inv = lax.rsqrt(jnp.sum(square, axis=1, keepdims=True) * (1.0 / DI) + norm_eps)
    slope = inv * inv * inv * (jnp.sum(cross, axis=1, keepdims=True) * (1.0 / DI))
    qt = q.T

    @pl.when(first)
    def _():
        dinc_ref[...] = jnp.zeros_like(dinc_ref)
        small_ref[...] = jnp.zeros_like(small_ref)

    for j in range(DI // 128):
        cols = slice(128 * j, 128 * (j + 1))
        gated = rbuf[:, cols]
        scaled = gated * inv
        gam = gam_ref[0:1, cols]
        out_ref[:, cols] = (scaled * gam).astype(bf16)
        g = g_ref[:, cols]
        dgated = inv * (g * gam) - gated * slope
        z = z_ref[:, cols]
        s = sigmoid(z)
        dy = dgated * (z * s)
        dy_ref[:, cols] = dy
        dz = dgated * ybuf[:, cols] * (s * (1.0 + z * (1.0 - s)))
        dz_ref[:, cols] = dz.astype(bf16)
        small_ref[2:3, cols] = jnp.maximum(
            small_ref[2:3, cols], jnp.max(jnp.abs(dz), axis=0, keepdims=True)
        )
        small_ref[0:1, cols] += jnp.sum(g * scaled, axis=0, keepdims=True)
        small_ref[1:2, cols] += jnp.sum(dy * v_ref[:, cols], axis=0, keepdims=True)
        dinc_ref[:, cols] += dot3(qt, dy * pair_lanes(inflow, j))


def gate(y, v, z, g, kq, inc, infd, dirx, gam):
    length = y.shape[0]
    tile = Q
    big = pl.BlockSpec((tile, DI), lambda i: (i, 0))
    return pl.pallas_call(
        gate_kernel,
        grid=(length // tile,),
        in_specs=[
            big, big, big, big,
            pl.BlockSpec((tile, 2 * STATE), lambda i: (i, 0)),
            pl.BlockSpec((STATE, DI), lambda i: (0, 0)),
            pl.BlockSpec((tile, HEADS), lambda i: (i, 0)),
            pl.BlockSpec((8, DI), lambda i: (0, 0)),
            pl.BlockSpec((8, DI), lambda i: (0, 0)),
        ],
        out_specs=(
            big, big, big,
            pl.BlockSpec((STATE, DI), lambda i: (0, 0)),
            pl.BlockSpec((8, DI), lambda i: (0, 0)),
        ),
        out_shape=(
            jax.ShapeDtypeStruct((length, DI), bf16),
            jax.ShapeDtypeStruct((length, DI), f32),
            jax.ShapeDtypeStruct((length + PAD, DI), bf16),
            jax.ShapeDtypeStruct((STATE, DI), f32),
            jax.ShapeDtypeStruct((8, DI), f32),
        ),
        scratch_shapes=[pltpu.VMEM((tile, DI), f32), pltpu.VMEM((tile, DI), f32)],
        compiler_params=params(),
        cost_estimate=pl.CostEstimate(flops=10**9, bytes_accessed=4 * 10**7, transcendentals=4 * 10**6),
        name="gate",
    )(y, v, z, g, kq, inc, infd, dirx, gam)


def back_kernel(
    final, v_ref, dy_ref, kq_ref, delta_ref, cum_ref, cumt_ref, infc_ref, tailc_ref, tailn_ref,
    keep_ref, inc_ref, dout_ref, dir_ref, segc_ref, segr_ref, dkq_in, dgram_in,
    dv_ref, dkq_ref, dgram, ddelta_ref, dcum_ref, drow_ref, flow_ref,
    gram, gramt, bias, biast, kt, qt, states,
):
    length = v_ref.shape[0]
    count = length // Q
    step = pl.program_id(0)

    @pl.when(step == 0)
    def _():
        for c in range(count):
            rows = slice(c * Q, (c + 1) * Q)
            k, q = kq_ref[rows, :STATE], kq_ref[rows, STATE:]
            b, bt = masks_of(segc_ref, segr_ref, rows)
            bias[rows, :] = b
            biast[rows, :] = bt
            scores = dot3(q, k, NT)
            gram[rows, :] = scores
            gramt[rows, :] = scores.T
            kt[:, rows] = k.T
            qt[:, rows] = q.T
        dgram[...] = dgram_in[...]
        dkq_ref[...] = dkq_in[...]

    low = iota((Q, 128), 1) < HEAD_DIM
    lane = iota((Q, GH), 1)
    line = iota((8, GW), 0)

    states[0] = inc_ref[...].astype(f32)
    for c in range(count):
        rows = slice(c * Q, (c + 1) * Q)
        weighted = v_ref[rows, :] * group_lanes(tailc_ref[0, rows, :])
        states[c + 1] = states[c] * keep_ref[c : c + 1, :] + dot3(kt[:, rows], weighted)

    back = dout_ref[...].astype(f32)
    flows = jnp.zeros((8, GW), f32)
    for c in reversed(range(count)):
        rows = slice(c * Q, (c + 1) * Q)
        flows = jnp.where(line == c, jnp.sum(back * states[c + 1], axis=0, keepdims=True), flows)
        delta, cum = delta_ref[0, rows, :], cum_ref[0, rows, :]
        inflow, tailc, tailn = infc_ref[0, rows, :], tailc_ref[0, rows, :], tailn_ref[0, rows, :]
        k, q = kq_ref[rows, :STATE], kq_ref[rows, STATE:]
        before = states[c]
        after = back
        y_in = dot3(q, before)
        w_in = dot3(k, after)
        g, gt, b, bt = gram[rows, :], gramt[rows, :], bias[rows, :], biast[rows, :]
        dg = dgram[rows, :]
        ddelta = jnp.zeros((Q, GH), f32)
        dcum = jnp.zeros((Q, GH), f32)
        dys, ws = [], []
        for j in range(GW // 128):
            cols = slice(128 * j, 128 * (j + 1))
            dy, v = dy_ref[rows, cols], v_ref[rows, cols]
            spread = pair_lanes(delta, j)
            w = v * spread
            stacked = jnp.concatenate(
                [jnp.where(low, dy, 0.0), jnp.where(low, 0.0, dy)], axis=0
            )
            inner = dot3(stacked, w, NT)
            turned = []
            for i in (0, 1):
                h = 2 * j + i
                col, row = cum[:, h : h + 1], cumt_ref[h : h + 1, rows]
                turned.append(gt * jnp.exp(row - col + bt))
                weighed = inner[Q * i : Q * (i + 1), :] * jnp.exp(col - row + b)
                dg = dg + weighed
                full = weighed * g
                dcum = dcum + jnp.where(lane == h, jnp.sum(full, axis=1, keepdims=True), 0.0)
                drow_ref[h : h + 1, rows] = jnp.sum(full, axis=0, keepdims=True)
            dw_in = w_in[:, cols] * pair_lanes(tailn, j)
            dw = dot3(jnp.concatenate(turned, axis=1), stacked) + dw_in
            dv_ref[rows, cols] = spread * dw + dir_ref[0:1, cols] * dy
            dflow = dy * pair_lanes(inflow, j)
            one = dflow * y_in[:, cols] - w * dw_in
            two = v * dw
            for i in (0, 1):
                h = 2 * j + i
                keep = low if i == 0 else jnp.logical_not(low)
                dcum = dcum + jnp.where(
                    lane == h, jnp.sum(jnp.where(keep, one, 0.0), axis=1, keepdims=True), 0.0
                )
                ddelta = ddelta + jnp.where(
                    lane == h, jnp.sum(jnp.where(keep, two, 0.0), axis=1, keepdims=True), 0.0
                )
            dys.append(dflow)
            ws.append(v * pair_lanes(tailc, j))
        dgram[rows, :] = dg
        ddelta_ref[0, rows, :] = ddelta
        dcum_ref[0, rows, :] = dcum
        flowing = jnp.concatenate(dys, axis=1)
        dkq_ref[rows, STATE:] += dot3(flowing, before, NT)
        dkq_ref[rows, :STATE] += dot3(jnp.concatenate(ws, axis=1), after, NT)
        if c:
            back = back * keep_ref[c : c + 1, :] + dot3(qt[:, rows], flowing)
    flow_ref[...] = flows

    @pl.when(jnp.logical_and(step == pl.num_programs(0) - 1, final))
    def _():
        for c in range(count):
            rows = slice(c * Q, (c + 1) * Q)
            k, q = kq_ref[rows, :STATE], kq_ref[rows, STATE:]
            dg = dgram[rows, :]
            dkq_ref[rows, STATE:] += dot3(dg, k)
            dkq_ref[rows, :STATE] += dot3(dg.T, q)


def back_local(
    first, last, held, v, dy, kq, delta, cum, cumt, infc, tailc, tailn, keep, inc, dout, dirx, segc, segr
):
    length = v.shape[0]
    count = length // Q
    groups = last - first
    if held is None:
        held = (jnp.zeros((length, 2 * STATE), f32), jnp.zeros((length, Q), f32))
    cols = pl.BlockSpec((1, length, GH), lambda g: (g + first, 0, 0))
    wide = pl.BlockSpec((length, GW), lambda g: (0, g + first))
    state = pl.BlockSpec((STATE, GW), lambda g: (0, g + first))
    lines = pl.BlockSpec((8, GW), lambda g: (0, g + first))
    turned = pl.BlockSpec((GH, length), lambda g: (g + first, 0))
    whole = pl.BlockSpec((length, 2 * STATE), lambda g: (0, 0))
    table = pl.BlockSpec((length, Q), lambda g: (0, 0))
    square = pltpu.VMEM((length, Q), f32)
    out_cols = pl.BlockSpec((1, length, GH), lambda g: (g, 0, 0))
    return pl.pallas_call(
        functools.partial(back_kernel, last == NG),
        grid=(groups,),
        in_specs=[
            wide, wide, whole, cols, cols, turned, cols, cols, cols, lines, state, state, lines,
            pl.BlockSpec((length, 8), lambda g: (0, 0)),
            pl.BlockSpec((8, length), lambda g: (0, 0)),
            whole, table,
        ],
        out_specs=(
            pl.BlockSpec((length, GW), lambda g: (0, g)), whole, table, out_cols, out_cols,
            pl.BlockSpec((GH, length), lambda g: (g, 0)),
            pl.BlockSpec((8, GW), lambda g: (0, g)),
        ),
        out_shape=(
            jax.ShapeDtypeStruct((length, groups * GW), f32),
            jax.ShapeDtypeStruct((length, 2 * STATE), f32),
            jax.ShapeDtypeStruct((length, Q), f32),
            jax.ShapeDtypeStruct((groups, length, GH), f32),
            jax.ShapeDtypeStruct((groups, length, GH), f32),
            jax.ShapeDtypeStruct((groups * GH, length), f32),
            jax.ShapeDtypeStruct((8, groups * GW), f32),
        ),
        scratch_shapes=[
            square, square, square, square,
            pltpu.VMEM((STATE, length), f32), pltpu.VMEM((STATE, length), f32),
            pltpu.VMEM((count + 1, STATE, GW), f32),
        ],
        compiler_params=params(),
        cost_estimate=pl.CostEstimate(
            flops=groups * 5 * 10**9, bytes_accessed=groups * 5 * 10**6, transcendentals=groups * 10**6
        ),
        name="back_first" if first == 0 else "back_second",
    )(v, dy, kq, delta, cum, cumt, infc, tailc, tailn, keep, inc, dout, dirx, segc, segr, *held)


def step_kernel(
    step_ref, par_ref, ddelta_a, ddelta_b, dcum_a, dcum_b, drow_a, drow_b, flow_a, flow_b,
    dstep_ref, small_ref,
):
    length = ddelta_a.shape[1]
    half = ddelta_a.shape[0]
    upper = (iota((Q, Q), 0) <= iota((Q, Q), 1)).astype(f32)
    eye = (iota((Q, Q), 0) == iota((Q, Q), 1)).astype(f32)
    last = iota((Q, 1), 0) == Q - 1
    rate = jnp.exp(par_ref[1:2, :])
    spread = head_onehot()
    wide = half * GW
    flows = dotf(flow_a[...], spread[:, :wide], NT) + dotf(flow_b[...], spread[:, wide:], NT)
    top = half * GH
    rise = (iota((HEADS, top), 0) == iota((HEADS, top), 1)).astype(f32)
    fall = (iota((HEADS, HEADS - top), 0) == iota((HEADS, HEADS - top), 1) + top).astype(f32)
    times = jnp.zeros((1, HEADS), f32)
    decays = jnp.zeros((1, HEADS), f32)
    most = jnp.zeros((1, HEADS), f32)
    dstep_ref[...] = jnp.zeros_like(dstep_ref)
    for c in range(length // Q):
        rows = slice(c * Q, (c + 1) * Q)
        ddelta = jnp.zeros((Q, HEADS), f32)
        turned = dotf(rise, drow_a[:, rows]) + dotf(fall, drow_b[:, rows])
        dcum = -dotf(eye, turned, NT)
        for g in range(NG):
            place = (iota((GH, HEADS), 0) + g * GH == iota((GH, HEADS), 1)).astype(f32)
            one, two = (ddelta_a[g, rows, :], dcum_a[g, rows, :]) if g < half else (
                ddelta_b[g - half, rows, :], dcum_b[g - half, rows, :]
            )
            ddelta = ddelta + dotf(one, place)
            dcum = dcum + dotf(two, place)
        dcum = dcum + jnp.where(last, flows[c : c + 1, :], 0.0)
        x = step_ref[pl.ds(HALO + c * Q, Q), :HEADS] + par_ref[0:1, :]
        dlog = dotf(upper, dcum) * rate
        decays = decays - jnp.sum(dlog * softplus(x), axis=0, keepdims=True)
        dstep = (ddelta - dlog) * sigmoid(x)
        times = times + jnp.sum(dstep, axis=0, keepdims=True)
        most = jnp.maximum(most, jnp.max(jnp.abs(dstep), axis=0, keepdims=True))
        dstep_ref[rows, :HEADS] = dstep.astype(bf16)
    dstep_ref[pl.ds(length, PAD), :HEADS] = jnp.broadcast_to(most * 1.01, (PAD, HEADS)).astype(bf16)
    small_ref[...] = jnp.zeros_like(small_ref)
    small_ref[0:1, :] = times
    small_ref[1:2, :] = decays


def step_back(rest, pars, first, second):
    length = first[0].shape[1]
    arrays = [part for both in zip(first, second) for part in both]
    shapes = (
        jax.ShapeDtypeStruct((length + PAD, 128), bf16),
        jax.ShapeDtypeStruct((8, HEADS), f32),
    )
    return pl.pallas_call(
        step_kernel,
        grid=(1,),
        in_specs=[steps_of(rest), whole(pars)] + [whole(array) for array in arrays],
        out_specs=tuple(whole(shape) for shape in shapes),
        out_shape=shapes,
        compiler_params=params(),
        cost_estimate=pl.CostEstimate(flops=10**7, bytes_accessed=10**7, transcendentals=10**5),
        name="step_back",
    )(rest, pars, *arrays)


def unconv_kernel(mixed, x_ref, tap_ref, match_ref, dv_ref, dkq_ref, dx_ref, edge_ref, dtap_ref, *held):
    length = match_ref.shape[1]
    count = length // Q
    wide = pl.program_id(0) < mixed
    for buf in held:
        buf[0:HALO, :] = jnp.zeros((HALO, TILE), f32)
        buf[HALO + length :, :] = jnp.zeros((HALO, TILE), f32)
    for j in range(TILE // 128):
        cols = slice(128 * j, 128 * (j + 1))
        sums = [jnp.zeros((1, 128), f32) for _ in range(KW + 1)]
        for c in range(count):
            rows = slice(c * Q, (c + 1) * Q)
            s = conv_sum(x_ref, tap_ref, match_ref, c * Q, Q, cols)
            sig = sigmoid(s)
            dm = jnp.where(wide, dv_ref[rows, cols], dkq_ref[rows, cols])
            ds = dm * (sig * (1.0 + s * (1.0 - sig)))
            sums[KW] = sums[KW] + jnp.sum(ds, axis=0, keepdims=True)
            for k in range(KW):
                e = ds if k == KW - 1 else ds * match_ref[k, rows, :]
                held[k][HALO + c * Q : HALO + (c + 1) * Q, cols] = e
                taken = x_ref[pl.ds(HALO - (KW - 1) + k + c * Q, Q), cols]
                sums[k] = sums[k] + jnp.sum(e * taken, axis=0, keepdims=True)
        for k in range(KW + 1):
            dtap_ref[k : k + 1, cols] = sums[k]

        def placed(start, rows):
            total = None
            for k in range(KW):
                term = tap_ref[k : k + 1, cols] * held[k][pl.ds(start + KW - 1 - k, rows), cols]
                total = term if total is None else total + term
            return total

        edge_ref[0:HALO, cols] = placed(0, HALO)
        most = jnp.zeros((1, 128), f32)
        for c in range(count):
            dx = placed(HALO + c * Q, Q)
            most = jnp.maximum(most, jnp.max(jnp.abs(dx), axis=0, keepdims=True))
            dx_ref[c * Q : (c + 1) * Q, cols] = dx.astype(bf16)
            if c == count - 1:
                edge_ref[HALO:, cols] = dx[Q - HALO :, :]
        dtap_ref[KW + 1 : KW + 2, cols] = most
    dtap_ref[KW + 2 :, :] = jnp.zeros((8 - KW - 2, TILE), f32)


def unconv(first, rest, taps, match, dv, dkq):
    length = match.shape[1]
    high = length + HALO
    mixed = dv.shape[1] // TILE
    tiles = mixed if dkq is None else mixed + 1
    lone = dv if dkq is None else dkq
    return pl.pallas_call(
        functools.partial(unconv_kernel, mixed),
        grid=(tiles,),
        in_specs=[
            pl.BlockSpec((high, TILE), lambda j: (0, j + first)),
            pl.BlockSpec((8, TILE), lambda j: (0, j + first)),
            pl.BlockSpec((KW - 1, length, 128), lambda j: (0, 0, 0)),
            pl.BlockSpec((length, TILE), lambda j: (0, jnp.minimum(j, mixed - 1))),
            pl.BlockSpec((length, TILE), lambda j: (0, 0)),
        ],
        out_specs=(
            pl.BlockSpec((length, TILE), lambda j: (0, j)),
            pl.BlockSpec((2 * HALO, TILE), lambda j: (0, j)),
            pl.BlockSpec((8, TILE), lambda j: (0, j)),
        ),
        out_shape=(
            jax.ShapeDtypeStruct((length + PAD, tiles * TILE), bf16),
            jax.ShapeDtypeStruct((2 * HALO, tiles * TILE), f32),
            jax.ShapeDtypeStruct((8, tiles * TILE), f32),
        ),
        scratch_shapes=[pltpu.VMEM((length + 2 * HALO, TILE), f32) for _ in range(KW)],
        compiler_params=params(),
        cost_estimate=pl.CostEstimate(flops=10**8, bytes_accessed=10**7, transcendentals=10**6),
    )(rest, taps, match, dv, lone)


def adamw(param, grad, moment, square, rate, shrink):
    moment_new = beta_one * moment + (1.0 - beta_one) * grad
    square_new = beta_two * square + (1.0 - beta_two) * grad * grad
    first_corr = 1.0 - beta_one**ADAM_STEP
    second_corr = 1.0 - beta_two**ADAM_STEP
    update = moment_new / first_corr / (jnp.sqrt(square_new / second_corr) + adam_eps)
    return (param - rate * (update + shrink * param), moment_new, square_new)


def shifted(value, axis, by):
    count = lax.axis_size(axis)
    pairs = [(i, i + by) for i in range(count) if 0 <= i + by < count]
    return lax.ppermute(value, axis, pairs)


TOKENS = (((0,), (0,)), ((), ()))


def gathered(value):
    return lax.all_gather(value, "dp", axis=0, tiled=True)


def shard_gathered(value):
    count, here = lax.axis_size("shard"), lax.axis_index("shard")
    rows, width = value.shape
    held = jnp.zeros((count * rows, width), value.dtype)
    for k in range(count):
        part = exchanged(value, "shard", k) if k else value
        held = lax.dynamic_update_slice(held, part, ((here ^ k) * rows, 0))
    return held


def exchanged(value, axis, by):
    return lax.ppermute(value, axis, [(i, i ^ by) for i in range(lax.axis_size(axis))])


def relative(value, block, core):
    base = lax.axis_index("dp") // 2
    length = value.shape[0]
    return [
        lax.dynamic_slice(value, (0, (((j ^ base) * 2) + core) * block), (length, block))
        for j in range(lax.axis_size("dp") // 2)
    ]


def both_cores(value):
    return jnp.concatenate([value, exchanged(value, "dp", 1)], axis=0)


def own_and_partner(value, block):
    core = lax.axis_index("dp") % 2
    return relative(value, block, core), relative(value, block, 1 - core)


def exponent(bound):
    return jnp.ceil(jnp.log2(jnp.maximum(bound, 1e-30)))


def coded(total, power, rows):
    own = iota(total.shape, 0) < rows
    return jnp.where(own, total * jnp.exp2(15.0 - power), power).astype(jnp.float16)


def decoded(payload, rows):
    power = payload[rows : rows + 1].astype(f32)
    return payload.astype(f32) * jnp.exp2(power - 15.0), power


def after(value, *earlier):
    return lax.optimization_barrier((value, earlier))[0]


def split_plan(order):
    kept, sends = [0], []
    for bit in reversed(order):
        send = [j ^ (1 << bit) for j in kept]
        sends.insert(0, send)
        kept = kept + send
    return kept, sends


def columns_of(blocks, order):
    kept, sends = split_plan(order)
    zeros = jnp.zeros((blocks[0].shape[0], PAD), bf16)
    return (
        jnp.concatenate([blocks[j] for j in sends[0]] + [zeros], axis=1),
        jnp.concatenate([blocks[j] for j in kept[: len(sends[0])]] + [zeros], axis=1),
    )


class Sum:
    def __init__(self, sent, held, rhs, bound, order):
        self.sent, self.held, self.rhs = sent, held, rhs
        self.power = exponent(bound)
        self.order = order
        self.rows = 2 * (sent.shape[1] - PAD)
        self.total = None
        self.at = 0

    def prepare(self):
        self.rows //= 2
        if self.total is None:
            part = lax.dot_general(self.sent, self.rhs, TOKENS, preferred_element_type=f32)
        else:
            part = self.total[self.rows : 2 * self.rows + PAD]
        self.payload = coded(part, self.power, self.rows)

    def send(self):
        self.got = exchanged(self.payload, "dp", 2 << self.order[self.at])
        self.at += 1
        if self.total is None:
            self.total = lax.dot_general(self.held, self.rhs, TOKENS, preferred_element_type=f32)

    def take(self, *earlier):
        got, other = decoded(after(self.got, earlier), self.rows)
        self.total = self.total[: self.rows + PAD] + got
        self.power = jnp.maximum(self.power, other) + 1.0

    def more(self):
        return self.at < len(self.order)

    def finish(self):
        while self.more():
            self.prepare()
            self.send()
            self.take()


class ShardSum:
    def __init__(self, sums):
        count, here = lax.axis_size("shard"), lax.axis_index("shard")
        self.rows = sums[0].rows // count
        self.total = jnp.concatenate([one.total for one in sums], axis=1) if len(sums) > 1 else sums[0].total
        power = jnp.concatenate([one.power for one in sums], axis=1) if len(sums) > 1 else sums[0].power
        width = self.total.shape[1]
        self.payloads = [
            coded(
                lax.dynamic_slice(self.total, ((here ^ k) * self.rows, 0), (self.rows + PAD, width)),
                power, self.rows,
            )
            for k in range(1, count)
        ]
        self.parts = [exchanged(part, "shard", k + 1) for k, part in enumerate(self.payloads)]

    def take(self, *earlier):
        here = lax.axis_index("shard")
        result = lax.dynamic_slice(self.total, (here * self.rows, 0), (self.rows, self.total.shape[1]))
        for part in self.parts:
            result = result + decoded(after(part, earlier), self.rows)[0][: self.rows]
        return result


def summed(value):
    for axis in ("dp", "shard"):
        count = lax.axis_size(axis)
        if count & (count - 1):
            value = lax.psum(value, axis)
            continue
        by = 1
        while by < count:
            value = value + lax.ppermute(value, axis, [(i, i ^ by) for i in range(count)])
            by *= 2
    return value


def carried(state, factor, by):
    incoming = shifted(state.astype(bf16), "shard", by)
    for _ in range(1, lax.axis_size("shard") - 1):
        passed = (state + factor * incoming.astype(f32)).astype(bf16)
        incoming = shifted(passed, "shard", by)
    return incoming


def both_with_most(rows):
    length = rows.shape[0] - PAD
    arrived = exchanged(rows, "dp", 1)
    most = jnp.maximum(rows[length : length + 1], arrived[length : length + 1]).astype(f32)
    return jnp.concatenate([rows[:length], arrived[:length]], axis=0), most


def mended(dx, edge, dtap, length):
    last = edge[HALO:] + shifted(edge[:HALO], "shard", -1)
    most = jnp.maximum(dtap[KW + 1 : KW + 2], jnp.max(jnp.abs(last), axis=0, keepdims=True)) * 1.01
    tail = jnp.concatenate([last, jnp.broadcast_to(most, (PAD, most.shape[1]))], axis=0).astype(bf16)
    return lax.dynamic_update_slice(dx, tail, (length - HALO, 0)), dtap


def rest_sums(both, bound, in_columns, orders):
    middle = both.shape[1] // 256 * 128
    return [
        Sum(*in_columns[0], both[:, :middle], bound[:, :middle], orders[0]),
        Sum(*in_columns[1], both[:, middle:], bound[:, middle:], orders[1]),
    ]


def shards(
    hidden_in, cotangent, segment_ids,
    param_prenorm, param_inputs, param_kernel, param_offsets, param_timestep, param_decays,
    param_direct, param_gating, param_outputs,
    moment_prenorm, moment_inputs, moment_kernel, moment_offsets, moment_timestep, moment_decays,
    moment_direct, moment_gating, moment_outputs,
    square_prenorm, square_inputs, square_kernel, square_offsets, square_timestep, square_decays,
    square_direct, square_gating, square_outputs,
):
    length, width = hidden_in.shape
    own_inputs = param_inputs.astype(bf16)
    spare = -(param_inputs.shape[1] - DI) % 128
    rest_rows = shard_gathered(jnp.pad(own_inputs[:, DI:], ((0, 0), (0, spare))))
    rest_w = gathered(rest_rows)

    seg = segment_ids.astype(f32)
    ends = jnp.pad(seg[length - HALO :], (0, width - HALO))[None, :]
    halo = shifted(
        jnp.concatenate([hidden_in[length - HALO :], jnp.broadcast_to(ends, (HALO, width))], axis=0),
        "shard", 1,
    )
    rim_seg = jnp.where(lax.axis_index("shard") == 0, -1.0, halo[HALO, :HALO])
    rim = rim_seg[HALO - 1]
    all_segs = jnp.concatenate([rim_seg, seg])
    match = jnp.stack(
        [
            (all_segs[HALO - (KW - 1) + k : HALO - (KW - 1) + k + length] == seg).astype(f32)
            for k in range(KW - 1)
        ]
    )
    match = jnp.broadcast_to(match[:, :, None], (KW - 1, length, 128))
    chunks = seg.reshape(-1, Q)
    before = jnp.concatenate([rim[None], chunks[:-1, Q - 1]])
    mask = jnp.stack(
        [
            (chunks == before[:, None]).reshape(-1),
            (chunks == chunks[:, Q - 1 :]).reshape(-1),
            seg == rim,
            seg == seg[length - 1],
        ]
        + [seg < -1.0] * 4,
        axis=1,
    ).astype(f32)
    segc = jnp.broadcast_to(seg[:, None], (length, 8))
    segr = jnp.broadcast_to(seg[None, :], (8, length))

    taps = jnp.concatenate([param_kernel, param_offsets[None, :], jnp.zeros((8 - KW - 1, CH), f32)], axis=0)
    pars = jnp.concatenate([param_timestep[None, :], param_decays[None, :], jnp.zeros((6, HEADS), f32)], axis=0)
    dirx = jnp.broadcast_to(jnp.repeat(param_direct, HEAD_DIM)[None, :], (8, DI))
    gam = jnp.broadcast_to(param_gating[None, :], (8, DI))

    hidden = jnp.concatenate([halo[:HALO], hidden_in], axis=0)
    inv = lax.rsqrt(jnp.mean(hidden * hidden, axis=1, keepdims=True) + norm_eps)
    normed = (hidden * inv * param_prenorm).astype(bf16)
    own_normed = normed[HALO:]
    upstream = cotangent.astype(bf16)

    groups = lax.axis_size("shard")
    spots = [bit for bit in range(20) if (2 << bit) < lax.axis_size("dp")]
    orders = (spots, spots[::-1])
    in_block, out_block = groups * param_inputs.shape[0], groups * param_outputs.shape[0]
    up_both = both_cores(upstream)
    own_blocks, partner_blocks = own_and_partner(own_normed, in_block)
    arrived = exchanged(jnp.concatenate(partner_blocks, axis=1), "dp", 1)
    both_blocks = [
        jnp.concatenate([one, arrived[:, j * in_block : (j + 1) * in_block]], axis=0)
        for j, one in enumerate(own_blocks)
    ]
    in_columns = [columns_of(both_blocks, order) for order in orders]
    norm_bound = 2.02 * length * width**0.5 * jnp.max(jnp.abs(param_prenorm))
    out_bound = 2.02 * length * DI**0.5 * jnp.max(jnp.abs(param_gating))
    out_bound = out_bound * jnp.max(jnp.abs(up_both), axis=0, keepdims=True).astype(f32)
    early = (match, mask, segc, segr, taps, pars, dirx, gam, up_both, out_bound, norm_bound, in_columns, normed)
    gate_rows = shard_gathered(after(own_inputs[:, :DI], rest_rows, early))
    gate_w = gathered(gate_rows)
    out_w = gathered(shard_gathered(after(param_outputs.astype(bf16), gate_rows)))
    rest_w = after(rest_w, early)

    rest = jnp.dot(normed, rest_w, preferred_element_type=f32)
    delta, cum, cumt, infc, tailc, tailn, taild, infd, keep, factor = prep(rest, pars, mask)
    v, kq, state = conv_state(rest, taps, match, taild)
    incoming = carried(state, factor[0:1], 1)
    y = local_out(v, kq, delta, cum, cumt, infc, tailc, keep, segc, segr)
    gate_w = after(gate_w, y)
    z = jnp.dot(own_normed, gate_w, preferred_element_type=f32)
    out_w = after(out_w, z)
    back_gated = lax.dot_general(upstream, out_w, NT, preferred_element_type=f32)
    gated, dy, dz, dinc, small = gate(y, v, z, back_gated, kq, incoming, infd, dirx, gam)

    outgoing = carried(dinc, factor[0:1], -1)
    own_blocks, partner_blocks = own_and_partner(gated, out_block)
    out_columns = [
        jnp.concatenate([mine, exchanged(theirs, "dp", 1)], axis=0)
        for mine, theirs in zip(columns_of(own_blocks, spots), columns_of(partner_blocks, spots))
    ]
    dz_most = jnp.broadcast_to(small[2:3] * 1.01, (PAD, DI)).astype(bf16)
    dz = lax.dynamic_update_slice(dz, dz_most, (length, 0))
    dz_both, dz_bound = both_with_most(dz)
    dz = dz[:length]
    block_out = hidden_in + jnp.dot(gated, out_w, preferred_element_type=f32)
    out_sum = Sum(*out_columns, up_both, out_bound, spots)
    gate_sum = Sum(*in_columns[1], dz_both, norm_bound * dz_bound, spots[::-1])
    first_sums = [out_sum, gate_sum]
    for one in first_sums:
        one.prepare()
        one.send()
    back_normed = lax.dot_general(dz, gate_w, NT, preferred_element_type=f32)
    outgoing = after(
        outgoing, out_sum.payload, gate_sum.payload, out_sum.total, gate_sum.total, back_normed, block_out
    )

    ssm = (kq, delta, cum, cumt, infc, tailc, tailn, keep, incoming)
    half = NG // 2
    dv1, *held1 = back_local(0, half, None, v, dy, *ssm, outgoing, dirx, segc, segr)
    for one in first_sums:
        one.take(dv1)
        if one.more():
            one.prepare()
            one.send()
    dv1 = after(dv1, *[one.payload for one in first_sums])
    drest1, dtap1 = mended(*unconv(0, rest, taps, match, dv1, None), length)
    both1, bound1 = both_with_most(drest1)
    sums1 = rest_sums(both1, norm_bound * bound1, in_columns, orders)
    for one in first_sums:
        one.take(dv1, both1)
        one.finish()
    shard_out, shard_gate = ShardSum([out_sum]), ShardSum([gate_sum])
    for one in sums1:
        one.prepare()
        one.send()
    dy = after(
        dy, [one.payload for one in sums1], [one.total for one in sums1], shard_out.payloads, shard_gate.payloads
    )
    dv2, *held2 = back_local(half, NG, held1[:2], v, dy, *ssm, outgoing, dirx, segc, segr)
    for one in sums1:
        one.take(dv2)
        if one.more():
            one.prepare()
            one.send()
    dv2 = after(dv2, *[one.payload for one in sums1])
    dstep, small_step = step_back(rest, pars, held1[2:], held2[2:])
    drest2, dtap2 = mended(*unconv(dv1.shape[1] // TILE, rest, taps, match, dv2, held2[0]), length)
    drest2 = jnp.concatenate([drest2, dstep], axis=1)
    both2, bound2 = both_with_most(drest2)
    sums2 = rest_sums(both2, norm_bound * bound2, in_columns, orders)
    for one in sums2:
        one.prepare()
        one.send()
    for one in sums1:
        one.take(dv2, dstep)
        one.finish()
    shard1 = ShardSum(sums1)
    drest1, drest2 = after((drest1, drest2), shard1.payloads, [two.payload for two in sums2])
    wide1 = drest1.shape[1]
    back_normed = back_normed + lax.dot_general(drest1[:length], rest_w[:, :wide1], NT, preferred_element_type=f32)
    back_normed = back_normed + lax.dot_general(drest2[:length], rest_w[:, wide1:], NT, preferred_element_type=f32)
    grad_outputs = shard_out.take(drest2)
    grad_gate = shard_gate.take(drest2)
    for one in sums2:
        one.take(back_normed)
        if one.more():
            one.prepare()
            one.send()
    sent = [one.payload for one in sums2]
    for one in sums2:
        one.take()
        one.finish()
    shard2 = ShardSum(sums2)
    grad_rest = jnp.concatenate([shard1.take(sent), shard2.take()], axis=1)
    grad_inputs = jnp.concatenate([grad_gate, grad_rest[:, : param_inputs.shape[1] - DI]], axis=1)
    dtap = jnp.concatenate([dtap1, dtap2], axis=1)

    own_inv = inv[HALO:]
    scaled = hidden_in * own_inv
    gained = back_normed * param_prenorm
    hidden_grad = cotangent + own_inv * (
        gained - scaled * jnp.mean(gained * scaled, axis=1, keepdims=True)
    )
    grad_prenorm = jnp.sum(back_normed * scaled, axis=0)

    pieces = [
        grad_prenorm,
        dtap[:KW].reshape(-1),
        dtap[KW],
        small_step[0],
        small_step[1],
        jnp.sum(small[1].reshape(HEADS, HEAD_DIM), axis=1),
        small[0],
    ]
    flat = after(jnp.concatenate(pieces), sent)
    count = flat.shape[0]
    lines = -(-count // 1024) * 8
    total = summed(jnp.pad(flat, (0, lines * 128 - count)).reshape(lines, 128)).reshape(-1)
    found, at = [], 0
    for piece in pieces:
        found.append(total[at : at + piece.shape[0]])
        at += piece.shape[0]
    grad_prenorm, grad_kernel, grad_offsets, grad_timestep, grad_decays, grad_direct, grad_gating = found
    grad_kernel = grad_kernel.reshape(KW, CH)

    params = (
        param_prenorm, param_inputs, param_kernel, param_offsets, param_timestep, param_decays,
        param_direct, param_gating, param_outputs,
    )
    moments = (
        moment_prenorm, moment_inputs, moment_kernel, moment_offsets, moment_timestep, moment_decays,
        moment_direct, moment_gating, moment_outputs,
    )
    squares = (
        square_prenorm, square_inputs, square_kernel, square_offsets, square_timestep, square_decays,
        square_direct, square_gating, square_outputs,
    )
    grads = (
        grad_prenorm, grad_inputs, grad_kernel, grad_offsets, grad_timestep, grad_decays,
        grad_direct, grad_gating, grad_outputs,
    )
    updated = [
        adamw(params[i], grads[i], moments[i], squares[i], rate_table[i], shrink_table[i])
        for i in range(9)
    ]
    return (
        (block_out, hidden_grad)
        + grads
        + tuple(u[0] for u in updated)
        + tuple(u[1] for u in updated)
        + tuple(u[2] for u in updated)
    )


def solution(mesh):
    rows = P(("dp", "shard"), None)
    member = (P(), rows, P(), P(), P(), P(), P(), P(), rows)

    return jax.shard_map(
        shards,
        mesh=mesh,
        in_specs=(rows, rows, P(("dp", "shard"))) + member * 3,
        out_specs=(rows, rows) + member * 4,
        check_vma=False,
    )
```

```python
import functools

import jax
import jax.numpy as jnp
from jax import lax
from jax.experimental import pallas as pl
from jax.experimental.pallas import tpu as pltpu
from jax.sharding import PartitionSpec as P


HEADS = 48
HEAD_DIM = 64
STATE = 128
KW = 4
ADAM_STEP = 10
DI = 3072
CH = 3328

Q = 128
GH = 8
GW = GH * HEAD_DIM
NG = HEADS // GH
HALO = 8
PAD = 16
TILE = 256

bf16 = jnp.bfloat16
f32 = jnp.float32
highest = lax.Precision.HIGHEST

norm_eps = 1e-05
beta_one = 0.9
beta_two = 0.95
adam_eps = 1e-08
rate_table = (0.2, 0.01, 0.2, 0.2, 0.2, 0.2, 0.2, 0.2, 0.01)
shrink_table = (0.0, 0.1, 0.1, 0.0, 0.0, 0.0, 0.0, 0.0, 0.1)

NN = (((1,), (0,)), ((), ()))
NT = (((1,), (1,)), ((), ()))


def halves(x):
    hi = x.astype(bf16)
    return hi, (x - hi.astype(f32)).astype(bf16)


def dot1(a, b, dims=NN):
    return lax.dot_general(a.astype(bf16), b.astype(bf16), dims, preferred_element_type=f32)


def dot3(a, b, dims=NN):
    ah, al = halves(a)
    bh, bl = halves(b)
    return dot1(ah, bh, dims) + (dot1(ah, bl, dims) + dot1(al, bh, dims))


def dotf(a, b, dims=NN):
    return lax.dot_general(a, b, dims, precision=highest, preferred_element_type=f32)


def iota(shape, dim):
    return lax.broadcasted_iota(jnp.int32, shape, dim)


def sigmoid(x):
    return 1.0 / (1.0 + jnp.exp(-x))


def softplus(x):
    u = jnp.exp(-jnp.abs(x))
    series = u * (1.0 - u * (0.5 - u * (1.0 / 3.0 - u * (0.25 - u * 0.2))))
    return jnp.maximum(x, 0.0) + jnp.where(u < 0.03, series, jnp.log(1.0 + u))


def pair_lanes(cols, j):
    rows = cols.shape[0]
    low = iota((rows, 128), 1) < HEAD_DIM
    return jnp.where(low, cols[:, 2 * j : 2 * j + 1], cols[:, 2 * j + 1 : 2 * j + 2])


def group_lanes(cols):
    return jnp.concatenate([pair_lanes(cols, j) for j in range(cols.shape[1] // 2)], axis=1)


def head_onehot():
    return (iota((HEADS, DI), 1) // HEAD_DIM == iota((HEADS, DI), 0)).astype(f32)


def params(limit=60000, **kw):
    return pltpu.CompilerParams(vmem_limit_bytes=limit * 1024, **kw)


def prep_kernel(
    step_ref, par_ref, mask_ref, delta_ref, cum_ref, cumt_ref, infc_ref, tailc_ref, tailn_ref,
    taild_ref, infd_ref, keep_ref, factor_ref,
):
    length = mask_ref.shape[0]
    count = length // Q
    tri = (iota((Q, Q), 0) >= iota((Q, Q), 1)).astype(f32)
    eye = (iota((HEADS, HEADS), 0) == iota((HEADS, HEADS), 1)).astype(f32)
    rate = jnp.exp(par_ref[1:2, :])
    base = jnp.zeros((1, HEADS), f32)
    held = []
    keeps = []
    for c in range(count):
        rows = slice(c * Q, (c + 1) * Q)
        delta = softplus(step_ref[pl.ds(HALO + c * Q, Q), :HEADS] + par_ref[0:1, :])
        cum = dotf(tri, -delta * rate)
        cumt_ref[:, rows] = dotf(eye, cum, NT)
        last = cum[Q - 1 : Q, :]
        alive, ending = mask_ref[rows, 0:1], mask_ref[rows, 1:2]
        infc = jnp.exp(cum) * alive
        tailn = jnp.exp(last - cum) * ending
        tailc = tailn * delta
        for g in range(NG):
            part = slice(g * GH, (g + 1) * GH)
            delta_ref[g, rows, :] = delta[:, part]
            cum_ref[g, rows, :] = cum[:, part]
            infc_ref[g, rows, :] = infc[:, part]
            tailn_ref[g, rows, :] = tailn[:, part]
            tailc_ref[g, rows, :] = tailc[:, part]
        keeps.append(infc[Q - 1 : Q, :])
        whole = cum + base
        infd_ref[rows, :] = jnp.exp(whole) * mask_ref[rows, 2:3]
        held.append((whole, delta))
        base = base + last
    for c in range(count):
        rows = slice(c * Q, (c + 1) * Q)
        whole, delta = held[c]
        taild = jnp.exp(base - whole) * mask_ref[rows, 3:4] * delta
        for g in range(NG):
            taild_ref[g, rows, :] = taild[:, g * GH : (g + 1) * GH]
    factor = jnp.exp(base) * mask_ref[length - 1 : length, 2:3]
    spread = head_onehot()
    line = iota((8, HEADS), 0)
    table = jnp.zeros((8, HEADS), f32)
    for c in range(count):
        table = jnp.where(line == c, keeps[c], table)
    keep_ref[...] = dotf(table, spread)
    factor_ref[...] = dotf(jnp.where(line == 0, factor, 0.0), spread)


def whole(array):
    return pl.BlockSpec(array.shape, lambda i: (0,) * array.ndim)


def steps_of(rest):
    return pl.BlockSpec((rest.shape[0], 128), lambda i: (0, CH // 128))


def prep(rest, pars, mask):
    length = mask.shape[0]
    cols = jax.ShapeDtypeStruct((NG, length, GH), f32)
    wide = jax.ShapeDtypeStruct((8, DI), f32)
    shapes = (
        cols, cols, jax.ShapeDtypeStruct((HEADS, length), f32), cols, cols, cols, cols,
        jax.ShapeDtypeStruct((length, HEADS), f32), wide, wide,
    )
    return pl.pallas_call(
        prep_kernel,
        grid=(1,),
        in_specs=[steps_of(rest), whole(pars), whole(mask)],
        out_specs=tuple(whole(shape) for shape in shapes),
        out_shape=shapes,
        compiler_params=params(),
        cost_estimate=pl.CostEstimate(flops=10**7, bytes_accessed=10**7, transcendentals=10**5),
        name="prep",
    )(rest, pars, mask)


def conv_sum(x_ref, tap_ref, match_ref, start, rows, cols):
    total = tap_ref[KW : KW + 1, cols] + tap_ref[KW - 1 : KW, cols] * x_ref[
        pl.ds(HALO + start, rows), cols
    ]
    for k in range(KW - 1):
        taken = x_ref[pl.ds(HALO - (KW - 1) + k + start, rows), cols]
        total = total + tap_ref[k : k + 1, cols] * (taken * match_ref[k, pl.ds(start, rows), :])
    return total


def conv_kernel(
    xv_ref, xk_ref, tv_ref, tk_ref, match_ref, taild_ref, v_ref, kq_ref, state_ref, state_half_ref, kt_hi, kt_lo
):
    length = v_ref.shape[0]
    count = length // Q

    @pl.when(pl.program_id(0) == 0)
    def _():
        for c in range(count):
            for j in range(2):
                cols = slice(128 * j, 128 * (j + 1))
                s = conv_sum(xk_ref, tk_ref, match_ref, c * Q, Q, cols)
                m = s * sigmoid(s)
                kq_ref[c * Q : (c + 1) * Q, cols] = m
                if j == 0:
                    hi, lo = halves(m.T)
                    kt_hi[:, c * Q : (c + 1) * Q] = hi
                    kt_lo[:, c * Q : (c + 1) * Q] = lo

    total = jnp.zeros((STATE, GW), f32)
    for c in range(count):
        rows = slice(c * Q, (c + 1) * Q)
        tail = taild_ref[0, rows, :]
        parts = []
        for j in range(GW // 128):
            cols = slice(128 * j, 128 * (j + 1))
            s = conv_sum(xv_ref, tv_ref, match_ref, c * Q, Q, cols)
            m = s * sigmoid(s)
            v_ref[rows, cols] = m
            parts.append(m * pair_lanes(tail, j))
        hi, lo = halves(jnp.concatenate(parts, axis=1))
        kh, kl = kt_hi[:, rows], kt_lo[:, rows]
        total = total + (dot1(kh, hi) + (dot1(kh, lo) + dot1(kl, hi)))
    state_ref[...] = total
    state_half_ref[...] = total.astype(bf16)


def conv_state(rest, taps, match, taild):
    length = match.shape[1]
    high = length + HALO
    kq_at = DI // (2 * STATE)
    return pl.pallas_call(
        conv_kernel,
        grid=(NG,),
        in_specs=[
            pl.BlockSpec((high, GW), lambda g: (0, g)),
            pl.BlockSpec((high, 2 * STATE), lambda g: (0, kq_at)),
            pl.BlockSpec((8, GW), lambda g: (0, g)),
            pl.BlockSpec((8, 2 * STATE), lambda g: (0, kq_at)),
            pl.BlockSpec((KW - 1, length, 128), lambda g: (0, 0, 0)),
            pl.BlockSpec((1, length, GH), lambda g: (g, 0, 0)),
        ],
        out_specs=(
            pl.BlockSpec((length, GW), lambda g: (0, g)),
            pl.BlockSpec((length, 2 * STATE), lambda g: (0, 0)),
            pl.BlockSpec((STATE, GW), lambda g: (0, g)),
            pl.BlockSpec((STATE, GW), lambda g: (0, g)),
        ),
        out_shape=(
            jax.ShapeDtypeStruct((length, DI), f32),
            jax.ShapeDtypeStruct((length, 2 * STATE), f32),
            jax.ShapeDtypeStruct((STATE, DI), f32),
            jax.ShapeDtypeStruct((STATE, DI), bf16),
        ),
        scratch_shapes=[pltpu.VMEM((STATE, length), bf16), pltpu.VMEM((STATE, length), bf16)],
        compiler_params=params(),
        cost_estimate=pl.CostEstimate(flops=2 * 10**9, bytes_accessed=2 * 10**7, transcendentals=2 * 10**6),
        name="conv_state",
    )(rest, rest, taps, taps, match, taild)


def masks_of(segc_ref, segr_ref, rows):
    same = segc_ref[rows, 0:1] == segr_ref[0:1, rows]
    later = iota((Q, Q), 0) >= iota((Q, Q), 1)
    earlier = iota((Q, Q), 0) <= iota((Q, Q), 1)
    return jnp.where(same & later, 0.0, -1e30), jnp.where(same & earlier, 0.0, -1e30)


def local_kernel(
    v_ref, kq_ref, delta_ref, cum_ref, cumt_ref, infc_ref, tailc_ref, keep_ref, segc_ref, segr_ref,
    y_ref, gram, bias, kt,
):
    length = v_ref.shape[0]
    count = length // Q

    @pl.when(pl.program_id(0) == 0)
    def _():
        for c in range(count):
            rows = slice(c * Q, (c + 1) * Q)
            k, q = kq_ref[rows, :STATE], kq_ref[rows, STATE:]
            bias[rows, :] = masks_of(segc_ref, segr_ref, rows)[0]
            gram[rows, :] = dot3(q, k, NT)
            kt[:, rows] = k.T

    low = iota((Q, 128), 1) < HEAD_DIM
    state = None
    for c in range(count):
        rows = slice(c * Q, (c + 1) * Q)
        delta, cum, tail, inflow = (r[0, rows, :] for r in (delta_ref, cum_ref, tailc_ref, infc_ref))
        g, b = gram[rows, :], bias[rows, :]
        if c:
            carried = dot3(kq_ref[rows, STATE:], state)
        tails = []
        for j in range(GW // 128):
            cols = slice(128 * j, 128 * (j + 1))
            v = v_ref[rows, cols]
            w = v * pair_lanes(delta, j)
            both = []
            for i in (2 * j, 2 * j + 1):
                both.append((g * jnp.exp(cum[:, i : i + 1] - cumt_ref[i : i + 1, rows] + b)))
            stacked = jnp.concatenate([jnp.where(low, w, 0.0), jnp.where(low, 0.0, w)], axis=0)
            y = dot3(jnp.concatenate(both, axis=1), stacked)
            if c:
                y = y + carried[:, cols] * pair_lanes(inflow, j)
            y_ref[rows, cols] = y
            if c < count - 1:
                tails.append(v * pair_lanes(tail, j))
        if c < count - 1:
            fresh = dot3(kt[:, rows], jnp.concatenate(tails, axis=1))
            state = fresh if state is None else state * keep_ref[c : c + 1, :] + fresh


def local_out(v, kq, delta, cum, cumt, infc, tailc, keep, segc, segr):
    length = v.shape[0]
    cols = pl.BlockSpec((1, length, GH), lambda g: (g, 0, 0))
    return pl.pallas_call(
        local_kernel,
        grid=(NG,),
        in_specs=[
            pl.BlockSpec((length, GW), lambda g: (0, g)),
            pl.BlockSpec((length, 2 * STATE), lambda g: (0, 0)),
            cols, cols,
            pl.BlockSpec((GH, length), lambda g: (g, 0)),
            cols, cols,
            pl.BlockSpec((8, GW), lambda g: (0, g)),
            pl.BlockSpec((length, 8), lambda g: (0, 0)),
            pl.BlockSpec((8, length), lambda g: (0, 0)),
        ],
        out_specs=pl.BlockSpec((length, GW), lambda g: (0, g)),
        out_shape=jax.ShapeDtypeStruct((length, DI), f32),
        scratch_shapes=[
            pltpu.VMEM((length, Q), f32), pltpu.VMEM((length, Q), f32),
            pltpu.VMEM((STATE, length), f32),
        ],
        compiler_params=params(),
        cost_estimate=pl.CostEstimate(flops=2 * 10**9, bytes_accessed=2 * 10**7, transcendentals=4 * 10**6),
        name="local_out",
    )(v, kq, delta, cum, cumt, infc, tailc, keep, segc, segr)


def gate_kernel(
    block, at_ref, y_ref, v_ref, z_ref, g_ref, kq_ref, inc_ref, infd_ref, dir_ref, gam_ref,
    out_ref, blocks_ref, dy_ref, dz_ref, dinc_ref, dinc_half_ref, small_ref, ybuf, rbuf,
):
    first = pl.program_id(0) == 0
    rows = y_ref.shape[0]
    q = kq_ref[:, STATE:]
    inflow = infd_ref[...]
    square = jnp.zeros((rows, 128), f32)
    cross = jnp.zeros((rows, 128), f32)
    for j in range(DI // 128):
        cols = slice(128 * j, 128 * (j + 1))
        carry = dot3(q, inc_ref[:, cols]) * pair_lanes(inflow, j)
        y = y_ref[:, cols] + carry + dir_ref[0:1, cols] * v_ref[:, cols]
        z = z_ref[:, cols]
        gated = y * (z * sigmoid(z))
        ybuf[:, cols] = y
        rbuf[:, cols] = gated
        square = square + gated * gated
        cross = cross + gated * (g_ref[:, cols] * gam_ref[0:1, cols])
    inv = lax.rsqrt(jnp.sum(square, axis=1, keepdims=True) * (1.0 / DI) + norm_eps)
    slope = inv * inv * inv * (jnp.sum(cross, axis=1, keepdims=True) * (1.0 / DI))
    qt = q.T

    @pl.when(first)
    def _():
        dinc_ref[...] = jnp.zeros_like(dinc_ref)
        small_ref[...] = jnp.zeros_like(small_ref)

    for j in range(DI // 128):
        cols = slice(128 * j, 128 * (j + 1))
        gated = rbuf[:, cols]
        scaled = gated * inv
        gam = gam_ref[0:1, cols]
        half = (scaled * gam).astype(bf16)
        out_ref[:, cols] = half
        if block:
            per = block // 128
            far = ((j // per) >> 1) ^ at_ref[0]
            which = 2 * (((j // per) & 1) ^ at_ref[1]) + (far & 1)
            place = pl.multiple_of((far >> 1) * block + (j % per) * 128, 128)
            blocks_ref[which, :, pl.ds(place, 128)] = half
        g = g_ref[:, cols]
        dgated = inv * (g * gam) - gated * slope
        z = z_ref[:, cols]
        s = sigmoid(z)
        dy = dgated * (z * s)
        dy_ref[:, cols] = dy
        dz = dgated * ybuf[:, cols] * (s * (1.0 + z * (1.0 - s)))
        dz_ref[:, cols] = dz.astype(bf16)
        small_ref[2:3, cols] = jnp.maximum(
            small_ref[2:3, cols], jnp.max(jnp.abs(dz), axis=0, keepdims=True)
        )
        small_ref[0:1, cols] += jnp.sum(g * scaled, axis=0, keepdims=True)
        small_ref[1:2, cols] += jnp.sum(dy * v_ref[:, cols], axis=0, keepdims=True)
        dinc_ref[:, cols] += dot3(qt, dy * pair_lanes(inflow, j))

    @pl.when(pl.program_id(0) == pl.num_programs(0) - 1)
    def _():
        dinc_half_ref[...] = dinc_ref[...].astype(bf16)


def gate(block, at, y, v, z, g, kq, inc, infd, dirx, gam):
    length = y.shape[0]
    tile = Q
    big = pl.BlockSpec((tile, DI), lambda i, at: (i, 0))
    fixed = lambda rows: pl.BlockSpec((rows, DI), lambda i, at: (0, 0))
    spare = 2 * block if block else 128
    return pl.pallas_call(
        functools.partial(gate_kernel, block),
        grid_spec=pltpu.PrefetchScalarGridSpec(
            num_scalar_prefetch=1,
            grid=(length // tile,),
            in_specs=[
                big, big, big, big,
                pl.BlockSpec((tile, 2 * STATE), lambda i, at: (i, 0)),
                fixed(STATE),
                pl.BlockSpec((tile, HEADS), lambda i, at: (i, 0)),
                fixed(8), fixed(8),
            ],
            out_specs=(
                big, pl.BlockSpec((4, tile, spare), lambda i, at: (0, i, 0)), big, big,
                fixed(STATE), fixed(STATE), fixed(8),
            ),
            scratch_shapes=[pltpu.VMEM((tile, DI), f32), pltpu.VMEM((tile, DI), f32)],
        ),
        out_shape=(
            jax.ShapeDtypeStruct((length, DI), bf16),
            jax.ShapeDtypeStruct((4, length, spare), bf16),
            jax.ShapeDtypeStruct((length, DI), f32),
            jax.ShapeDtypeStruct((length + PAD, DI), bf16),
            jax.ShapeDtypeStruct((STATE, DI), f32),
            jax.ShapeDtypeStruct((STATE, DI), bf16),
            jax.ShapeDtypeStruct((8, DI), f32),
        ),
        compiler_params=params(),
        cost_estimate=pl.CostEstimate(flops=10**9, bytes_accessed=4 * 10**7, transcendentals=4 * 10**6),
        name="gate",
    )(at, y, v, z, g, kq, inc, infd, dirx, gam)


def back_kernel(
    final, v_ref, dy_ref, kq_ref, delta_ref, cum_ref, cumt_ref, infc_ref, tailc_ref, tailn_ref,
    keep_ref, inc_ref, dout_ref, dir_ref, segc_ref, segr_ref, dkq_in, dgram_in,
    dv_ref, dkq_ref, dgram, ddelta_ref, dcum_ref, drow_ref, flow_ref,
    gram, gramt, bias, biast, kt, qt, states,
):
    length = v_ref.shape[0]
    count = length // Q
    step = pl.program_id(0)

    @pl.when(step == 0)
    def _():
        for c in range(count):
            rows = slice(c * Q, (c + 1) * Q)
            k, q = kq_ref[rows, :STATE], kq_ref[rows, STATE:]
            b, bt = masks_of(segc_ref, segr_ref, rows)
            bias[rows, :] = b
            biast[rows, :] = bt
            scores = dot3(q, k, NT)
            gram[rows, :] = scores
            gramt[rows, :] = scores.T
            kt[:, rows] = k.T
            qt[:, rows] = q.T
        dgram[...] = dgram_in[...]
        dkq_ref[...] = dkq_in[...]

    low = iota((Q, 128), 1) < HEAD_DIM
    lane = iota((Q, GH), 1)
    line = iota((8, GW), 0)

    states[0] = inc_ref[...].astype(f32)
    for c in range(count):
        rows = slice(c * Q, (c + 1) * Q)
        weighted = v_ref[rows, :] * group_lanes(tailc_ref[0, rows, :])
        states[c + 1] = states[c] * keep_ref[c : c + 1, :] + dot3(kt[:, rows], weighted)

    back = dout_ref[...].astype(f32)
    flows = jnp.zeros((8, GW), f32)
    for c in reversed(range(count)):
        rows = slice(c * Q, (c + 1) * Q)
        flows = jnp.where(line == c, jnp.sum(back * states[c + 1], axis=0, keepdims=True), flows)
        delta, cum = delta_ref[0, rows, :], cum_ref[0, rows, :]
        inflow, tailc, tailn = infc_ref[0, rows, :], tailc_ref[0, rows, :], tailn_ref[0, rows, :]
        k, q = kq_ref[rows, :STATE], kq_ref[rows, STATE:]
        before = states[c]
        after = back
        y_in = dot3(q, before)
        w_in = dot3(k, after)
        g, gt, b, bt = gram[rows, :], gramt[rows, :], bias[rows, :], biast[rows, :]
        dg = dgram[rows, :]
        ddelta = jnp.zeros((Q, GH), f32)
        dcum = jnp.zeros((Q, GH), f32)
        dys, ws = [], []
        for j in range(GW // 128):
            cols = slice(128 * j, 128 * (j + 1))
            dy, v = dy_ref[rows, cols], v_ref[rows, cols]
            spread = pair_lanes(delta, j)
            w = v * spread
            stacked = jnp.concatenate(
                [jnp.where(low, dy, 0.0), jnp.where(low, 0.0, dy)], axis=0
            )
            inner = dot3(stacked, w, NT)
            turned = []
            for i in (0, 1):
                h = 2 * j + i
                col, row = cum[:, h : h + 1], cumt_ref[h : h + 1, rows]
                turned.append(gt * jnp.exp(row - col + bt))
                weighed = inner[Q * i : Q * (i + 1), :] * jnp.exp(col - row + b)
                dg = dg + weighed
                full = weighed * g
                dcum = dcum + jnp.where(lane == h, jnp.sum(full, axis=1, keepdims=True), 0.0)
                drow_ref[h : h + 1, rows] = jnp.sum(full, axis=0, keepdims=True)
            dw_in = w_in[:, cols] * pair_lanes(tailn, j)
            dw = dot3(jnp.concatenate(turned, axis=1), stacked) + dw_in
            dv_ref[rows, cols] = spread * dw + dir_ref[0:1, cols] * dy
            dflow = dy * pair_lanes(inflow, j)
            one = dflow * y_in[:, cols] - w * dw_in
            two = v * dw
            for i in (0, 1):
                h = 2 * j + i
                keep = low if i == 0 else jnp.logical_not(low)
                dcum = dcum + jnp.where(
                    lane == h, jnp.sum(jnp.where(keep, one, 0.0), axis=1, keepdims=True), 0.0
                )
                ddelta = ddelta + jnp.where(
                    lane == h, jnp.sum(jnp.where(keep, two, 0.0), axis=1, keepdims=True), 0.0
                )
            dys.append(dflow)
            ws.append(v * pair_lanes(tailc, j))
        dgram[rows, :] = dg
        ddelta_ref[0, rows, :] = ddelta
        dcum_ref[0, rows, :] = dcum
        flowing = jnp.concatenate(dys, axis=1)
        dkq_ref[rows, STATE:] += dot3(flowing, before, NT)
        dkq_ref[rows, :STATE] += dot3(jnp.concatenate(ws, axis=1), after, NT)
        if c:
            back = back * keep_ref[c : c + 1, :] + dot3(qt[:, rows], flowing)
    flow_ref[...] = flows

    @pl.when(jnp.logical_and(step == pl.num_programs(0) - 1, final))
    def _():
        for c in range(count):
            rows = slice(c * Q, (c + 1) * Q)
            k, q = kq_ref[rows, :STATE], kq_ref[rows, STATE:]
            dg = dgram[rows, :]
            dkq_ref[rows, STATE:] += dot3(dg, k)
            dkq_ref[rows, :STATE] += dot3(dg.T, q)


def back_local(
    first, last, held, v, dy, kq, delta, cum, cumt, infc, tailc, tailn, keep, inc, dout, dirx, segc, segr
):
    length = v.shape[0]
    count = length // Q
    groups = last - first
    if held is None:
        held = (jnp.zeros((length, 2 * STATE), f32), jnp.zeros((length, Q), f32))
    cols = pl.BlockSpec((1, length, GH), lambda g: (g + first, 0, 0))
    wide = pl.BlockSpec((length, GW), lambda g: (0, g + first))
    state = pl.BlockSpec((STATE, GW), lambda g: (0, g + first))
    lines = pl.BlockSpec((8, GW), lambda g: (0, g + first))
    turned = pl.BlockSpec((GH, length), lambda g: (g + first, 0))
    whole = pl.BlockSpec((length, 2 * STATE), lambda g: (0, 0))
    table = pl.BlockSpec((length, Q), lambda g: (0, 0))
    square = pltpu.VMEM((length, Q), f32)
    out_cols = pl.BlockSpec((1, length, GH), lambda g: (g, 0, 0))
    return pl.pallas_call(
        functools.partial(back_kernel, last == NG),
        grid=(groups,),
        in_specs=[
            wide, wide, whole, cols, cols, turned, cols, cols, cols, lines, state, state, lines,
            pl.BlockSpec((length, 8), lambda g: (0, 0)),
            pl.BlockSpec((8, length), lambda g: (0, 0)),
            whole, table,
        ],
        out_specs=(
            pl.BlockSpec((length, GW), lambda g: (0, g)), whole, table, out_cols, out_cols,
            pl.BlockSpec((GH, length), lambda g: (g, 0)),
            pl.BlockSpec((8, GW), lambda g: (0, g)),
        ),
        out_shape=(
            jax.ShapeDtypeStruct((length, groups * GW), f32),
            jax.ShapeDtypeStruct((length, 2 * STATE), f32),
            jax.ShapeDtypeStruct((length, Q), f32),
            jax.ShapeDtypeStruct((groups, length, GH), f32),
            jax.ShapeDtypeStruct((groups, length, GH), f32),
            jax.ShapeDtypeStruct((groups * GH, length), f32),
            jax.ShapeDtypeStruct((8, groups * GW), f32),
        ),
        scratch_shapes=[
            square, square, square, square,
            pltpu.VMEM((STATE, length), f32), pltpu.VMEM((STATE, length), f32),
            pltpu.VMEM((count + 1, STATE, GW), f32),
        ],
        compiler_params=params(),
        cost_estimate=pl.CostEstimate(
            flops=groups * 5 * 10**9, bytes_accessed=groups * 5 * 10**6, transcendentals=groups * 10**6
        ),
        name="back_first" if first == 0 else "back_second",
    )(v, dy, kq, delta, cum, cumt, infc, tailc, tailn, keep, inc, dout, dirx, segc, segr, *held)


def step_kernel(
    step_ref, par_ref, ddelta_a, ddelta_b, dcum_a, dcum_b, drow_a, drow_b, flow_a, flow_b,
    dstep_ref, small_ref,
):
    length = ddelta_a.shape[1]
    half = ddelta_a.shape[0]
    upper = (iota((Q, Q), 0) <= iota((Q, Q), 1)).astype(f32)
    eye = (iota((Q, Q), 0) == iota((Q, Q), 1)).astype(f32)
    last = iota((Q, 1), 0) == Q - 1
    rate = jnp.exp(par_ref[1:2, :])
    spread = head_onehot()
    wide = half * GW
    flows = dotf(flow_a[...], spread[:, :wide], NT) + dotf(flow_b[...], spread[:, wide:], NT)
    top = half * GH
    rise = (iota((HEADS, top), 0) == iota((HEADS, top), 1)).astype(f32)
    fall = (iota((HEADS, HEADS - top), 0) == iota((HEADS, HEADS - top), 1) + top).astype(f32)
    times = jnp.zeros((1, HEADS), f32)
    decays = jnp.zeros((1, HEADS), f32)
    most = jnp.zeros((1, HEADS), f32)
    dstep_ref[...] = jnp.zeros_like(dstep_ref)
    for c in range(length // Q):
        rows = slice(c * Q, (c + 1) * Q)
        ddelta = jnp.zeros((Q, HEADS), f32)
        turned = dotf(rise, drow_a[:, rows]) + dotf(fall, drow_b[:, rows])
        dcum = -dotf(eye, turned, NT)
        for g in range(NG):
            place = (iota((GH, HEADS), 0) + g * GH == iota((GH, HEADS), 1)).astype(f32)
            one, two = (ddelta_a[g, rows, :], dcum_a[g, rows, :]) if g < half else (
                ddelta_b[g - half, rows, :], dcum_b[g - half, rows, :]
            )
            ddelta = ddelta + dotf(one, place)
            dcum = dcum + dotf(two, place)
        dcum = dcum + jnp.where(last, flows[c : c + 1, :], 0.0)
        x = step_ref[pl.ds(HALO + c * Q, Q), :HEADS] + par_ref[0:1, :]
        dlog = dotf(upper, dcum) * rate
        decays = decays - jnp.sum(dlog * softplus(x), axis=0, keepdims=True)
        dstep = (ddelta - dlog) * sigmoid(x)
        times = times + jnp.sum(dstep, axis=0, keepdims=True)
        most = jnp.maximum(most, jnp.max(jnp.abs(dstep), axis=0, keepdims=True))
        dstep_ref[rows, :HEADS] = dstep.astype(bf16)
    dstep_ref[pl.ds(length, PAD), :HEADS] = jnp.broadcast_to(most * 1.01, (PAD, HEADS)).astype(bf16)
    small_ref[...] = jnp.zeros_like(small_ref)
    small_ref[0:1, :] = times
    small_ref[1:2, :] = decays


def step_back(rest, pars, first, second):
    length = first[0].shape[1]
    arrays = [part for both in zip(first, second) for part in both]
    shapes = (
        jax.ShapeDtypeStruct((length + PAD, 128), bf16),
        jax.ShapeDtypeStruct((8, HEADS), f32),
    )
    return pl.pallas_call(
        step_kernel,
        grid=(1,),
        in_specs=[steps_of(rest), whole(pars)] + [whole(array) for array in arrays],
        out_specs=tuple(whole(shape) for shape in shapes),
        out_shape=shapes,
        compiler_params=params(),
        cost_estimate=pl.CostEstimate(flops=10**7, bytes_accessed=10**7, transcendentals=10**5),
        name="step_back",
    )(rest, pars, *arrays)


def unconv_kernel(mixed, x_ref, tap_ref, match_ref, dv_ref, dkq_ref, dx_ref, edge_ref, dtap_ref, *held):
    length = match_ref.shape[1]
    count = length // Q
    wide = pl.program_id(0) < mixed
    for buf in held:
        buf[0:HALO, :] = jnp.zeros((HALO, TILE), f32)
        buf[HALO + length :, :] = jnp.zeros((HALO, TILE), f32)
    for j in range(TILE // 128):
        cols = slice(128 * j, 128 * (j + 1))
        sums = [jnp.zeros((1, 128), f32) for _ in range(KW + 1)]
        for c in range(count):
            rows = slice(c * Q, (c + 1) * Q)
            s = conv_sum(x_ref, tap_ref, match_ref, c * Q, Q, cols)
            sig = sigmoid(s)
            dm = jnp.where(wide, dv_ref[rows, cols], dkq_ref[rows, cols])
            ds = dm * (sig * (1.0 + s * (1.0 - sig)))
            sums[KW] = sums[KW] + jnp.sum(ds, axis=0, keepdims=True)
            for k in range(KW):
                e = ds if k == KW - 1 else ds * match_ref[k, rows, :]
                held[k][HALO + c * Q : HALO + (c + 1) * Q, cols] = e
                taken = x_ref[pl.ds(HALO - (KW - 1) + k + c * Q, Q), cols]
                sums[k] = sums[k] + jnp.sum(e * taken, axis=0, keepdims=True)
        for k in range(KW + 1):
            dtap_ref[k : k + 1, cols] = sums[k]

        def placed(start, rows):
            total = None
            for k in range(KW):
                term = tap_ref[k : k + 1, cols] * held[k][pl.ds(start + KW - 1 - k, rows), cols]
                total = term if total is None else total + term
            return total

        edge_ref[0:HALO, cols] = placed(0, HALO)
        most = jnp.zeros((1, 128), f32)
        for c in range(count):
            dx = placed(HALO + c * Q, Q)
            most = jnp.maximum(most, jnp.max(jnp.abs(dx), axis=0, keepdims=True))
            dx_ref[c * Q : (c + 1) * Q, cols] = dx.astype(bf16)
            if c == count - 1:
                edge_ref[HALO:, cols] = dx[Q - HALO :, :]
        dtap_ref[KW + 1 : KW + 2, cols] = most
    dtap_ref[KW + 2 :, :] = jnp.zeros((8 - KW - 2, TILE), f32)


def unconv(first, rest, taps, match, dv, dkq):
    length = match.shape[1]
    high = length + HALO
    mixed = dv.shape[1] // TILE
    tiles = mixed if dkq is None else mixed + 1
    lone = dv if dkq is None else dkq
    return pl.pallas_call(
        functools.partial(unconv_kernel, mixed),
        grid=(tiles,),
        in_specs=[
            pl.BlockSpec((high, TILE), lambda j: (0, j + first)),
            pl.BlockSpec((8, TILE), lambda j: (0, j + first)),
            pl.BlockSpec((KW - 1, length, 128), lambda j: (0, 0, 0)),
            pl.BlockSpec((length, TILE), lambda j: (0, jnp.minimum(j, mixed - 1))),
            pl.BlockSpec((length, TILE), lambda j: (0, 0)),
        ],
        out_specs=(
            pl.BlockSpec((length, TILE), lambda j: (0, j)),
            pl.BlockSpec((2 * HALO, TILE), lambda j: (0, j)),
            pl.BlockSpec((8, TILE), lambda j: (0, j)),
        ),
        out_shape=(
            jax.ShapeDtypeStruct((length + PAD, tiles * TILE), bf16),
            jax.ShapeDtypeStruct((2 * HALO, tiles * TILE), f32),
            jax.ShapeDtypeStruct((8, tiles * TILE), f32),
        ),
        scratch_shapes=[pltpu.VMEM((length + 2 * HALO, TILE), f32) for _ in range(KW)],
        compiler_params=params(),
        cost_estimate=pl.CostEstimate(flops=10**8, bytes_accessed=10**7, transcendentals=10**6),
    )(rest, taps, match, dv, lone)


def adamw(param, grad, moment, square, rate, shrink):
    moment_new = beta_one * moment + (1.0 - beta_one) * grad
    square_new = beta_two * square + (1.0 - beta_two) * grad * grad
    first_corr = 1.0 - beta_one**ADAM_STEP
    second_corr = 1.0 - beta_two**ADAM_STEP
    update = moment_new / first_corr / (jnp.sqrt(square_new / second_corr) + adam_eps)
    return (param - rate * (update + shrink * param), moment_new, square_new)


def shifted(value, axis, by):
    count = lax.axis_size(axis)
    pairs = [(i, i + by) for i in range(count) if 0 <= i + by < count]
    return lax.ppermute(value, axis, pairs)


TOKENS = (((0,), (0,)), ((), ()))


def gathered(value):
    return lax.all_gather(value, "dp", axis=0, tiled=True)


def shard_gathered(value, *earlier):
    count, here = lax.axis_size("shard"), lax.axis_index("shard")
    rows, width = value.shape
    parts = [exchanged(value, "shard", k) for k in range(1, count)]
    held = jnp.zeros((count * rows, width), value.dtype)
    for k, part in enumerate([value] + parts):
        held = lax.dynamic_update_slice(held, after(part, earlier) if k else part, ((here ^ k) * rows, 0))
    return held


def exchanged(value, axis, by):
    return lax.ppermute(value, axis, [(i, i ^ by) for i in range(lax.axis_size(axis))])


def relative(value, block, core):
    base = lax.axis_index("dp") // 2
    length = value.shape[0]
    return [
        lax.dynamic_slice(value, (0, (((j ^ base) * 2) + core) * block), (length, block))
        for j in range(lax.axis_size("dp") // 2)
    ]


def both_cores(value):
    return jnp.concatenate([value, exchanged(value, "dp", 1)], axis=0)


def own_and_partner(value, block):
    core = lax.axis_index("dp") % 2
    return relative(value, block, core), relative(value, block, 1 - core)


def exponent(bound):
    return jnp.ceil(jnp.log2(jnp.maximum(bound, 1e-30)))


def coded(total, power, rows):
    scaled = total * jnp.exp2(15.0 - power)
    if total.shape[0] > rows:
        scaled = jnp.where(iota(total.shape, 0) < rows, scaled, power)
    return scaled.astype(jnp.float16)


def decoded(payload, power, rows):
    if payload.shape[0] == rows:
        return payload.astype(f32) * jnp.exp2(power - 15.0), power
    other = payload[rows : rows + 1].astype(f32)
    return payload.astype(f32) * jnp.exp2(other - 15.0), jnp.maximum(power, other) + 1.0


def after(value, *earlier):
    return lax.optimization_barrier((value, earlier))[0]


def split_plan(order):
    kept, sends = [0], []
    for bit in reversed(order):
        send = [j ^ (1 << bit) for j in kept]
        sends.insert(0, send)
        kept = kept + send
    return kept, sends


def columns_of(blocks, order, pad):
    kept, sends = split_plan(order)
    zeros = [jnp.zeros((blocks[0].shape[0], pad), bf16)] if pad else []
    return (
        jnp.concatenate([blocks[j] for j in kept[: len(sends[0])]] + zeros, axis=1),
        jnp.concatenate([blocks[j] for j in sends[0]] + zeros, axis=1),
    )


class Sum:
    def __init__(self, held, sent, rhs, power, order, pad):
        self.held, self.sent, self.rhs = held, sent, rhs
        self.power = power
        self.order = order
        self.pad = pad
        self.rows = 2 * (sent.shape[1] - pad)
        self.total = None
        self.at = 0

    def prepare(self):
        self.rows //= 2
        if self.total is None:
            part = lax.dot_general(self.sent, self.rhs, TOKENS, preferred_element_type=f32)
        else:
            part = self.total[self.rows : 2 * self.rows + self.pad]
        self.payload = coded(part, self.power, self.rows)

    def send(self):
        self.got = exchanged(self.payload, "dp", 2 << self.order[self.at])
        self.at += 1
        if self.total is None:
            self.total = lax.dot_general(self.held, self.rhs, TOKENS, preferred_element_type=f32)

    def take(self, *earlier):
        got, self.power = decoded(after(self.got, earlier), self.power, self.rows)
        self.total = self.total[: self.rows + self.pad] + got

    def more(self):
        return self.at < len(self.order)

    def finish(self):
        while self.more():
            self.prepare()
            self.send()
            self.take()


class ShardSum:
    def __init__(self, sums):
        count, here = lax.axis_size("shard"), lax.axis_index("shard")
        self.rows = sums[0].rows // count
        self.total = jnp.concatenate([one.total for one in sums], axis=1) if len(sums) > 1 else sums[0].total
        self.power = jnp.concatenate([one.power for one in sums], axis=1) if len(sums) > 1 else sums[0].power
        taken = (self.rows + sums[0].pad, self.total.shape[1])
        self.payloads = [
            coded(lax.dynamic_slice(self.total, ((here ^ k) * self.rows, 0), taken), self.power, self.rows)
            for k in range(1, count)
        ]
        self.parts = [exchanged(part, "shard", k + 1) for k, part in enumerate(self.payloads)]

    def take(self, *earlier):
        here = lax.axis_index("shard")
        result = lax.dynamic_slice(self.total, (here * self.rows, 0), (self.rows, self.total.shape[1]))
        for part in self.parts:
            result = result + decoded(after(part, earlier), self.power, self.rows)[0][: self.rows]
        return result


def summed(value):
    for axis in ("dp", "shard"):
        count = lax.axis_size(axis)
        if count & (count - 1):
            value = lax.psum(value, axis)
            continue
        by = 1
        while by < count:
            value = value + lax.ppermute(value, axis, [(i, i ^ by) for i in range(count)])
            by *= 2
    return value


def carried(state, half, factor, by):
    incoming = shifted(half, "shard", by)
    for _ in range(1, lax.axis_size("shard") - 1):
        passed = (state + factor * incoming.astype(f32)).astype(bf16)
        incoming = shifted(passed, "shard", by)
    return incoming


def both_with_most(rows):
    length = rows.shape[0] - PAD
    arrived = exchanged(rows, "dp", 1)
    most = jnp.maximum(rows[length : length + 1], arrived[length : length + 1]).astype(f32)
    return jnp.concatenate([rows[:length], arrived[:length]], axis=0), most


def mended(dx, edge, dtap, length):
    last = edge[HALO:] + shifted(edge[:HALO], "shard", -1)
    most = jnp.maximum(dtap[KW + 1 : KW + 2], jnp.max(jnp.abs(last), axis=0, keepdims=True)) * 1.01
    tail = jnp.concatenate([last, jnp.broadcast_to(most, (PAD, most.shape[1]))], axis=0).astype(bf16)
    return lax.dynamic_update_slice(dx, tail, (length - HALO, 0)), dtap


def rest_sums(both, bound, in_columns, orders):
    middle = both.shape[1] // 256 * 128
    power = exponent(bound)
    return [
        Sum(*in_columns[0], both[:, :middle], power[:, :middle], orders[0], PAD),
        Sum(*in_columns[1], both[:, middle:], power[:, middle:], orders[1], PAD),
    ]


def shards(
    hidden_in, cotangent, segment_ids,
    param_prenorm, param_inputs, param_kernel, param_offsets, param_timestep, param_decays,
    param_direct, param_gating, param_outputs,
    moment_prenorm, moment_inputs, moment_kernel, moment_offsets, moment_timestep, moment_decays,
    moment_direct, moment_gating, moment_outputs,
    square_prenorm, square_inputs, square_kernel, square_offsets, square_timestep, square_decays,
    square_direct, square_gating, square_outputs,
):
    length, width = hidden_in.shape
    own_inputs = param_inputs.astype(bf16)
    spare = -(param_inputs.shape[1] - DI) % 128
    upstream = cotangent.astype(bf16)
    own_rows = param_inputs.shape[0]
    most = jnp.broadcast_to((jnp.max(jnp.abs(cotangent)) * 1.01).astype(bf16), (own_rows, 1))
    rest_rows = shard_gathered(
        jnp.concatenate([own_inputs[:, DI:], most, jnp.zeros((own_rows, spare - 1), bf16)], axis=1),
    )
    rest_w = gathered(rest_rows)

    seg = segment_ids.astype(f32)
    ends = jnp.pad(seg[length - HALO :], (0, width - HALO))[None, :]
    halo = shifted(
        jnp.concatenate([hidden_in[length - HALO :], jnp.broadcast_to(ends, (HALO, width))], axis=0),
        "shard", 1,
    )
    rim_seg = jnp.where(lax.axis_index("shard") == 0, -1.0, halo[HALO, :HALO])
    rim = rim_seg[HALO - 1]
    all_segs = jnp.concatenate([rim_seg, seg])
    match = jnp.stack(
        [
            (all_segs[HALO - (KW - 1) + k : HALO - (KW - 1) + k + length] == seg).astype(f32)
            for k in range(KW - 1)
        ]
    )
    match = jnp.broadcast_to(match[:, :, None], (KW - 1, length, 128))
    chunks = seg.reshape(-1, Q)
    before = jnp.concatenate([rim[None], chunks[:-1, Q - 1]])
    mask = jnp.stack(
        [
            (chunks == before[:, None]).reshape(-1),
            (chunks == chunks[:, Q - 1 :]).reshape(-1),
            seg == rim,
            seg == seg[length - 1],
        ]
        + [seg < -1.0] * 4,
        axis=1,
    ).astype(f32)
    segc = jnp.broadcast_to(seg[:, None], (length, 8))
    segr = jnp.broadcast_to(seg[None, :], (8, length))

    taps = jnp.concatenate([param_kernel, param_offsets[None, :], jnp.zeros((8 - KW - 1, CH), f32)], axis=0)
    pars = jnp.concatenate([param_timestep[None, :], param_decays[None, :], jnp.zeros((6, HEADS), f32)], axis=0)
    dirx = jnp.broadcast_to(jnp.repeat(param_direct, HEAD_DIM)[None, :], (8, DI))
    gam = jnp.broadcast_to(param_gating[None, :], (8, DI))

    hidden = jnp.concatenate([halo[:HALO], hidden_in], axis=0)
    inv = lax.rsqrt(jnp.mean(hidden * hidden, axis=1, keepdims=True) + norm_eps)
    normed = (hidden * inv * param_prenorm).astype(bf16)
    own_normed = normed[HALO:]

    groups = lax.axis_size("shard")
    spots = [bit for bit in range(20) if (2 << bit) < lax.axis_size("dp")]
    orders = (spots, spots[::-1])
    in_block, out_block = groups * param_inputs.shape[0], groups * param_outputs.shape[0]
    up_both = both_cores(after(upstream, rest_rows))
    own_blocks, partner_blocks = own_and_partner(own_normed, in_block)
    arrived = exchanged(jnp.concatenate(partner_blocks, axis=1), "dp", 1)
    both_blocks = [
        jnp.concatenate([one, arrived[:, j * in_block : (j + 1) * in_block]], axis=0)
        for j, one in enumerate(own_blocks)
    ]
    in_columns = [columns_of(both_blocks, order, PAD) for order in orders]
    norm_bound = 2.02 * length * width**0.5 * jnp.max(jnp.abs(param_prenorm))
    early = (match, mask, segc, segr, taps, pars, dirx, gam, up_both, norm_bound, in_columns, normed)
    gate_rows = shard_gathered(after(own_inputs[:, :DI], rest_rows), early)
    gate_w = gathered(gate_rows)
    rest_w = after(rest_w, early)

    rest = jnp.dot(normed, rest_w, preferred_element_type=f32)
    delta, cum, cumt, infc, tailc, tailn, taild, infd, keep, factor = prep(rest, pars, mask)
    v, kq, state, state_half = conv_state(rest, taps, match, taild)
    out_rows = shard_gathered(after(param_outputs.astype(bf16), gate_rows), v)
    out_w = gathered(out_rows)
    state = after(state, out_rows)
    incoming = carried(state, state_half, factor[0:1], 1)
    y = local_out(v, kq, delta, cum, cumt, infc, tailc, keep, segc, segr)
    gate_w = after(gate_w, y)
    z = jnp.dot(own_normed, gate_w, preferred_element_type=f32)
    out_w = after(out_w, z)
    back_gated = lax.dot_general(upstream, out_w, NT, preferred_element_type=f32)
    tokens = length * lax.axis_size("dp") * groups
    cotangent_most = jnp.max(rest_w[:, param_inputs.shape[1] - DI]).astype(f32)
    out_power = exponent(1.02 * tokens * DI**0.5 * jnp.max(jnp.abs(param_gating)) * cotangent_most)
    place = lax.axis_index("dp")
    block = out_block if out_block % 128 == 0 and len(spots) == 2 else 0
    at = jnp.stack([place // 2, place % 2]).astype(jnp.int32)
    gated, blocks, dy, dz, dinc, dinc_half, small = gate(
        block, at, y, v, z, back_gated, kq, incoming, infd, dirx, gam
    )

    outgoing = carried(dinc, dinc_half, factor[0:1], -1)
    if not block:
        own_blocks, partner_blocks = own_and_partner(gated, out_block)
        blocks = jnp.stack([*columns_of(own_blocks, spots, 0), *columns_of(partner_blocks, spots, 0)])
    arrived = exchanged(blocks[2:], "dp", 1)
    out_columns = [jnp.concatenate([blocks[i], arrived[i]], axis=0) for i in range(2)]
    dz_most = jnp.broadcast_to(small[2:3] * 1.01, (PAD, DI)).astype(bf16)
    dz = lax.dynamic_update_slice(dz, dz_most, (length, 0))
    dz_both, dz_bound = both_with_most(dz)
    block_out = hidden_in + jnp.dot(gated, out_w, preferred_element_type=f32)
    out_sum = Sum(*out_columns, up_both, out_power, spots, 0)
    gate_sum = Sum(*in_columns[1], dz_both, exponent(norm_bound * dz_bound), spots[::-1], PAD)
    first_sums = [out_sum, gate_sum]
    for one in first_sums:
        one.prepare()
        one.send()
    back_normed = lax.dot_general(dz, gate_w, NT, preferred_element_type=f32)
    outgoing = after(
        outgoing, out_sum.payload, gate_sum.payload, out_sum.total, gate_sum.total, back_normed, block_out
    )

    ssm = (kq, delta, cum, cumt, infc, tailc, tailn, keep, incoming)
    half = NG // 2
    dv1, *held1 = back_local(0, half, None, v, dy, *ssm, outgoing, dirx, segc, segr)
    for one in first_sums:
        one.take(dv1)
        if one.more():
            one.prepare()
            one.send()
    dv1 = after(dv1, *[one.payload for one in first_sums])
    drest1, dtap1 = mended(*unconv(0, rest, taps, match, dv1, None), length)
    both1, bound1 = both_with_most(drest1)
    sums1 = rest_sums(both1, norm_bound * bound1, in_columns, orders)
    for one in first_sums:
        one.take(dv1, both1)
        one.finish()
    shard_out, shard_gate = ShardSum([out_sum]), ShardSum([gate_sum])
    for one in sums1:
        one.prepare()
        one.send()
    dy = after(
        dy, [one.payload for one in sums1], [one.total for one in sums1], shard_out.payloads, shard_gate.payloads
    )
    dv2, *held2 = back_local(half, NG, held1[:2], v, dy, *ssm, outgoing, dirx, segc, segr)
    for one in sums1:
        one.take(dv2)
        if one.more():
            one.prepare()
            one.send()
    dv2 = after(dv2, *[one.payload for one in sums1])
    dstep, small_step = step_back(rest, pars, held1[2:], held2[2:])
    drest2, dtap2 = mended(*unconv(dv1.shape[1] // TILE, rest, taps, match, dv2, held2[0]), length)
    drest2 = jnp.concatenate([drest2, dstep], axis=1)
    both2, bound2 = both_with_most(drest2)
    sums2 = rest_sums(both2, norm_bound * bound2, in_columns, orders)
    for one in sums2:
        one.prepare()
        one.send()
    for one in sums1:
        one.take(dv2, dstep)
        one.finish()
    shard1 = ShardSum(sums1)
    drest1, drest2 = after((drest1, drest2), shard1.payloads, [two.payload for two in sums2])
    wide1 = drest1.shape[1]
    back_normed = back_normed + lax.dot_general(drest1, rest_w[:, :wide1], NT, preferred_element_type=f32)
    back_normed = back_normed + lax.dot_general(drest2, rest_w[:, wide1:], NT, preferred_element_type=f32)
    back_normed = back_normed[:length]
    for one in sums2:
        one.take(back_normed)
        if one.more():
            one.prepare()
            one.send()
    sent = [one.payload for one in sums2]
    grad_outputs = shard_out.take(sent)
    grad_gate = shard_gate.take(sent)
    for one in sums2:
        one.take()
        one.finish()
    shard2 = ShardSum(sums2)
    grad_rest = jnp.concatenate([shard1.take(sent), shard2.take()], axis=1)
    grad_inputs = jnp.concatenate([grad_gate, grad_rest[:, : param_inputs.shape[1] - DI]], axis=1)
    dtap = jnp.concatenate([dtap1, dtap2], axis=1)

    own_inv = inv[HALO:]
    scaled = hidden_in * own_inv
    gained = back_normed * param_prenorm
    hidden_grad = cotangent + own_inv * (
        gained - scaled * jnp.mean(gained * scaled, axis=1, keepdims=True)
    )
    grad_prenorm = jnp.sum(back_normed * scaled, axis=0)

    pieces = [
        grad_prenorm,
        dtap[:KW].reshape(-1),
        dtap[KW],
        small_step[0],
        small_step[1],
        jnp.sum(small[1].reshape(HEADS, HEAD_DIM), axis=1),
        small[0],
    ]
    flat = after(jnp.concatenate(pieces), sent)
    count = flat.shape[0]
    lines = -(-count // 1024) * 8
    total = summed(jnp.pad(flat, (0, lines * 128 - count)).reshape(lines, 128)).reshape(-1)
    found, at = [], 0
    for piece in pieces:
        found.append(total[at : at + piece.shape[0]])
        at += piece.shape[0]
    grad_prenorm, grad_kernel, grad_offsets, grad_timestep, grad_decays, grad_direct, grad_gating = found
    grad_kernel = grad_kernel.reshape(KW, CH)

    params = (
        param_prenorm, param_inputs, param_kernel, param_offsets, param_timestep, param_decays,
        param_direct, param_gating, param_outputs,
    )
    moments = (
        moment_prenorm, moment_inputs, moment_kernel, moment_offsets, moment_timestep, moment_decays,
        moment_direct, moment_gating, moment_outputs,
    )
    squares = (
        square_prenorm, square_inputs, square_kernel, square_offsets, square_timestep, square_decays,
        square_direct, square_gating, square_outputs,
    )
    grads = (
        grad_prenorm, grad_inputs, grad_kernel, grad_offsets, grad_timestep, grad_decays,
        grad_direct, grad_gating, grad_outputs,
    )
    updated = [
        adamw(params[i], grads[i], moments[i], squares[i], rate_table[i], shrink_table[i])
        for i in range(9)
    ]
    return (
        (block_out, hidden_grad)
        + grads
        + tuple(u[0] for u in updated)
        + tuple(u[1] for u in updated)
        + tuple(u[2] for u in updated)
    )


def solution(mesh):
    rows = P(("dp", "shard"), None)
    member = (P(), rows, P(), P(), P(), P(), P(), P(), rows)

    return jax.shard_map(
        shards,
        mesh=mesh,
        in_specs=(rows, rows, P(("dp", "shard"))) + member * 3,
        out_specs=(rows, rows) + member * 4,
        check_vma=False,
    )
```

```python
import functools

import jax
import jax.numpy as jnp
from jax import lax
from jax.experimental import pallas as pl
from jax.experimental.pallas import tpu as pltpu
from jax.sharding import PartitionSpec as P


HEADS = 48
HEAD_DIM = 64
STATE = 128
KW = 4
ADAM_STEP = 10
DI = 3072
CH = 3328

Q = 128
GH = 8
GW = GH * HEAD_DIM
NG = HEADS // GH
HALO = 8
PAD = 16
TILE = 256

bf16 = jnp.bfloat16
f32 = jnp.float32
highest = lax.Precision.HIGHEST

norm_eps = 1e-05
beta_one = 0.9
beta_two = 0.95
adam_eps = 1e-08
rate_table = (0.2, 0.01, 0.2, 0.2, 0.2, 0.2, 0.2, 0.2, 0.01)
shrink_table = (0.0, 0.1, 0.1, 0.0, 0.0, 0.0, 0.0, 0.0, 0.1)

NN = (((1,), (0,)), ((), ()))
NT = (((1,), (1,)), ((), ()))


def halves(x):
    hi = x.astype(bf16)
    return hi, (x - hi.astype(f32)).astype(bf16)


def dot1(a, b, dims=NN):
    return lax.dot_general(a.astype(bf16), b.astype(bf16), dims, preferred_element_type=f32)


def dot3(a, b, dims=NN):
    ah, al = halves(a)
    bh, bl = halves(b)
    return dot1(ah, bh, dims) + (dot1(ah, bl, dims) + dot1(al, bh, dims))


def dot_halves(a, b, dims=NN):
    return dot1(a[0], b[0], dims) + (dot1(a[0], b[1], dims) + dot1(a[1], b[0], dims))


def dotf(a, b, dims=NN):
    return lax.dot_general(a, b, dims, precision=highest, preferred_element_type=f32)


def iota(shape, dim):
    return lax.broadcasted_iota(jnp.int32, shape, dim)


def sigmoid(x):
    return 0.5 * jnp.tanh(0.5 * x) + 0.5


def softplus(x):
    u = jnp.exp(-jnp.abs(x))
    series = u * (1.0 - u * (0.5 - u * (1.0 / 3.0 - u * (0.25 - u * 0.2))))
    return jnp.maximum(x, 0.0) + jnp.where(u < 0.03, series, jnp.log(1.0 + u))


def pair_lanes(cols, j):
    rows = cols.shape[0]
    low = iota((rows, 128), 1) < HEAD_DIM
    return jnp.where(low, cols[:, 2 * j : 2 * j + 1], cols[:, 2 * j + 1 : 2 * j + 2])


def group_lanes(cols):
    return jnp.concatenate([pair_lanes(cols, j) for j in range(cols.shape[1] // 2)], axis=1)


def head_onehot():
    return (iota((HEADS, DI), 1) // HEAD_DIM == iota((HEADS, DI), 0)).astype(f32)


def params(limit=60000, **kw):
    return pltpu.CompilerParams(vmem_limit_bytes=limit * 1024, **kw)


def prep_kernel(
    step_ref, par_ref, mask_ref, delta_ref, cum_ref, cumt_ref, tailc_ref,
    taild_ref, infd_ref, keep_ref, factor_ref,
):
    length = mask_ref.shape[0]
    count = length // Q
    tri = (iota((Q, Q), 0) >= iota((Q, Q), 1)).astype(f32)
    eye = (iota((HEADS, HEADS), 0) == iota((HEADS, HEADS), 1)).astype(f32)
    rate = jnp.exp(par_ref[1:2, :])
    base = jnp.zeros((1, HEADS), f32)
    held = []
    keeps = []
    for c in range(count):
        rows = slice(c * Q, (c + 1) * Q)
        delta = softplus(step_ref[pl.ds(HALO + c * Q, Q), :HEADS] + par_ref[0:1, :])
        cum = dotf(tri, -delta * rate)
        cumt_ref[:, rows] = dotf(eye, cum, NT)
        last = cum[Q - 1 : Q, :]
        tailc = jnp.exp(last - cum) * mask_ref[rows, 1:2] * delta
        for g in range(NG):
            part = slice(g * GH, (g + 1) * GH)
            delta_ref[g, rows, :] = delta[:, part]
            cum_ref[g, rows, :] = cum[:, part]
            tailc_ref[g, rows, :] = tailc[:, part]
        keeps.append(jnp.exp(last) * mask_ref[(c + 1) * Q - 1 : (c + 1) * Q, 0:1])
        whole = cum + base
        infd_ref[rows, :] = jnp.exp(whole) * mask_ref[rows, 2:3]
        held.append((whole, delta))
        base = base + last
    for c in range(count):
        rows = slice(c * Q, (c + 1) * Q)
        whole, delta = held[c]
        taild = jnp.exp(base - whole) * mask_ref[rows, 3:4] * delta
        for g in range(NG):
            taild_ref[g, rows, :] = taild[:, g * GH : (g + 1) * GH]
    factor = jnp.exp(base) * mask_ref[length - 1 : length, 2:3]
    spread = head_onehot()
    line = iota((8, HEADS), 0)
    table = jnp.zeros((8, HEADS), f32)
    for c in range(count):
        table = jnp.where(line == c, keeps[c], table)
    keep_ref[...] = dotf(table, spread)
    factor_ref[...] = dotf(jnp.where(line == 0, factor, 0.0), spread)


def whole(array):
    return pl.BlockSpec(array.shape, lambda i: (0,) * array.ndim)


def steps_of(rest):
    return pl.BlockSpec((rest.shape[0], 128), lambda i: (0, CH // 128))


def prep(rest, pars, mask):
    length = mask.shape[0]
    cols = jax.ShapeDtypeStruct((NG, length, GH), f32)
    wide = jax.ShapeDtypeStruct((8, DI), f32)
    shapes = (
        cols, cols, jax.ShapeDtypeStruct((HEADS, length), f32), cols, cols,
        jax.ShapeDtypeStruct((length, HEADS), f32), wide, wide,
    )
    return pl.pallas_call(
        prep_kernel,
        grid=(1,),
        in_specs=[steps_of(rest), whole(pars), whole(mask)],
        out_specs=tuple(whole(shape) for shape in shapes),
        out_shape=shapes,
        compiler_params=params(),
        cost_estimate=pl.CostEstimate(flops=10**7, bytes_accessed=10**7, transcendentals=10**5),
        name="prep",
    )(rest, pars, mask)


def conv_sum(x_ref, tap_ref, match_ref, start, rows, cols):
    total = tap_ref[KW : KW + 1, cols] + tap_ref[KW - 1 : KW, cols] * x_ref[
        pl.ds(HALO + start, rows), cols
    ]
    for k in range(KW - 1):
        taken = x_ref[pl.ds(HALO - (KW - 1) + k + start, rows), cols]
        total = total + tap_ref[k : k + 1, cols] * (taken * match_ref[k, pl.ds(start, rows), :])
    return total


def conv_kernel(
    xv_ref, xk_ref, tv_ref, tk_ref, match_ref, taild_ref, v_ref, kq_ref, state_ref, state_half_ref, kt_hi, kt_lo
):
    length = v_ref.shape[0]
    count = length // Q

    @pl.when(pl.program_id(0) == 0)
    def _():
        for c in range(count):
            for j in range(2):
                cols = slice(128 * j, 128 * (j + 1))
                s = conv_sum(xk_ref, tk_ref, match_ref, c * Q, Q, cols)
                m = s * sigmoid(s)
                kq_ref[c * Q : (c + 1) * Q, cols] = m
                if j == 0:
                    hi, lo = halves(m.T)
                    kt_hi[:, c * Q : (c + 1) * Q] = hi
                    kt_lo[:, c * Q : (c + 1) * Q] = lo

    total = jnp.zeros((STATE, GW), f32)
    for c in range(count):
        rows = slice(c * Q, (c + 1) * Q)
        tail = taild_ref[0, rows, :]
        parts = []
        for j in range(GW // 128):
            cols = slice(128 * j, 128 * (j + 1))
            s = conv_sum(xv_ref, tv_ref, match_ref, c * Q, Q, cols)
            m = s * sigmoid(s)
            v_ref[rows, cols] = m
            parts.append(m * pair_lanes(tail, j))
        hi, lo = halves(jnp.concatenate(parts, axis=1))
        kh, kl = kt_hi[:, rows], kt_lo[:, rows]
        total = total + (dot1(kh, hi) + (dot1(kh, lo) + dot1(kl, hi)))
    state_ref[...] = total
    state_half_ref[...] = total.astype(bf16)


def conv_state(rest, taps, match, taild):
    length = match.shape[1]
    high = length + HALO
    kq_at = DI // (2 * STATE)
    return pl.pallas_call(
        conv_kernel,
        grid=(NG,),
        in_specs=[
            pl.BlockSpec((high, GW), lambda g: (0, g)),
            pl.BlockSpec((high, 2 * STATE), lambda g: (0, kq_at)),
            pl.BlockSpec((8, GW), lambda g: (0, g)),
            pl.BlockSpec((8, 2 * STATE), lambda g: (0, kq_at)),
            pl.BlockSpec((KW - 1, length, 128), lambda g: (0, 0, 0)),
            pl.BlockSpec((1, length, GH), lambda g: (g, 0, 0)),
        ],
        out_specs=(
            pl.BlockSpec((length, GW), lambda g: (0, g)),
            pl.BlockSpec((length, 2 * STATE), lambda g: (0, 0)),
            pl.BlockSpec((STATE, GW), lambda g: (0, g)),
            pl.BlockSpec((STATE, GW), lambda g: (0, g)),
        ),
        out_shape=(
            jax.ShapeDtypeStruct((length, DI), f32),
            jax.ShapeDtypeStruct((length, 2 * STATE), f32),
            jax.ShapeDtypeStruct((STATE, DI), f32),
            jax.ShapeDtypeStruct((STATE, DI), bf16),
        ),
        scratch_shapes=[pltpu.VMEM((STATE, length), bf16), pltpu.VMEM((STATE, length), bf16)],
        compiler_params=params(),
        cost_estimate=pl.CostEstimate(flops=2 * 10**9, bytes_accessed=2 * 10**7, transcendentals=2 * 10**6),
        name="conv_state",
    )(rest, rest, taps, taps, match, taild)


def masks_of(segc_ref, segr_ref, rows):
    same = segc_ref[rows, 0:1] == segr_ref[0:1, rows]
    later = iota((Q, Q), 0) >= iota((Q, Q), 1)
    earlier = iota((Q, Q), 0) <= iota((Q, Q), 1)
    return jnp.where(same & later, 0.0, -1e30), jnp.where(same & earlier, 0.0, -1e30)


def local_kernel(
    v_ref, kq_ref, delta_ref, cum_ref, cumt_ref, mask_ref, keep_ref, segc_ref, segr_ref,
    y_ref, gram, bias, kt_hi, kt_lo,
):
    length = v_ref.shape[0]
    count = length // Q

    @pl.when(pl.program_id(0) == 0)
    def _():
        for c in range(count):
            rows = slice(c * Q, (c + 1) * Q)
            k, q = kq_ref[rows, :STATE], kq_ref[rows, STATE:]
            bias[rows, :] = masks_of(segc_ref, segr_ref, rows)[0]
            gram[rows, :] = dot3(q, k, NT)
            kt_hi[:, rows], kt_lo[:, rows] = halves(k.T)

    low = iota((Q, 128), 1) < HEAD_DIM
    state = None
    for c in range(count):
        rows = slice(c * Q, (c + 1) * Q)
        delta, cum = delta_ref[0, rows, :], cum_ref[0, rows, :]
        alive = jnp.broadcast_to(mask_ref[rows, 0:1], (Q, 128))
        ending = jnp.broadcast_to(mask_ref[rows, 1:2], (Q, 128))
        if c:
            carried = dot3(kq_ref[rows, STATE:], state)
        tails = []
        for j in range(GW // 128):
            cols = slice(128 * j, 128 * (j + 1))
            w = v_ref[rows, cols] * pair_lanes(delta, j)
            run = pair_lanes(cum, j)
            both = []
            for i in (2 * j, 2 * j + 1):
                fade = jnp.exp(cum[:, i : i + 1] - cumt_ref[i : i + 1, rows] + bias[rows, :])
                both.append(halves(gram[rows, :] * fade))
            parts = halves(w)
            zero = jnp.zeros_like(parts[0])
            stacked = tuple(
                jnp.concatenate([jnp.where(low, part, zero), jnp.where(low, zero, part)], axis=0)
                for part in parts
            )
            y = dot_halves(tuple(jnp.concatenate([both[0][i], both[1][i]], axis=1) for i in (0, 1)), stacked)
            if c:
                y = y + carried[:, cols] * (jnp.exp(run) * alive)
            y_ref[rows, cols] = y
            if c < count - 1:
                tails.append(halves(w * (jnp.exp(run[Q - 1 : Q, :] - run) * ending)))
        if c < count - 1:
            fresh = dot_halves(
                (kt_hi[:, rows], kt_lo[:, rows]),
                tuple(jnp.concatenate([part[i] for part in tails], axis=1) for i in (0, 1)),
            )
            state = fresh if state is None else state * keep_ref[c : c + 1, :] + fresh


def local_out(v, kq, delta, cum, cumt, mask, keep, segc, segr):
    length = v.shape[0]
    cols = pl.BlockSpec((1, length, GH), lambda g: (g, 0, 0))
    return pl.pallas_call(
        local_kernel,
        grid=(NG,),
        in_specs=[
            pl.BlockSpec((length, GW), lambda g: (0, g)),
            pl.BlockSpec((length, 2 * STATE), lambda g: (0, 0)),
            cols, cols,
            pl.BlockSpec((GH, length), lambda g: (g, 0)),
            pl.BlockSpec((length, 8), lambda g: (0, 0)),
            pl.BlockSpec((8, GW), lambda g: (0, g)),
            pl.BlockSpec((length, 8), lambda g: (0, 0)),
            pl.BlockSpec((8, length), lambda g: (0, 0)),
        ],
        out_specs=pl.BlockSpec((length, GW), lambda g: (0, g)),
        out_shape=jax.ShapeDtypeStruct((length, DI), f32),
        scratch_shapes=[
            pltpu.VMEM((length, Q), f32), pltpu.VMEM((length, Q), f32),
            pltpu.VMEM((STATE, length), bf16), pltpu.VMEM((STATE, length), bf16),
        ],
        compiler_params=params(),
        cost_estimate=pl.CostEstimate(flops=2 * 10**9, bytes_accessed=2 * 10**7, transcendentals=4 * 10**6),
        name="local_out",
    )(v, kq, delta, cum, cumt, mask, keep, segc, segr)


def gate_kernel(
    block, at_ref, y_ref, v_ref, z_ref, g_ref, kq_ref, inc_ref, infd_ref, dir_ref, gam_ref,
    out_ref, blocks_ref, dy_ref, dz_ref, dinc_ref, dinc_half_ref, small_ref, ybuf, rbuf,
):
    first = pl.program_id(0) == 0
    rows = y_ref.shape[0]
    q = kq_ref[:, STATE:]
    inflow = infd_ref[...]
    square = jnp.zeros((rows, 128), f32)
    cross = jnp.zeros((rows, 128), f32)
    for j in range(DI // 128):
        cols = slice(128 * j, 128 * (j + 1))
        carry = dot3(q, inc_ref[:, cols]) * pair_lanes(inflow, j)
        y = y_ref[:, cols] + carry + dir_ref[0:1, cols] * v_ref[:, cols]
        z = z_ref[:, cols]
        gated = y * (z * sigmoid(z))
        ybuf[:, cols] = y
        rbuf[:, cols] = gated
        square = square + gated * gated
        cross = cross + gated * (g_ref[:, cols] * gam_ref[0:1, cols])
    inv = lax.rsqrt(jnp.sum(square, axis=1, keepdims=True) * (1.0 / DI) + norm_eps)
    slope = inv * inv * inv * (jnp.sum(cross, axis=1, keepdims=True) * (1.0 / DI))
    qt = q.T

    @pl.when(first)
    def _():
        dinc_ref[...] = jnp.zeros_like(dinc_ref)
        small_ref[...] = jnp.zeros_like(small_ref)

    for j in range(DI // 128):
        cols = slice(128 * j, 128 * (j + 1))
        gated = rbuf[:, cols]
        scaled = gated * inv
        gam = gam_ref[0:1, cols]
        half = (scaled * gam).astype(bf16)
        out_ref[:, cols] = half
        if block:
            per = block // 128
            far = ((j // per) >> 1) ^ at_ref[0]
            which = 2 * (((j // per) & 1) ^ at_ref[1]) + (far & 1)
            place = pl.multiple_of((far >> 1) * block + (j % per) * 128, 128)
            blocks_ref[which, :, pl.ds(place, 128)] = half
        g = g_ref[:, cols]
        dgated = inv * (g * gam) - gated * slope
        z = z_ref[:, cols]
        s = sigmoid(z)
        dy = dgated * (z * s)
        dy_ref[:, cols] = dy
        dz = dgated * ybuf[:, cols] * (s * (1.0 + z * (1.0 - s)))
        dz_ref[:, cols] = dz.astype(bf16)
        small_ref[2:3, cols] = jnp.maximum(
            small_ref[2:3, cols], jnp.max(jnp.abs(dz), axis=0, keepdims=True)
        )
        small_ref[0:1, cols] += jnp.sum(g * scaled, axis=0, keepdims=True)
        small_ref[1:2, cols] += jnp.sum(dy * v_ref[:, cols], axis=0, keepdims=True)
        dinc_ref[:, cols] += dot3(qt, dy * pair_lanes(inflow, j))

    @pl.when(pl.program_id(0) == pl.num_programs(0) - 1)
    def _():
        dinc_half_ref[...] = dinc_ref[...].astype(bf16)


def gate(block, at, y, v, z, g, kq, inc, infd, dirx, gam):
    length = y.shape[0]
    tile = Q
    big = pl.BlockSpec((tile, DI), lambda i, at: (i, 0))
    fixed = lambda rows: pl.BlockSpec((rows, DI), lambda i, at: (0, 0))
    spare = 2 * block if block else 128
    return pl.pallas_call(
        functools.partial(gate_kernel, block),
        grid_spec=pltpu.PrefetchScalarGridSpec(
            num_scalar_prefetch=1,
            grid=(length // tile,),
            in_specs=[
                big, big, big, big,
                pl.BlockSpec((tile, 2 * STATE), lambda i, at: (i, 0)),
                fixed(STATE),
                pl.BlockSpec((tile, HEADS), lambda i, at: (i, 0)),
                fixed(8), fixed(8),
            ],
            out_specs=(
                big, pl.BlockSpec((4, tile, spare), lambda i, at: (0, i, 0)), big, big,
                fixed(STATE), fixed(STATE), fixed(8),
            ),
            scratch_shapes=[pltpu.VMEM((tile, DI), f32), pltpu.VMEM((tile, DI), f32)],
        ),
        out_shape=(
            jax.ShapeDtypeStruct((length, DI), bf16),
            jax.ShapeDtypeStruct((4, length, spare), bf16),
            jax.ShapeDtypeStruct((length, DI), f32),
            jax.ShapeDtypeStruct((length + PAD, DI), bf16),
            jax.ShapeDtypeStruct((STATE, DI), f32),
            jax.ShapeDtypeStruct((STATE, DI), bf16),
            jax.ShapeDtypeStruct((8, DI), f32),
        ),
        compiler_params=params(),
        cost_estimate=pl.CostEstimate(flops=10**9, bytes_accessed=4 * 10**7, transcendentals=4 * 10**6),
        name="gate",
    )(at, y, v, z, g, kq, inc, infd, dirx, gam)


def back_kernel(
    final, v_ref, dy_ref, kq_ref, delta_ref, cum_ref, cumt_ref, tailc_ref, mask_ref, keep_ref,
    inc_ref, dout_ref, dir_ref, segc_ref, segr_ref, dkq_in, dgram_in,
    dv_ref, dkq_ref, dgram, ddelta_ref, dcum_ref, drow_ref, flow_ref,
    gram, gramt, bias, biast, kt_hi, kt_lo, qt_hi, qt_lo, kq_hi, kq_lo, states,
):
    length = v_ref.shape[0]
    count = length // Q
    step = pl.program_id(0)

    @pl.when(step == 0)
    def _():
        for c in range(count):
            rows = slice(c * Q, (c + 1) * Q)
            k, q = kq_ref[rows, :STATE], kq_ref[rows, STATE:]
            b, bt = masks_of(segc_ref, segr_ref, rows)
            bias[rows, :] = b
            biast[rows, :] = bt
            scores = dot3(q, k, NT)
            gram[rows, :] = scores
            gramt[rows, :] = scores.T
            kt_hi[:, rows], kt_lo[:, rows] = halves(k.T)
            qt_hi[:, rows], qt_lo[:, rows] = halves(q.T)
            kq_hi[rows, :], kq_lo[rows, :] = halves(kq_ref[rows, :])
        dgram[...] = dgram_in[...]
        dkq_ref[...] = dkq_in[...]

    low = iota((Q, 128), 1) < HEAD_DIM
    lane = iota((Q, GH), 1)
    line = iota((8, GW), 0)

    states[0] = inc_ref[...].astype(f32)
    for c in range(count):
        rows = slice(c * Q, (c + 1) * Q)
        weighted = halves(v_ref[rows, :] * group_lanes(tailc_ref[0, rows, :]))
        states[c + 1] = states[c] * keep_ref[c : c + 1, :] + dot_halves(
            (kt_hi[:, rows], kt_lo[:, rows]), weighted
        )

    back = dout_ref[...].astype(f32)
    flows = jnp.zeros((8, GW), f32)
    for c in reversed(range(count)):
        rows = slice(c * Q, (c + 1) * Q)
        flows = jnp.where(line == c, jnp.sum(back * states[c + 1], axis=0, keepdims=True), flows)
        delta, cum = delta_ref[0, rows, :], cum_ref[0, rows, :]
        before = halves(states[c])
        after = halves(back)
        k, q = (kq_hi[rows, :STATE], kq_lo[rows, :STATE]), (kq_hi[rows, STATE:], kq_lo[rows, STATE:])
        y_in = dot_halves(q, before)
        w_in = dot_halves(k, after)
        alive = jnp.broadcast_to(mask_ref[rows, 0:1], (Q, 128))
        ending = jnp.broadcast_to(mask_ref[rows, 1:2], (Q, 128))
        ddelta = jnp.zeros((Q, GH), f32)
        dcum = jnp.zeros((Q, GH), f32)
        dys, ws = [], []
        for j in range(GW // 128):
            cols = slice(128 * j, 128 * (j + 1))
            dy, v = dy_ref[rows, cols], v_ref[rows, cols]
            spread = pair_lanes(delta, j)
            w = v * spread
            dy_hi, dy_lo = halves(dy)
            zero = jnp.zeros_like(dy_hi)
            stacked = tuple(
                jnp.concatenate([jnp.where(low, part, zero), jnp.where(low, zero, part)], axis=0)
                for part in (dy_hi, dy_lo)
            )
            inner = dot_halves(stacked, halves(w), NT)
            run = jnp.where(low, cum[:, 2 * j : 2 * j + 1], cum[:, 2 * j + 1 : 2 * j + 2])
            dflow = dy * (jnp.exp(run) * alive)
            tail = jnp.exp(run[Q - 1 : Q, :] - run) * ending
            dw_in = w_in[:, cols] * tail
            one = dflow * y_in[:, cols] - w * dw_in
            turned = []
            for i in (0, 1):
                h = 2 * j + i
                col, row = cum[:, h : h + 1], cumt_ref[h : h + 1, rows]
                turned.append(halves(gramt[rows, :] * jnp.exp(row - col + biast[rows, :])))
                weighed = inner[Q * i : Q * (i + 1), :] * jnp.exp(col - row + bias[rows, :])
                dgram[rows, :] += weighed
                full = weighed * gram[rows, :]
                drow_ref[h : h + 1, rows] = jnp.sum(full, axis=0, keepdims=True)
                keep = low if i == 0 else jnp.logical_not(low)
                full = full + jnp.where(keep, one, 0.0)
                dcum_ref[0, rows, h : h + 1] = jnp.sum(full, axis=1, keepdims=True)
            dw = dot_halves(
                tuple(jnp.concatenate([turned[0][i], turned[1][i]], axis=1) for i in (0, 1)), stacked
            ) + dw_in
            dv_ref[rows, cols] = spread * dw + dir_ref[0:1, cols] * dy
            two = v * dw
            for i in (0, 1):
                keep = low if i == 0 else jnp.logical_not(low)
                h = 2 * j + i
                ddelta_ref[0, rows, h : h + 1] = jnp.sum(jnp.where(keep, two, 0.0), axis=1, keepdims=True)
            dys.append(halves(dflow))
            ws.append(halves(w * tail))
        flowing = tuple(jnp.concatenate([part[i] for part in dys], axis=1) for i in (0, 1))
        leaving = tuple(jnp.concatenate([part[i] for part in ws], axis=1) for i in (0, 1))
        dkq_ref[rows, STATE:] += dot_halves(flowing, before, NT)
        dkq_ref[rows, :STATE] += dot_halves(leaving, after, NT)
        if c:
            back = back * keep_ref[c : c + 1, :] + dot_halves((qt_hi[:, rows], qt_lo[:, rows]), flowing)
    flow_ref[...] = flows

    @pl.when(jnp.logical_and(step == pl.num_programs(0) - 1, final))
    def _():
        for c in range(count):
            rows = slice(c * Q, (c + 1) * Q)
            k, q = kq_ref[rows, :STATE], kq_ref[rows, STATE:]
            dg = dgram[rows, :]
            dkq_ref[rows, STATE:] += dot3(dg, k)
            dkq_ref[rows, :STATE] += dot3(dg.T, q)


def back_local(
    first, last, held, v, dy, kq, delta, cum, cumt, tailc, mask, keep, inc, dout, dirx, segc, segr
):
    length = v.shape[0]
    count = length // Q
    groups = last - first
    if held is None:
        held = (jnp.zeros((length, 2 * STATE), f32), jnp.zeros((length, Q), f32))
    cols = pl.BlockSpec((1, length, GH), lambda g: (g + first, 0, 0))
    wide = pl.BlockSpec((length, GW), lambda g: (0, g + first))
    state = pl.BlockSpec((STATE, GW), lambda g: (0, g + first))
    lines = pl.BlockSpec((8, GW), lambda g: (0, g + first))
    turned = pl.BlockSpec((GH, length), lambda g: (g + first, 0))
    whole = pl.BlockSpec((length, 2 * STATE), lambda g: (0, 0))
    table = pl.BlockSpec((length, Q), lambda g: (0, 0))
    square = pltpu.VMEM((length, Q), f32)
    out_cols = pl.BlockSpec((1, length, GH), lambda g: (g, 0, 0))
    return pl.pallas_call(
        functools.partial(back_kernel, last == NG),
        grid=(groups,),
        in_specs=[
            wide, wide, whole, cols, cols, turned, cols, pl.BlockSpec((length, 8), lambda g: (0, 0)), lines,
            state, state, lines,
            pl.BlockSpec((length, 8), lambda g: (0, 0)),
            pl.BlockSpec((8, length), lambda g: (0, 0)),
            whole, table,
        ],
        out_specs=(
            pl.BlockSpec((length, GW), lambda g: (0, g)), whole, table, out_cols, out_cols,
            pl.BlockSpec((GH, length), lambda g: (g, 0)),
            pl.BlockSpec((8, GW), lambda g: (0, g)),
        ),
        out_shape=(
            jax.ShapeDtypeStruct((length, groups * GW), f32),
            jax.ShapeDtypeStruct((length, 2 * STATE), f32),
            jax.ShapeDtypeStruct((length, Q), f32),
            jax.ShapeDtypeStruct((groups, length, GH), f32),
            jax.ShapeDtypeStruct((groups, length, GH), f32),
            jax.ShapeDtypeStruct((groups * GH, length), f32),
            jax.ShapeDtypeStruct((8, groups * GW), f32),
        ),
        scratch_shapes=[
            square, square, square, square,
            *[pltpu.VMEM((STATE, length), bf16) for _ in range(4)],
            *[pltpu.VMEM((length, 2 * STATE), bf16) for _ in range(2)],
            pltpu.VMEM((count + 1, STATE, GW), f32),
        ],
        compiler_params=params(),
        cost_estimate=pl.CostEstimate(
            flops=groups * 5 * 10**9, bytes_accessed=groups * 5 * 10**6, transcendentals=groups * 10**6
        ),
        name="back_first" if first == 0 else "back_second",
    )(v, dy, kq, delta, cum, cumt, tailc, mask, keep, inc, dout, dirx, segc, segr, *held)


def step_kernel(
    step_ref, par_ref, ddelta_a, ddelta_b, dcum_a, dcum_b, drow_a, drow_b, flow_a, flow_b,
    dstep_ref, small_ref,
):
    length = ddelta_a.shape[1]
    half = ddelta_a.shape[0]
    upper = (iota((Q, Q), 0) <= iota((Q, Q), 1)).astype(f32)
    eye = (iota((Q, Q), 0) == iota((Q, Q), 1)).astype(f32)
    last = iota((Q, 1), 0) == Q - 1
    rate = jnp.exp(par_ref[1:2, :])
    spread = head_onehot()
    wide = half * GW
    flows = dotf(flow_a[...], spread[:, :wide], NT) + dotf(flow_b[...], spread[:, wide:], NT)
    top = half * GH
    rise = (iota((HEADS, top), 0) == iota((HEADS, top), 1)).astype(f32)
    fall = (iota((HEADS, HEADS - top), 0) == iota((HEADS, HEADS - top), 1) + top).astype(f32)
    times = jnp.zeros((1, HEADS), f32)
    decays = jnp.zeros((1, HEADS), f32)
    most = jnp.zeros((1, HEADS), f32)
    dstep_ref[...] = jnp.zeros_like(dstep_ref)
    for c in range(length // Q):
        rows = slice(c * Q, (c + 1) * Q)
        ddelta = jnp.zeros((Q, HEADS), f32)
        turned = dotf(rise, drow_a[:, rows]) + dotf(fall, drow_b[:, rows])
        dcum = -dotf(eye, turned, NT)
        for g in range(NG):
            place = (iota((GH, HEADS), 0) + g * GH == iota((GH, HEADS), 1)).astype(f32)
            one, two = (ddelta_a[g, rows, :], dcum_a[g, rows, :]) if g < half else (
                ddelta_b[g - half, rows, :], dcum_b[g - half, rows, :]
            )
            ddelta = ddelta + dotf(one, place)
            dcum = dcum + dotf(two, place)
        dcum = dcum + jnp.where(last, flows[c : c + 1, :], 0.0)
        x = step_ref[pl.ds(HALO + c * Q, Q), :HEADS] + par_ref[0:1, :]
        dlog = dotf(upper, dcum) * rate
        decays = decays - jnp.sum(dlog * softplus(x), axis=0, keepdims=True)
        dstep = (ddelta - dlog) * sigmoid(x)
        times = times + jnp.sum(dstep, axis=0, keepdims=True)
        most = jnp.maximum(most, jnp.max(jnp.abs(dstep), axis=0, keepdims=True))
        dstep_ref[rows, :HEADS] = dstep.astype(bf16)
    dstep_ref[pl.ds(length, PAD), :HEADS] = jnp.broadcast_to(most * 1.01, (PAD, HEADS)).astype(bf16)
    small_ref[...] = jnp.zeros_like(small_ref)
    small_ref[0:1, :] = times
    small_ref[1:2, :] = decays


def step_back(rest, pars, first, second):
    length = first[0].shape[1]
    arrays = [part for both in zip(first, second) for part in both]
    shapes = (
        jax.ShapeDtypeStruct((length + PAD, 128), bf16),
        jax.ShapeDtypeStruct((8, HEADS), f32),
    )
    return pl.pallas_call(
        step_kernel,
        grid=(1,),
        in_specs=[steps_of(rest), whole(pars)] + [whole(array) for array in arrays],
        out_specs=tuple(whole(shape) for shape in shapes),
        out_shape=shapes,
        compiler_params=params(),
        cost_estimate=pl.CostEstimate(flops=10**7, bytes_accessed=10**7, transcendentals=10**5),
        name="step_back",
    )(rest, pars, *arrays)


def unconv_kernel(mixed, x_ref, tap_ref, match_ref, dv_ref, dkq_ref, dx_ref, edge_ref, dtap_ref, *held):
    length = match_ref.shape[1]
    count = length // Q
    wide = pl.program_id(0) < mixed
    for buf in held:
        buf[0:HALO, :] = jnp.zeros((HALO, TILE), f32)
        buf[HALO + length :, :] = jnp.zeros((HALO, TILE), f32)
    for j in range(TILE // 128):
        cols = slice(128 * j, 128 * (j + 1))
        sums = [jnp.zeros((1, 128), f32) for _ in range(KW + 1)]
        for c in range(count):
            rows = slice(c * Q, (c + 1) * Q)
            s = conv_sum(x_ref, tap_ref, match_ref, c * Q, Q, cols)
            sig = sigmoid(s)
            dm = jnp.where(wide, dv_ref[rows, cols], dkq_ref[rows, cols])
            ds = dm * (sig * (1.0 + s * (1.0 - sig)))
            sums[KW] = sums[KW] + jnp.sum(ds, axis=0, keepdims=True)
            for k in range(KW):
                e = ds if k == KW - 1 else ds * match_ref[k, rows, :]
                held[k][HALO + c * Q : HALO + (c + 1) * Q, cols] = e
                taken = x_ref[pl.ds(HALO - (KW - 1) + k + c * Q, Q), cols]
                sums[k] = sums[k] + jnp.sum(e * taken, axis=0, keepdims=True)
        for k in range(KW + 1):
            dtap_ref[k : k + 1, cols] = sums[k]

        def placed(start, rows):
            total = None
            for k in range(KW):
                term = tap_ref[k : k + 1, cols] * held[k][pl.ds(start + KW - 1 - k, rows), cols]
                total = term if total is None else total + term
            return total

        edge_ref[0:HALO, cols] = placed(0, HALO)
        most = jnp.zeros((1, 128), f32)
        for c in range(count):
            dx = placed(HALO + c * Q, Q)
            most = jnp.maximum(most, jnp.max(jnp.abs(dx), axis=0, keepdims=True))
            dx_ref[c * Q : (c + 1) * Q, cols] = dx.astype(bf16)
            if c == count - 1:
                edge_ref[HALO:, cols] = dx[Q - HALO :, :]
        dtap_ref[KW + 1 : KW + 2, cols] = most
    dtap_ref[KW + 2 :, :] = jnp.zeros((8 - KW - 2, TILE), f32)


def unconv(first, rest, taps, match, dv, dkq):
    length = match.shape[1]
    high = length + HALO
    mixed = dv.shape[1] // TILE
    tiles = mixed if dkq is None else mixed + 1
    lone = dv if dkq is None else dkq
    return pl.pallas_call(
        functools.partial(unconv_kernel, mixed),
        grid=(tiles,),
        in_specs=[
            pl.BlockSpec((high, TILE), lambda j: (0, j + first)),
            pl.BlockSpec((8, TILE), lambda j: (0, j + first)),
            pl.BlockSpec((KW - 1, length, 128), lambda j: (0, 0, 0)),
            pl.BlockSpec((length, TILE), lambda j: (0, jnp.minimum(j, mixed - 1))),
            pl.BlockSpec((length, TILE), lambda j: (0, 0)),
        ],
        out_specs=(
            pl.BlockSpec((length, TILE), lambda j: (0, j)),
            pl.BlockSpec((2 * HALO, TILE), lambda j: (0, j)),
            pl.BlockSpec((8, TILE), lambda j: (0, j)),
        ),
        out_shape=(
            jax.ShapeDtypeStruct((length + PAD, tiles * TILE), bf16),
            jax.ShapeDtypeStruct((2 * HALO, tiles * TILE), f32),
            jax.ShapeDtypeStruct((8, tiles * TILE), f32),
        ),
        scratch_shapes=[pltpu.VMEM((length + 2 * HALO, TILE), f32) for _ in range(KW)],
        compiler_params=params(),
        cost_estimate=pl.CostEstimate(flops=10**8, bytes_accessed=10**7, transcendentals=10**6),
    )(rest, taps, match, dv, lone)


def adamw(param, grad, moment, square, rate, shrink):
    moment_new = beta_one * moment + (1.0 - beta_one) * grad
    square_new = beta_two * square + (1.0 - beta_two) * grad * grad
    first_corr = 1.0 - beta_one**ADAM_STEP
    second_corr = 1.0 - beta_two**ADAM_STEP
    update = moment_new / first_corr / (jnp.sqrt(square_new / second_corr) + adam_eps)
    return (param - rate * (update + shrink * param), moment_new, square_new)


def shifted(value, axis, by):
    count = lax.axis_size(axis)
    pairs = [(i, i + by) for i in range(count) if 0 <= i + by < count]
    return lax.ppermute(value, axis, pairs)


TOKENS = (((0,), (0,)), ((), ()))


def gathered(value):
    return lax.all_gather(value, "dp", axis=0, tiled=True)


def shard_gathered(value, *earlier):
    count, here = lax.axis_size("shard"), lax.axis_index("shard")
    rows, width = value.shape
    parts = [exchanged(value, "shard", k) for k in range(1, count)]
    held = jnp.zeros((count * rows, width), value.dtype)
    for k, part in enumerate([value] + parts):
        held = lax.dynamic_update_slice(held, after(part, earlier) if k else part, ((here ^ k) * rows, 0))
    return held


def exchanged(value, axis, by):
    return lax.ppermute(value, axis, [(i, i ^ by) for i in range(lax.axis_size(axis))])


def relative(value, block, core):
    base = lax.axis_index("dp") // 2
    length = value.shape[0]
    return [
        lax.dynamic_slice(value, (0, (((j ^ base) * 2) + core) * block), (length, block))
        for j in range(lax.axis_size("dp") // 2)
    ]


def both_cores(value):
    return jnp.concatenate([value, exchanged(value, "dp", 1)], axis=0)


def own_and_partner(value, block):
    core = lax.axis_index("dp") % 2
    return relative(value, block, core), relative(value, block, 1 - core)


def exponent(bound):
    return jnp.ceil(jnp.log2(jnp.maximum(bound, 1e-30)))


def coded(total, power, rows):
    scaled = total * jnp.exp2(15.0 - power)
    if total.shape[0] > rows:
        scaled = jnp.where(iota(total.shape, 0) < rows, scaled, power)
    return scaled.astype(jnp.float16)


def decoded(payload, power, rows):
    if payload.shape[0] == rows:
        return payload.astype(f32) * jnp.exp2(power - 15.0), power
    other = payload[rows : rows + 1].astype(f32)
    return payload.astype(f32) * jnp.exp2(other - 15.0), jnp.maximum(power, other) + 1.0


def after(value, *earlier):
    return lax.optimization_barrier((value, earlier))[0]


def split_plan(order):
    kept, sends = [0], []
    for bit in reversed(order):
        send = [j ^ (1 << bit) for j in kept]
        sends.insert(0, send)
        kept = kept + send
    return kept, sends


def columns_of(blocks, order, pad):
    kept, sends = split_plan(order)
    zeros = [jnp.zeros((blocks[0].shape[0], pad), bf16)] if pad else []
    return (
        jnp.concatenate([blocks[j] for j in kept[: len(sends[0])]] + zeros, axis=1),
        jnp.concatenate([blocks[j] for j in sends[0]] + zeros, axis=1),
    )


class Sum:
    def __init__(self, held, sent, rhs, power, order, pad):
        self.held, self.sent, self.rhs = held, sent, rhs
        self.power = power
        self.order = order
        self.pad = pad
        self.rows = 2 * (sent.shape[1] - pad)
        self.total = None
        self.at = 0

    def prepare(self):
        self.rows //= 2
        if self.total is None:
            part = lax.dot_general(self.sent, self.rhs, TOKENS, preferred_element_type=f32)
        else:
            part = self.total[self.rows : 2 * self.rows + self.pad]
        self.payload = coded(part, self.power, self.rows)

    def send(self):
        self.got = exchanged(self.payload, "dp", 2 << self.order[self.at])
        self.at += 1
        if self.total is None:
            self.total = lax.dot_general(self.held, self.rhs, TOKENS, preferred_element_type=f32)

    def take(self, *earlier):
        got, self.power = decoded(after(self.got, earlier), self.power, self.rows)
        self.total = self.total[: self.rows + self.pad] + got

    def more(self):
        return self.at < len(self.order)

    def finish(self):
        while self.more():
            self.prepare()
            self.send()
            self.take()


class ShardSum:
    def __init__(self, sums):
        count, here = lax.axis_size("shard"), lax.axis_index("shard")
        self.rows = sums[0].rows // count
        self.total = jnp.concatenate([one.total for one in sums], axis=1) if len(sums) > 1 else sums[0].total
        self.power = jnp.concatenate([one.power for one in sums], axis=1) if len(sums) > 1 else sums[0].power
        taken = (self.rows + sums[0].pad, self.total.shape[1])
        self.payloads = [
            coded(lax.dynamic_slice(self.total, ((here ^ k) * self.rows, 0), taken), self.power, self.rows)
            for k in range(1, count)
        ]
        self.parts = [exchanged(part, "shard", k + 1) for k, part in enumerate(self.payloads)]

    def take(self, *earlier):
        here = lax.axis_index("shard")
        result = lax.dynamic_slice(self.total, (here * self.rows, 0), (self.rows, self.total.shape[1]))
        for part in self.parts:
            result = result + decoded(after(part, earlier), self.power, self.rows)[0][: self.rows]
        return result


def summed(value):
    for axis in ("dp", "shard"):
        count = lax.axis_size(axis)
        if count & (count - 1):
            value = lax.psum(value, axis)
            continue
        by = 1
        while by < count:
            value = value + lax.ppermute(value, axis, [(i, i ^ by) for i in range(count)])
            by *= 2
    return value


def carried(state, half, factor, by):
    incoming = shifted(half, "shard", by)
    for _ in range(1, lax.axis_size("shard") - 1):
        passed = (state + factor * incoming.astype(f32)).astype(bf16)
        incoming = shifted(passed, "shard", by)
    return incoming


def both_with_most(rows):
    length = rows.shape[0] - PAD
    arrived = exchanged(rows, "dp", 1)
    most = jnp.maximum(rows[length : length + 1], arrived[length : length + 1]).astype(f32)
    return jnp.concatenate([rows[:length], arrived[:length]], axis=0), most


def mended(dx, edge, dtap, length):
    last = edge[HALO:] + shifted(edge[:HALO], "shard", -1)
    most = jnp.maximum(dtap[KW + 1 : KW + 2], jnp.max(jnp.abs(last), axis=0, keepdims=True)) * 1.01
    tail = jnp.concatenate([last, jnp.broadcast_to(most, (PAD, most.shape[1]))], axis=0).astype(bf16)
    return lax.dynamic_update_slice(dx, tail, (length - HALO, 0)), dtap


def rest_sums(both, bound, in_columns, orders):
    middle = both.shape[1] // 256 * 128
    power = exponent(bound)
    return [
        Sum(*in_columns[0], both[:, :middle], power[:, :middle], orders[0], PAD),
        Sum(*in_columns[1], both[:, middle:], power[:, middle:], orders[1], PAD),
    ]


def shards(
    hidden_in, cotangent, segment_ids,
    param_prenorm, param_inputs, param_kernel, param_offsets, param_timestep, param_decays,
    param_direct, param_gating, param_outputs,
    moment_prenorm, moment_inputs, moment_kernel, moment_offsets, moment_timestep, moment_decays,
    moment_direct, moment_gating, moment_outputs,
    square_prenorm, square_inputs, square_kernel, square_offsets, square_timestep, square_decays,
    square_direct, square_gating, square_outputs,
):
    length, width = hidden_in.shape
    own_inputs = param_inputs.astype(bf16)
    spare = -(param_inputs.shape[1] - DI) % 128
    upstream = cotangent.astype(bf16)
    own_rows = param_inputs.shape[0]
    most = jnp.broadcast_to((jnp.max(jnp.abs(cotangent)) * 1.01).astype(bf16), (own_rows, 1))
    rest_rows = shard_gathered(
        jnp.concatenate([own_inputs[:, DI:], most, jnp.zeros((own_rows, spare - 1), bf16)], axis=1),
    )
    rest_w = gathered(rest_rows)

    seg = segment_ids.astype(f32)
    ends = jnp.pad(seg[length - HALO :], (0, width - HALO))[None, :]
    halo = shifted(
        jnp.concatenate([hidden_in[length - HALO :], jnp.broadcast_to(ends, (HALO, width))], axis=0),
        "shard", 1,
    )
    rim_seg = jnp.where(lax.axis_index("shard") == 0, -1.0, halo[HALO, :HALO])
    rim = rim_seg[HALO - 1]
    all_segs = jnp.concatenate([rim_seg, seg])
    match = jnp.stack(
        [
            (all_segs[HALO - (KW - 1) + k : HALO - (KW - 1) + k + length] == seg).astype(f32)
            for k in range(KW - 1)
        ]
    )
    match = jnp.broadcast_to(match[:, :, None], (KW - 1, length, 128))
    chunks = seg.reshape(-1, Q)
    before = jnp.concatenate([rim[None], chunks[:-1, Q - 1]])
    mask = jnp.stack(
        [
            (chunks == before[:, None]).reshape(-1),
            (chunks == chunks[:, Q - 1 :]).reshape(-1),
            seg == rim,
            seg == seg[length - 1],
        ]
        + [seg < -1.0] * 4,
        axis=1,
    ).astype(f32)
    segc = jnp.broadcast_to(seg[:, None], (length, 8))
    segr = jnp.broadcast_to(seg[None, :], (8, length))

    taps = jnp.concatenate([param_kernel, param_offsets[None, :], jnp.zeros((8 - KW - 1, CH), f32)], axis=0)
    pars = jnp.concatenate([param_timestep[None, :], param_decays[None, :], jnp.zeros((6, HEADS), f32)], axis=0)
    dirx = jnp.broadcast_to(jnp.repeat(param_direct, HEAD_DIM)[None, :], (8, DI))
    gam = jnp.broadcast_to(param_gating[None, :], (8, DI))

    hidden = jnp.concatenate([halo[:HALO], hidden_in], axis=0)
    inv = lax.rsqrt(jnp.mean(hidden * hidden, axis=1, keepdims=True) + norm_eps)
    normed = (hidden * inv * param_prenorm).astype(bf16)
    own_normed = normed[HALO:]

    groups = lax.axis_size("shard")
    spots = [bit for bit in range(20) if (2 << bit) < lax.axis_size("dp")]
    orders = (spots, spots[::-1])
    in_block, out_block = groups * param_inputs.shape[0], groups * param_outputs.shape[0]
    up_both = both_cores(after(upstream, rest_rows))
    own_blocks, partner_blocks = own_and_partner(own_normed, in_block)
    arrived = exchanged(jnp.concatenate(partner_blocks, axis=1), "dp", 1)
    both_blocks = [
        jnp.concatenate([one, arrived[:, j * in_block : (j + 1) * in_block]], axis=0)
        for j, one in enumerate(own_blocks)
    ]
    in_columns = [columns_of(both_blocks, order, PAD) for order in orders]
    norm_bound = 2.02 * length * width**0.5 * jnp.max(jnp.abs(param_prenorm))
    early = (match, mask, segc, segr, taps, pars, dirx, gam, up_both, norm_bound, in_columns, normed)
    gate_rows = shard_gathered(after(own_inputs[:, :DI], rest_rows), early)
    gate_w = gathered(gate_rows)
    rest_w = after(rest_w, early)

    rest = jnp.dot(normed, rest_w, preferred_element_type=f32)
    delta, cum, cumt, tailc, taild, infd, keep, factor = prep(rest, pars, mask)
    v, kq, state, state_half = conv_state(rest, taps, match, taild)
    out_rows = shard_gathered(after(param_outputs.astype(bf16), gate_rows), v)
    out_w = gathered(out_rows)
    state = after(state, out_rows)
    incoming = carried(state, state_half, factor[0:1], 1)
    y = local_out(v, kq, delta, cum, cumt, mask, keep, segc, segr)
    gate_w = after(gate_w, y)
    z = jnp.dot(own_normed, gate_w, preferred_element_type=f32)
    out_w = after(out_w, z)
    back_gated = lax.dot_general(upstream, out_w, NT, preferred_element_type=f32)
    tokens = length * lax.axis_size("dp") * groups
    cotangent_most = jnp.max(rest_w[:, param_inputs.shape[1] - DI]).astype(f32)
    out_power = exponent(1.02 * tokens * DI**0.5 * jnp.max(jnp.abs(param_gating)) * cotangent_most)
    place = lax.axis_index("dp")
    block = out_block if out_block % 128 == 0 and len(spots) == 2 else 0
    at = jnp.stack([place // 2, place % 2]).astype(jnp.int32)
    gated, blocks, dy, dz, dinc, dinc_half, small = gate(
        block, at, y, v, z, back_gated, kq, incoming, infd, dirx, gam
    )

    outgoing = carried(dinc, dinc_half, factor[0:1], -1)
    if not block:
        own_blocks, partner_blocks = own_and_partner(gated, out_block)
        blocks = jnp.stack([*columns_of(own_blocks, spots, 0), *columns_of(partner_blocks, spots, 0)])
    arrived = exchanged(blocks[2:], "dp", 1)
    out_columns = [jnp.concatenate([blocks[i], arrived[i]], axis=0) for i in range(2)]
    dz_most = jnp.broadcast_to(small[2:3] * 1.01, (PAD, DI)).astype(bf16)
    dz = lax.dynamic_update_slice(dz, dz_most, (length, 0))
    dz_both, dz_bound = both_with_most(dz)
    block_out = hidden_in + jnp.dot(gated, out_w, preferred_element_type=f32)
    out_sum = Sum(*out_columns, up_both, out_power, spots, 0)
    gate_sum = Sum(*in_columns[1], dz_both, exponent(norm_bound * dz_bound), spots[::-1], PAD)
    first_sums = [out_sum, gate_sum]
    for one in first_sums:
        one.prepare()
        one.send()
    back_normed = lax.dot_general(dz, gate_w, NT, preferred_element_type=f32)
    outgoing = after(
        outgoing, out_sum.payload, gate_sum.payload, out_sum.total, gate_sum.total, back_normed, block_out
    )

    ssm = (kq, delta, cum, cumt, tailc, mask, keep, incoming)
    half = NG // 2
    dv1, *held1 = back_local(0, half, None, v, dy, *ssm, outgoing, dirx, segc, segr)
    for one in first_sums:
        one.take(dv1)
        if one.more():
            one.prepare()
            one.send()
    dv1 = after(dv1, *[one.payload for one in first_sums])
    drest1, dtap1 = mended(*unconv(0, rest, taps, match, dv1, None), length)
    both1, bound1 = both_with_most(drest1)
    sums1 = rest_sums(both1, norm_bound * bound1, in_columns, orders)
    for one in first_sums:
        one.take(dv1, both1)
        one.finish()
    shard_out, shard_gate = ShardSum([out_sum]), ShardSum([gate_sum])
    for one in sums1:
        one.prepare()
        one.send()
    dy = after(
        dy, [one.payload for one in sums1], [one.total for one in sums1], shard_out.payloads, shard_gate.payloads
    )
    dv2, *held2 = back_local(half, NG, held1[:2], v, dy, *ssm, outgoing, dirx, segc, segr)
    for one in sums1:
        one.take(dv2)
        if one.more():
            one.prepare()
            one.send()
    dv2 = after(dv2, *[one.payload for one in sums1])
    dstep, small_step = step_back(rest, pars, held1[2:], held2[2:])
    drest2, dtap2 = mended(*unconv(dv1.shape[1] // TILE, rest, taps, match, dv2, held2[0]), length)
    drest2 = jnp.concatenate([drest2, dstep], axis=1)
    both2, bound2 = both_with_most(drest2)
    sums2 = rest_sums(both2, norm_bound * bound2, in_columns, orders)
    for one in sums2:
        one.prepare()
        one.send()
    for one in sums1:
        one.take(dv2, dstep)
        one.finish()
    shard1 = ShardSum(sums1)
    drest1, drest2 = after((drest1, drest2), shard1.payloads, [two.payload for two in sums2])
    wide1 = drest1.shape[1]
    back_normed = back_normed + lax.dot_general(drest1, rest_w[:, :wide1], NT, preferred_element_type=f32)
    back_normed = back_normed + lax.dot_general(drest2, rest_w[:, wide1:], NT, preferred_element_type=f32)
    back_normed = back_normed[:length]
    for one in sums2:
        one.take(back_normed)
        if one.more():
            one.prepare()
            one.send()
    sent = [one.payload for one in sums2]
    grad_outputs = shard_out.take(sent)
    grad_gate = shard_gate.take(sent)
    for one in sums2:
        one.take()
        one.finish()
    shard2 = ShardSum(sums2)
    grad_rest = jnp.concatenate([shard1.take(sent), shard2.take()], axis=1)
    grad_inputs = jnp.concatenate([grad_gate, grad_rest[:, : param_inputs.shape[1] - DI]], axis=1)
    dtap = jnp.concatenate([dtap1, dtap2], axis=1)

    own_inv = inv[HALO:]
    scaled = hidden_in * own_inv
    gained = back_normed * param_prenorm
    hidden_grad = cotangent + own_inv * (
        gained - scaled * jnp.mean(gained * scaled, axis=1, keepdims=True)
    )
    grad_prenorm = jnp.sum(back_normed * scaled, axis=0)

    pieces = [
        grad_prenorm,
        dtap[:KW].reshape(-1),
        dtap[KW],
        small_step[0],
        small_step[1],
        jnp.sum(small[1].reshape(HEADS, HEAD_DIM), axis=1),
        small[0],
    ]
    flat = after(jnp.concatenate(pieces), sent)
    count = flat.shape[0]
    lines = -(-count // 1024) * 8
    total = summed(jnp.pad(flat, (0, lines * 128 - count)).reshape(lines, 128)).reshape(-1)
    found, at = [], 0
    for piece in pieces:
        found.append(total[at : at + piece.shape[0]])
        at += piece.shape[0]
    grad_prenorm, grad_kernel, grad_offsets, grad_timestep, grad_decays, grad_direct, grad_gating = found
    grad_kernel = grad_kernel.reshape(KW, CH)

    params = (
        param_prenorm, param_inputs, param_kernel, param_offsets, param_timestep, param_decays,
        param_direct, param_gating, param_outputs,
    )
    moments = (
        moment_prenorm, moment_inputs, moment_kernel, moment_offsets, moment_timestep, moment_decays,
        moment_direct, moment_gating, moment_outputs,
    )
    squares = (
        square_prenorm, square_inputs, square_kernel, square_offsets, square_timestep, square_decays,
        square_direct, square_gating, square_outputs,
    )
    grads = (
        grad_prenorm, grad_inputs, grad_kernel, grad_offsets, grad_timestep, grad_decays,
        grad_direct, grad_gating, grad_outputs,
    )
    updated = [
        adamw(params[i], grads[i], moments[i], squares[i], rate_table[i], shrink_table[i])
        for i in range(9)
    ]
    return (
        (block_out, hidden_grad)
        + grads
        + tuple(u[0] for u in updated)
        + tuple(u[1] for u in updated)
        + tuple(u[2] for u in updated)
    )


def solution(mesh):
    rows = P(("dp", "shard"), None)
    member = (P(), rows, P(), P(), P(), P(), P(), P(), rows)

    return jax.shard_map(
        shards,
        mesh=mesh,
        in_specs=(rows, rows, P(("dp", "shard"))) + member * 3,
        out_specs=(rows, rows) + member * 4,
        check_vma=False,
    )
```

```python
import functools

import jax
import jax.numpy as jnp
from jax import lax
from jax.experimental import pallas as pl
from jax.experimental.pallas import tpu as pltpu
from jax.sharding import PartitionSpec as P


HEADS = 48
HEAD_DIM = 64
STATE = 128
KW = 4
ADAM_STEP = 10
DI = 3072
CH = 3328

Q = 128
GH = 8
GW = GH * HEAD_DIM
NG = HEADS // GH
HALO = 8
PAD = 16
TILE = 256

bf16 = jnp.bfloat16
f32 = jnp.float32
highest = lax.Precision.HIGHEST

norm_eps = 1e-05
beta_one = 0.9
beta_two = 0.95
adam_eps = 1e-08
rate_table = (0.2, 0.01, 0.2, 0.2, 0.2, 0.2, 0.2, 0.2, 0.01)
shrink_table = (0.0, 0.1, 0.1, 0.0, 0.0, 0.0, 0.0, 0.0, 0.1)

NN = (((1,), (0,)), ((), ()))
NT = (((1,), (1,)), ((), ()))


def halves(x):
    hi = x.astype(bf16)
    return hi, (x - hi.astype(f32)).astype(bf16)


def dot1(a, b, dims=NN):
    return lax.dot_general(a.astype(bf16), b.astype(bf16), dims, preferred_element_type=f32)


def dot3(a, b, dims=NN):
    ah, al = halves(a)
    bh, bl = halves(b)
    return dot1(ah, bh, dims) + (dot1(ah, bl, dims) + dot1(al, bh, dims))


def dot_halves(a, b, dims=NN):
    return dot1(a[0], b[0], dims) + (dot1(a[0], b[1], dims) + dot1(a[1], b[0], dims))


def dotf(a, b, dims=NN):
    return lax.dot_general(a, b, dims, precision=highest, preferred_element_type=f32)


def iota(shape, dim):
    return lax.broadcasted_iota(jnp.int32, shape, dim)


def sigmoid(x):
    return 0.5 * jnp.tanh(0.5 * x) + 0.5


def softplus(x):
    u = jnp.exp(-jnp.abs(x))
    series = u * (1.0 - u * (0.5 - u * (1.0 / 3.0 - u * (0.25 - u * 0.2))))
    return jnp.maximum(x, 0.0) + jnp.where(u < 0.03, series, jnp.log(1.0 + u))


def pair_lanes(cols, j):
    rows = cols.shape[0]
    low = iota((rows, 128), 1) < HEAD_DIM
    return jnp.where(low, cols[:, 2 * j : 2 * j + 1], cols[:, 2 * j + 1 : 2 * j + 2])


def group_lanes(cols):
    return jnp.concatenate([pair_lanes(cols, j) for j in range(cols.shape[1] // 2)], axis=1)


def head_onehot():
    return (iota((HEADS, DI), 1) // HEAD_DIM == iota((HEADS, DI), 0)).astype(f32)


def params(limit=60000, **kw):
    return pltpu.CompilerParams(vmem_limit_bytes=limit * 1024, **kw)


def prep_kernel(
    step_ref, par_ref, mask_ref, delta_ref, cum_ref, cumt_ref, tailc_ref,
    taild_ref, infd_ref, keep_ref, factor_ref,
):
    length = mask_ref.shape[0]
    count = length // Q
    tri = (iota((Q, Q), 0) >= iota((Q, Q), 1)).astype(f32)
    eye = (iota((HEADS, HEADS), 0) == iota((HEADS, HEADS), 1)).astype(f32)
    rate = jnp.exp(par_ref[1:2, :])
    base = jnp.zeros((1, HEADS), f32)
    held = []
    keeps = []
    for c in range(count):
        rows = slice(c * Q, (c + 1) * Q)
        delta = softplus(step_ref[pl.ds(HALO + c * Q, Q), :HEADS] + par_ref[0:1, :])
        cum = dotf(tri, -delta * rate)
        cumt_ref[:, rows] = dotf(eye, cum, NT)
        last = cum[Q - 1 : Q, :]
        tailc = jnp.exp(last - cum) * mask_ref[rows, 1:2] * delta
        for g in range(NG):
            part = slice(g * GH, (g + 1) * GH)
            delta_ref[g, rows, :] = delta[:, part]
            cum_ref[g, rows, :] = cum[:, part]
            tailc_ref[g, rows, :] = tailc[:, part]
        keeps.append(jnp.exp(last) * mask_ref[(c + 1) * Q - 1 : (c + 1) * Q, 0:1])
        whole = cum + base
        infd_ref[rows, :] = jnp.exp(whole) * mask_ref[rows, 2:3]
        held.append((whole, delta))
        base = base + last
    for c in range(count):
        rows = slice(c * Q, (c + 1) * Q)
        whole, delta = held[c]
        taild = jnp.exp(base - whole) * mask_ref[rows, 3:4] * delta
        for g in range(NG):
            taild_ref[g, rows, :] = taild[:, g * GH : (g + 1) * GH]
    factor = jnp.exp(base) * mask_ref[length - 1 : length, 2:3]
    spread = head_onehot()
    line = iota((8, HEADS), 0)
    table = jnp.zeros((8, HEADS), f32)
    for c in range(count):
        table = jnp.where(line == c, keeps[c], table)
    keep_ref[...] = dotf(table, spread)
    factor_ref[...] = dotf(jnp.where(line == 0, factor, 0.0), spread)


def whole(array):
    return pl.BlockSpec(array.shape, lambda i: (0,) * array.ndim)


def steps_of(rest):
    return pl.BlockSpec((rest.shape[0], 128), lambda i: (0, CH // 128))


def prep(rest, pars, mask):
    length = mask.shape[0]
    cols = jax.ShapeDtypeStruct((NG, length, GH), f32)
    wide = jax.ShapeDtypeStruct((8, DI), f32)
    shapes = (
        cols, cols, jax.ShapeDtypeStruct((HEADS, length), f32), cols, cols,
        jax.ShapeDtypeStruct((length, HEADS), f32), wide, wide,
    )
    return pl.pallas_call(
        prep_kernel,
        grid=(1,),
        in_specs=[steps_of(rest), whole(pars), whole(mask)],
        out_specs=tuple(whole(shape) for shape in shapes),
        out_shape=shapes,
        compiler_params=params(),
        cost_estimate=pl.CostEstimate(flops=10**7, bytes_accessed=10**7, transcendentals=10**5),
        name="prep",
    )(rest, pars, mask)


def conv_sum(x_ref, tap_ref, match_ref, start, rows, cols):
    total = tap_ref[KW : KW + 1, cols] + tap_ref[KW - 1 : KW, cols] * x_ref[
        pl.ds(HALO + start, rows), cols
    ]
    for k in range(KW - 1):
        taken = x_ref[pl.ds(HALO - (KW - 1) + k + start, rows), cols]
        total = total + tap_ref[k : k + 1, cols] * (taken * match_ref[k, pl.ds(start, rows), :])
    return total


def conv_kernel(
    xv_ref, xk_ref, tv_ref, tk_ref, match_ref, taild_ref, v_ref, kq_ref, state_ref, state_half_ref, kt_hi, kt_lo
):
    length = v_ref.shape[0]
    count = length // Q

    @pl.when(pl.program_id(0) == 0)
    def _():
        for c in range(count):
            for j in range(2):
                cols = slice(128 * j, 128 * (j + 1))
                s = conv_sum(xk_ref, tk_ref, match_ref, c * Q, Q, cols)
                m = s * sigmoid(s)
                kq_ref[c * Q : (c + 1) * Q, cols] = m
                if j == 0:
                    hi, lo = halves(m.T)
                    kt_hi[:, c * Q : (c + 1) * Q] = hi
                    kt_lo[:, c * Q : (c + 1) * Q] = lo

    total = jnp.zeros((STATE, GW), f32)
    for c in range(count):
        rows = slice(c * Q, (c + 1) * Q)
        tail = taild_ref[0, rows, :]
        parts = []
        for j in range(GW // 128):
            cols = slice(128 * j, 128 * (j + 1))
            s = conv_sum(xv_ref, tv_ref, match_ref, c * Q, Q, cols)
            m = s * sigmoid(s)
            v_ref[rows, cols] = m
            parts.append(m * pair_lanes(tail, j))
        hi, lo = halves(jnp.concatenate(parts, axis=1))
        kh, kl = kt_hi[:, rows], kt_lo[:, rows]
        total = total + (dot1(kh, hi) + (dot1(kh, lo) + dot1(kl, hi)))
    state_ref[...] = total
    state_half_ref[...] = total.astype(bf16)


def conv_state(rest, taps, match, taild):
    length = match.shape[1]
    high = length + HALO
    kq_at = DI // (2 * STATE)
    return pl.pallas_call(
        conv_kernel,
        grid=(NG,),
        in_specs=[
            pl.BlockSpec((high, GW), lambda g: (0, g)),
            pl.BlockSpec((high, 2 * STATE), lambda g: (0, kq_at)),
            pl.BlockSpec((8, GW), lambda g: (0, g)),
            pl.BlockSpec((8, 2 * STATE), lambda g: (0, kq_at)),
            pl.BlockSpec((KW - 1, length, 128), lambda g: (0, 0, 0)),
            pl.BlockSpec((1, length, GH), lambda g: (g, 0, 0)),
        ],
        out_specs=(
            pl.BlockSpec((length, GW), lambda g: (0, g)),
            pl.BlockSpec((length, 2 * STATE), lambda g: (0, 0)),
            pl.BlockSpec((STATE, GW), lambda g: (0, g)),
            pl.BlockSpec((STATE, GW), lambda g: (0, g)),
        ),
        out_shape=(
            jax.ShapeDtypeStruct((length, DI), f32),
            jax.ShapeDtypeStruct((length, 2 * STATE), f32),
            jax.ShapeDtypeStruct((STATE, DI), f32),
            jax.ShapeDtypeStruct((STATE, DI), bf16),
        ),
        scratch_shapes=[pltpu.VMEM((STATE, length), bf16), pltpu.VMEM((STATE, length), bf16)],
        compiler_params=params(),
        cost_estimate=pl.CostEstimate(flops=2 * 10**9, bytes_accessed=2 * 10**7, transcendentals=2 * 10**6),
        name="conv_state",
    )(rest, rest, taps, taps, match, taild)


def masks_of(segc_ref, segr_ref, rows):
    same = segc_ref[rows, 0:1] == segr_ref[0:1, rows]
    later = iota((Q, Q), 0) >= iota((Q, Q), 1)
    earlier = iota((Q, Q), 0) <= iota((Q, Q), 1)
    return jnp.where(same & later, 0.0, -1e30), jnp.where(same & earlier, 0.0, -1e30)


def local_kernel(
    v_ref, kq_ref, delta_ref, cum_ref, cumt_ref, mask_ref, keep_ref, segc_ref, segr_ref,
    y_ref, gram, bias, kt_hi, kt_lo,
):
    length = v_ref.shape[0]
    count = length // Q

    @pl.when(pl.program_id(0) == 0)
    def _():
        for c in range(count):
            rows = slice(c * Q, (c + 1) * Q)
            k, q = kq_ref[rows, :STATE], kq_ref[rows, STATE:]
            bias[rows, :] = masks_of(segc_ref, segr_ref, rows)[0]
            gram[rows, :] = dot3(q, k, NT)
            kt_hi[:, rows], kt_lo[:, rows] = halves(k.T)

    low = iota((Q, 128), 1) < HEAD_DIM
    state = None
    for c in range(count):
        rows = slice(c * Q, (c + 1) * Q)
        delta, cum = delta_ref[0, rows, :], cum_ref[0, rows, :]
        alive = jnp.broadcast_to(mask_ref[rows, 0:1], (Q, 128))
        ending = jnp.broadcast_to(mask_ref[rows, 1:2], (Q, 128))
        if c:
            carried = dot3(kq_ref[rows, STATE:], state)
        tails = []
        for j in range(GW // 128):
            cols = slice(128 * j, 128 * (j + 1))
            w = v_ref[rows, cols] * pair_lanes(delta, j)
            run = pair_lanes(cum, j)
            both = []
            for i in (2 * j, 2 * j + 1):
                fade = jnp.exp(cum[:, i : i + 1] - cumt_ref[i : i + 1, rows] + bias[rows, :])
                both.append(halves(gram[rows, :] * fade))
            parts = halves(w)
            zero = jnp.zeros_like(parts[0])
            stacked = tuple(
                jnp.concatenate([jnp.where(low, part, zero), jnp.where(low, zero, part)], axis=0)
                for part in parts
            )
            y = dot_halves(tuple(jnp.concatenate([both[0][i], both[1][i]], axis=1) for i in (0, 1)), stacked)
            if c:
                y = y + carried[:, cols] * (jnp.exp(run) * alive)
            y_ref[rows, cols] = y
            if c < count - 1:
                tails.append(halves(w * (jnp.exp(run[Q - 1 : Q, :] - run) * ending)))
        if c < count - 1:
            fresh = dot_halves(
                (kt_hi[:, rows], kt_lo[:, rows]),
                tuple(jnp.concatenate([part[i] for part in tails], axis=1) for i in (0, 1)),
            )
            state = fresh if state is None else state * keep_ref[c : c + 1, :] + fresh


def local_out(v, kq, delta, cum, cumt, mask, keep, segc, segr):
    length = v.shape[0]
    cols = pl.BlockSpec((1, length, GH), lambda g: (g, 0, 0))
    return pl.pallas_call(
        local_kernel,
        grid=(NG,),
        in_specs=[
            pl.BlockSpec((length, GW), lambda g: (0, g)),
            pl.BlockSpec((length, 2 * STATE), lambda g: (0, 0)),
            cols, cols,
            pl.BlockSpec((GH, length), lambda g: (g, 0)),
            pl.BlockSpec((length, 8), lambda g: (0, 0)),
            pl.BlockSpec((8, GW), lambda g: (0, g)),
            pl.BlockSpec((length, 8), lambda g: (0, 0)),
            pl.BlockSpec((8, length), lambda g: (0, 0)),
        ],
        out_specs=pl.BlockSpec((length, GW), lambda g: (0, g)),
        out_shape=jax.ShapeDtypeStruct((length, DI), f32),
        scratch_shapes=[
            pltpu.VMEM((length, Q), f32), pltpu.VMEM((length, Q), f32),
            pltpu.VMEM((STATE, length), bf16), pltpu.VMEM((STATE, length), bf16),
        ],
        compiler_params=params(),
        cost_estimate=pl.CostEstimate(flops=2 * 10**9, bytes_accessed=2 * 10**7, transcendentals=4 * 10**6),
        name="local_out",
    )(v, kq, delta, cum, cumt, mask, keep, segc, segr)


def gate_kernel(
    block, at_ref, y_ref, v_ref, z_ref, g_ref, kq_ref, inc_ref, infd_ref, dir_ref, gam_ref,
    out_ref, blocks_ref, dy_ref, dz_ref, dinc_ref, dinc_half_ref, small_ref, ybuf, rbuf,
):
    first = pl.program_id(0) == 0
    rows = y_ref.shape[0]
    q = kq_ref[:, STATE:]
    inflow = infd_ref[...]
    square = jnp.zeros((rows, 128), f32)
    cross = jnp.zeros((rows, 128), f32)
    for j in range(DI // 128):
        cols = slice(128 * j, 128 * (j + 1))
        carry = dot3(q, inc_ref[:, cols]) * pair_lanes(inflow, j)
        y = y_ref[:, cols] + carry + dir_ref[0:1, cols] * v_ref[:, cols]
        z = z_ref[:, cols]
        gated = y * (z * sigmoid(z))
        ybuf[:, cols] = y
        rbuf[:, cols] = gated
        square = square + gated * gated
        cross = cross + gated * (g_ref[:, cols] * gam_ref[0:1, cols])
    inv = lax.rsqrt(jnp.sum(square, axis=1, keepdims=True) * (1.0 / DI) + norm_eps)
    slope = inv * inv * inv * (jnp.sum(cross, axis=1, keepdims=True) * (1.0 / DI))
    qt = q.T

    @pl.when(first)
    def _():
        dinc_ref[...] = jnp.zeros_like(dinc_ref)
        small_ref[...] = jnp.zeros_like(small_ref)

    for j in range(DI // 128):
        cols = slice(128 * j, 128 * (j + 1))
        gated = rbuf[:, cols]
        scaled = gated * inv
        gam = gam_ref[0:1, cols]
        half = (scaled * gam).astype(bf16)
        out_ref[:, cols] = half
        if block:
            per = block // 128
            far = ((j // per) >> 1) ^ at_ref[0]
            which = 2 * (((j // per) & 1) ^ at_ref[1]) + (far & 1)
            place = pl.multiple_of((far >> 1) * block + (j % per) * 128, 128)
            blocks_ref[which, :, pl.ds(place, 128)] = half
        g = g_ref[:, cols]
        dgated = inv * (g * gam) - gated * slope
        z = z_ref[:, cols]
        s = sigmoid(z)
        dy = dgated * (z * s)
        dy_ref[:, cols] = dy
        dz = dgated * ybuf[:, cols] * (s * (1.0 + z * (1.0 - s)))
        dz_ref[:, cols] = dz.astype(bf16)
        small_ref[2:3, cols] = jnp.maximum(
            small_ref[2:3, cols], jnp.max(jnp.abs(dz), axis=0, keepdims=True)
        )
        small_ref[0:1, cols] += jnp.sum(g * scaled, axis=0, keepdims=True)
        small_ref[1:2, cols] += jnp.sum(dy * v_ref[:, cols], axis=0, keepdims=True)
        dinc_ref[:, cols] += dot3(qt, dy * pair_lanes(inflow, j))

    @pl.when(pl.program_id(0) == pl.num_programs(0) - 1)
    def _():
        dinc_half_ref[...] = dinc_ref[...].astype(bf16)


def gate(block, at, y, v, z, g, kq, inc, infd, dirx, gam):
    length = y.shape[0]
    tile = Q
    big = pl.BlockSpec((tile, DI), lambda i, at: (i, 0))
    fixed = lambda rows: pl.BlockSpec((rows, DI), lambda i, at: (0, 0))
    spare = 2 * block if block else 128
    return pl.pallas_call(
        functools.partial(gate_kernel, block),
        grid_spec=pltpu.PrefetchScalarGridSpec(
            num_scalar_prefetch=1,
            grid=(length // tile,),
            in_specs=[
                big, big, big, big,
                pl.BlockSpec((tile, 2 * STATE), lambda i, at: (i, 0)),
                fixed(STATE),
                pl.BlockSpec((tile, HEADS), lambda i, at: (i, 0)),
                fixed(8), fixed(8),
            ],
            out_specs=(
                big, pl.BlockSpec((4, tile, spare), lambda i, at: (0, i, 0)), big, big,
                fixed(STATE), fixed(STATE), fixed(8),
            ),
            scratch_shapes=[pltpu.VMEM((tile, DI), f32), pltpu.VMEM((tile, DI), f32)],
        ),
        out_shape=(
            jax.ShapeDtypeStruct((length, DI), bf16),
            jax.ShapeDtypeStruct((4, length, spare), bf16),
            jax.ShapeDtypeStruct((length, DI), f32),
            jax.ShapeDtypeStruct((length + PAD, DI), bf16),
            jax.ShapeDtypeStruct((STATE, DI), f32),
            jax.ShapeDtypeStruct((STATE, DI), bf16),
            jax.ShapeDtypeStruct((8, DI), f32),
        ),
        compiler_params=params(),
        cost_estimate=pl.CostEstimate(flops=10**9, bytes_accessed=4 * 10**7, transcendentals=4 * 10**6),
        name="gate",
    )(at, y, v, z, g, kq, inc, infd, dirx, gam)


def back_kernel(
    final, v_ref, dy_ref, kq_ref, delta_ref, cum_ref, cumt_ref, tailc_ref, mask_ref, keep_ref,
    inc_ref, dout_ref, dir_ref, segc_ref, segr_ref, dkq_in, dgram_in,
    dv_ref, dkq_ref, dgram, ddelta_ref, dcum_ref, drow_ref, flow_ref,
    gram, gramt, bias, biast, kt_hi, kt_lo, qt_hi, qt_lo, kq_hi, kq_lo, states,
):
    length = v_ref.shape[0]
    count = length // Q
    step = pl.program_id(0)

    @pl.when(step == 0)
    def _():
        for c in range(count):
            rows = slice(c * Q, (c + 1) * Q)
            k, q = kq_ref[rows, :STATE], kq_ref[rows, STATE:]
            b, bt = masks_of(segc_ref, segr_ref, rows)
            bias[rows, :] = b
            biast[rows, :] = bt
            scores = dot3(q, k, NT)
            gram[rows, :] = scores
            gramt[rows, :] = scores.T
            kt_hi[:, rows], kt_lo[:, rows] = halves(k.T)
            qt_hi[:, rows], qt_lo[:, rows] = halves(q.T)
            kq_hi[rows, :], kq_lo[rows, :] = halves(kq_ref[rows, :])
        dgram[...] = dgram_in[...]
        dkq_ref[...] = dkq_in[...]

    low = iota((Q, 128), 1) < HEAD_DIM
    lane = iota((Q, GH), 1)
    line = iota((8, GW), 0)

    states[0] = inc_ref[...].astype(f32)
    for c in range(count):
        rows = slice(c * Q, (c + 1) * Q)
        weighted = halves(v_ref[rows, :] * group_lanes(tailc_ref[0, rows, :]))
        states[c + 1] = states[c] * keep_ref[c : c + 1, :] + dot_halves(
            (kt_hi[:, rows], kt_lo[:, rows]), weighted
        )

    back = dout_ref[...].astype(f32)
    flows = jnp.zeros((8, GW), f32)
    for c in reversed(range(count)):
        rows = slice(c * Q, (c + 1) * Q)
        flows = jnp.where(line == c, jnp.sum(back * states[c + 1], axis=0, keepdims=True), flows)
        delta, cum = delta_ref[0, rows, :], cum_ref[0, rows, :]
        before = halves(states[c])
        after = halves(back)
        k, q = (kq_hi[rows, :STATE], kq_lo[rows, :STATE]), (kq_hi[rows, STATE:], kq_lo[rows, STATE:])
        y_in = dot_halves(q, before)
        w_in = dot_halves(k, after)
        alive = jnp.broadcast_to(mask_ref[rows, 0:1], (Q, 128))
        ending = jnp.broadcast_to(mask_ref[rows, 1:2], (Q, 128))
        ddelta = jnp.zeros((Q, GH), f32)
        dcum = jnp.zeros((Q, GH), f32)
        dys, ws = [], []
        for j in range(GW // 128):
            cols = slice(128 * j, 128 * (j + 1))
            dy, v = dy_ref[rows, cols], v_ref[rows, cols]
            spread = pair_lanes(delta, j)
            w = v * spread
            dy_hi, dy_lo = halves(dy)
            zero = jnp.zeros_like(dy_hi)
            stacked = tuple(
                jnp.concatenate([jnp.where(low, part, zero), jnp.where(low, zero, part)], axis=0)
                for part in (dy_hi, dy_lo)
            )
            inner = dot_halves(stacked, halves(w), NT)
            run = jnp.where(low, cum[:, 2 * j : 2 * j + 1], cum[:, 2 * j + 1 : 2 * j + 2])
            dflow = dy * (jnp.exp(run) * alive)
            tail = jnp.exp(run[Q - 1 : Q, :] - run) * ending
            dw_in = w_in[:, cols] * tail
            one = dflow * y_in[:, cols] - w * dw_in
            turned = []
            for i in (0, 1):
                h = 2 * j + i
                col, row = cum[:, h : h + 1], cumt_ref[h : h + 1, rows]
                turned.append(halves(gramt[rows, :] * jnp.exp(row - col + biast[rows, :])))
                weighed = inner[Q * i : Q * (i + 1), :] * jnp.exp(col - row + bias[rows, :])
                dgram[rows, :] += weighed
                full = weighed * gram[rows, :]
                drow_ref[h : h + 1, rows] = jnp.sum(full, axis=0, keepdims=True)
                keep = low if i == 0 else jnp.logical_not(low)
                full = full + jnp.where(keep, one, 0.0)
                dcum_ref[0, rows, h : h + 1] = jnp.sum(full, axis=1, keepdims=True)
            dw = dot_halves(
                tuple(jnp.concatenate([turned[0][i], turned[1][i]], axis=1) for i in (0, 1)), stacked
            ) + dw_in
            dv_ref[rows, cols] = spread * dw + dir_ref[0:1, cols] * dy
            two = v * dw
            for i in (0, 1):
                keep = low if i == 0 else jnp.logical_not(low)
                h = 2 * j + i
                ddelta_ref[0, rows, h : h + 1] = jnp.sum(jnp.where(keep, two, 0.0), axis=1, keepdims=True)
            dys.append(halves(dflow))
            ws.append(halves(w * tail))
        flowing = tuple(jnp.concatenate([part[i] for part in dys], axis=1) for i in (0, 1))
        leaving = tuple(jnp.concatenate([part[i] for part in ws], axis=1) for i in (0, 1))
        dkq_ref[rows, STATE:] += dot_halves(flowing, before, NT)
        dkq_ref[rows, :STATE] += dot_halves(leaving, after, NT)
        if c:
            back = back * keep_ref[c : c + 1, :] + dot_halves((qt_hi[:, rows], qt_lo[:, rows]), flowing)
    flow_ref[...] = flows

    @pl.when(jnp.logical_and(step == pl.num_programs(0) - 1, final))
    def _():
        for c in range(count):
            rows = slice(c * Q, (c + 1) * Q)
            k, q = kq_ref[rows, :STATE], kq_ref[rows, STATE:]
            dg = dgram[rows, :]
            dkq_ref[rows, STATE:] += dot3(dg, k)
            dkq_ref[rows, :STATE] += dot3(dg.T, q)


def back_local(
    first, last, held, v, dy, kq, delta, cum, cumt, tailc, mask, keep, inc, dout, dirx, segc, segr
):
    length = v.shape[0]
    count = length // Q
    groups = last - first
    if held is None:
        held = (jnp.zeros((length, 2 * STATE), f32), jnp.zeros((length, Q), f32))
    cols = pl.BlockSpec((1, length, GH), lambda g: (g + first, 0, 0))
    wide = pl.BlockSpec((length, GW), lambda g: (0, g + first))
    state = pl.BlockSpec((STATE, GW), lambda g: (0, g + first))
    lines = pl.BlockSpec((8, GW), lambda g: (0, g + first))
    turned = pl.BlockSpec((GH, length), lambda g: (g + first, 0))
    whole = pl.BlockSpec((length, 2 * STATE), lambda g: (0, 0))
    table = pl.BlockSpec((length, Q), lambda g: (0, 0))
    square = pltpu.VMEM((length, Q), f32)
    out_cols = pl.BlockSpec((1, length, GH), lambda g: (g, 0, 0))
    return pl.pallas_call(
        functools.partial(back_kernel, last == NG),
        grid=(groups,),
        in_specs=[
            wide, wide, whole, cols, cols, turned, cols, pl.BlockSpec((length, 8), lambda g: (0, 0)), lines,
            state, state, lines,
            pl.BlockSpec((length, 8), lambda g: (0, 0)),
            pl.BlockSpec((8, length), lambda g: (0, 0)),
            whole, table,
        ],
        out_specs=(
            pl.BlockSpec((length, GW), lambda g: (0, g)), whole, table, out_cols, out_cols,
            pl.BlockSpec((GH, length), lambda g: (g, 0)),
            pl.BlockSpec((8, GW), lambda g: (0, g)),
        ),
        out_shape=(
            jax.ShapeDtypeStruct((length, groups * GW), f32),
            jax.ShapeDtypeStruct((length, 2 * STATE), f32),
            jax.ShapeDtypeStruct((length, Q), f32),
            jax.ShapeDtypeStruct((groups, length, GH), f32),
            jax.ShapeDtypeStruct((groups, length, GH), f32),
            jax.ShapeDtypeStruct((groups * GH, length), f32),
            jax.ShapeDtypeStruct((8, groups * GW), f32),
        ),
        scratch_shapes=[
            square, square, square, square,
            *[pltpu.VMEM((STATE, length), bf16) for _ in range(4)],
            *[pltpu.VMEM((length, 2 * STATE), bf16) for _ in range(2)],
            pltpu.VMEM((count + 1, STATE, GW), f32),
        ],
        compiler_params=params(),
        cost_estimate=pl.CostEstimate(
            flops=groups * 5 * 10**9, bytes_accessed=groups * 5 * 10**6, transcendentals=groups * 10**6
        ),
        name="back_first" if first == 0 else "back_second",
    )(v, dy, kq, delta, cum, cumt, tailc, mask, keep, inc, dout, dirx, segc, segr, *held)


def step_kernel(
    step_ref, par_ref, ddelta_a, ddelta_b, dcum_a, dcum_b, drow_a, drow_b, flow_a, flow_b,
    dstep_ref, small_ref,
):
    length = ddelta_a.shape[1]
    half = ddelta_a.shape[0]
    upper = (iota((Q, Q), 0) <= iota((Q, Q), 1)).astype(f32)
    eye = (iota((Q, Q), 0) == iota((Q, Q), 1)).astype(f32)
    last = iota((Q, 1), 0) == Q - 1
    rate = jnp.exp(par_ref[1:2, :])
    spread = head_onehot()
    wide = half * GW
    flows = dotf(flow_a[...], spread[:, :wide], NT) + dotf(flow_b[...], spread[:, wide:], NT)
    top = half * GH
    rise = (iota((HEADS, top), 0) == iota((HEADS, top), 1)).astype(f32)
    fall = (iota((HEADS, HEADS - top), 0) == iota((HEADS, HEADS - top), 1) + top).astype(f32)
    times = jnp.zeros((1, HEADS), f32)
    decays = jnp.zeros((1, HEADS), f32)
    most = jnp.zeros((1, HEADS), f32)
    dstep_ref[...] = jnp.zeros_like(dstep_ref)
    for c in range(length // Q):
        rows = slice(c * Q, (c + 1) * Q)
        ddelta = jnp.zeros((Q, HEADS), f32)
        turned = dotf(rise, drow_a[:, rows]) + dotf(fall, drow_b[:, rows])
        dcum = -dotf(eye, turned, NT)
        for g in range(NG):
            place = (iota((GH, HEADS), 0) + g * GH == iota((GH, HEADS), 1)).astype(f32)
            one, two = (ddelta_a[g, rows, :], dcum_a[g, rows, :]) if g < half else (
                ddelta_b[g - half, rows, :], dcum_b[g - half, rows, :]
            )
            ddelta = ddelta + dotf(one, place)
            dcum = dcum + dotf(two, place)
        dcum = dcum + jnp.where(last, flows[c : c + 1, :], 0.0)
        x = step_ref[pl.ds(HALO + c * Q, Q), :HEADS] + par_ref[0:1, :]
        dlog = dotf(upper, dcum) * rate
        decays = decays - jnp.sum(dlog * softplus(x), axis=0, keepdims=True)
        dstep = (ddelta - dlog) * sigmoid(x)
        times = times + jnp.sum(dstep, axis=0, keepdims=True)
        most = jnp.maximum(most, jnp.max(jnp.abs(dstep), axis=0, keepdims=True))
        dstep_ref[rows, :HEADS] = dstep.astype(bf16)
    dstep_ref[pl.ds(length, PAD), :HEADS] = jnp.broadcast_to(most * 1.01, (PAD, HEADS)).astype(bf16)
    small_ref[...] = jnp.zeros_like(small_ref)
    small_ref[0:1, :] = times
    small_ref[1:2, :] = decays


def step_back(rest, pars, first, second):
    length = first[0].shape[1]
    arrays = [part for both in zip(first, second) for part in both]
    shapes = (
        jax.ShapeDtypeStruct((length + PAD, 128), bf16),
        jax.ShapeDtypeStruct((8, HEADS), f32),
    )
    return pl.pallas_call(
        step_kernel,
        grid=(1,),
        in_specs=[steps_of(rest), whole(pars)] + [whole(array) for array in arrays],
        out_specs=tuple(whole(shape) for shape in shapes),
        out_shape=shapes,
        compiler_params=params(),
        cost_estimate=pl.CostEstimate(flops=10**7, bytes_accessed=10**7, transcendentals=10**5),
        name="step_back",
    )(rest, pars, *arrays)


def unconv_kernel(mixed, x_ref, tap_ref, match_ref, dv_ref, dkq_ref, dx_ref, edge_ref, dtap_ref, *held):
    length = match_ref.shape[1]
    count = length // Q
    wide = pl.program_id(0) < mixed
    for buf in held:
        buf[0:HALO, :] = jnp.zeros((HALO, TILE), f32)
        buf[HALO + length :, :] = jnp.zeros((HALO, TILE), f32)
    for j in range(TILE // 128):
        cols = slice(128 * j, 128 * (j + 1))
        sums = [jnp.zeros((1, 128), f32) for _ in range(KW + 1)]
        for c in range(count):
            rows = slice(c * Q, (c + 1) * Q)
            s = conv_sum(x_ref, tap_ref, match_ref, c * Q, Q, cols)
            sig = sigmoid(s)
            dm = jnp.where(wide, dv_ref[rows, cols], dkq_ref[rows, cols])
            ds = dm * (sig * (1.0 + s * (1.0 - sig)))
            sums[KW] = sums[KW] + jnp.sum(ds, axis=0, keepdims=True)
            for k in range(KW):
                e = ds if k == KW - 1 else ds * match_ref[k, rows, :]
                held[k][HALO + c * Q : HALO + (c + 1) * Q, cols] = e
                taken = x_ref[pl.ds(HALO - (KW - 1) + k + c * Q, Q), cols]
                sums[k] = sums[k] + jnp.sum(e * taken, axis=0, keepdims=True)
        for k in range(KW + 1):
            dtap_ref[k : k + 1, cols] = sums[k]

        def placed(start, rows):
            total = None
            for k in range(KW):
                term = tap_ref[k : k + 1, cols] * held[k][pl.ds(start + KW - 1 - k, rows), cols]
                total = term if total is None else total + term
            return total

        edge_ref[0:HALO, cols] = placed(0, HALO)
        most = jnp.zeros((1, 128), f32)
        for c in range(count):
            dx = placed(HALO + c * Q, Q)
            most = jnp.maximum(most, jnp.max(jnp.abs(dx), axis=0, keepdims=True))
            dx_ref[c * Q : (c + 1) * Q, cols] = dx.astype(bf16)
            if c == count - 1:
                edge_ref[HALO:, cols] = dx[Q - HALO :, :]
        dtap_ref[KW + 1 : KW + 2, cols] = most
    dtap_ref[KW + 2 :, :] = jnp.zeros((8 - KW - 2, TILE), f32)


def unconv(first, rest, taps, match, dv, dkq):
    length = match.shape[1]
    high = length + HALO
    mixed = dv.shape[1] // TILE
    tiles = mixed if dkq is None else mixed + 1
    lone = dv if dkq is None else dkq
    return pl.pallas_call(
        functools.partial(unconv_kernel, mixed),
        grid=(tiles,),
        in_specs=[
            pl.BlockSpec((high, TILE), lambda j: (0, j + first)),
            pl.BlockSpec((8, TILE), lambda j: (0, j + first)),
            pl.BlockSpec((KW - 1, length, 128), lambda j: (0, 0, 0)),
            pl.BlockSpec((length, TILE), lambda j: (0, jnp.minimum(j, mixed - 1))),
            pl.BlockSpec((length, TILE), lambda j: (0, 0)),
        ],
        out_specs=(
            pl.BlockSpec((length, TILE), lambda j: (0, j)),
            pl.BlockSpec((2 * HALO, TILE), lambda j: (0, j)),
            pl.BlockSpec((8, TILE), lambda j: (0, j)),
        ),
        out_shape=(
            jax.ShapeDtypeStruct((length + PAD, tiles * TILE), bf16),
            jax.ShapeDtypeStruct((2 * HALO, tiles * TILE), f32),
            jax.ShapeDtypeStruct((8, tiles * TILE), f32),
        ),
        scratch_shapes=[pltpu.VMEM((length + 2 * HALO, TILE), f32) for _ in range(KW)],
        compiler_params=params(),
        cost_estimate=pl.CostEstimate(flops=10**8, bytes_accessed=10**7, transcendentals=10**6),
    )(rest, taps, match, dv, lone)


def adamw(param, grad, moment, square, rate, shrink):
    moment_new = beta_one * moment + (1.0 - beta_one) * grad
    square_new = beta_two * square + (1.0 - beta_two) * grad * grad
    first_corr = 1.0 - beta_one**ADAM_STEP
    second_corr = 1.0 - beta_two**ADAM_STEP
    update = moment_new / first_corr / (jnp.sqrt(square_new / second_corr) + adam_eps)
    return (param - rate * (update + shrink * param), moment_new, square_new)


def shifted(value, axis, by):
    count = lax.axis_size(axis)
    pairs = [(i, i + by) for i in range(count) if 0 <= i + by < count]
    return lax.ppermute(value, axis, pairs)


TOKENS = (((0,), (0,)), ((), ()))


def gathered(value):
    return lax.all_gather(value, "dp", axis=0, tiled=True)


def shard_gathered(value, *earlier):
    count, here = lax.axis_size("shard"), lax.axis_index("shard")
    rows, width = value.shape
    parts = [exchanged(value, "shard", k) for k in range(1, count)]
    held = jnp.zeros((count * rows, width), value.dtype)
    for k, part in enumerate([value] + parts):
        held = lax.dynamic_update_slice(held, after(part, earlier) if k else part, ((here ^ k) * rows, 0))
    return held


def exchanged(value, axis, by):
    return lax.ppermute(value, axis, [(i, i ^ by) for i in range(lax.axis_size(axis))])


def relative(value, block, core):
    base = lax.axis_index("dp") // 2
    length = value.shape[0]
    return [
        lax.dynamic_slice(value, (0, (((j ^ base) * 2) + core) * block), (length, block))
        for j in range(lax.axis_size("dp") // 2)
    ]


def both_cores(value):
    return jnp.concatenate([value, exchanged(value, "dp", 1)], axis=0)


def own_and_partner(value, block):
    core = lax.axis_index("dp") % 2
    return relative(value, block, core), relative(value, block, 1 - core)


def exponent(bound):
    return jnp.ceil(jnp.log2(jnp.maximum(bound, 1e-30)))


def coded(total, power, rows):
    scaled = total * jnp.exp2(15.0 - power)
    if total.shape[0] > rows:
        scaled = jnp.where(iota(total.shape, 0) < rows, scaled, power)
    return scaled.astype(jnp.float16)


def decoded(payload, power, rows):
    if payload.shape[0] == rows:
        return payload.astype(f32) * jnp.exp2(power - 15.0), power
    other = payload[rows : rows + 1].astype(f32)
    return payload.astype(f32) * jnp.exp2(other - 15.0), jnp.maximum(power, other) + 1.0


def after(value, *earlier):
    return lax.optimization_barrier((value, earlier))[0]


def split_plan(order):
    kept, sends = [0], []
    for bit in reversed(order):
        send = [j ^ (1 << bit) for j in kept]
        sends.insert(0, send)
        kept = kept + send
    return kept, sends


def columns_of(blocks, order, pad):
    kept, sends = split_plan(order)
    zeros = [jnp.zeros((blocks[0].shape[0], pad), bf16)] if pad else []
    return (
        jnp.concatenate([blocks[j] for j in kept[: len(sends[0])]] + zeros, axis=1),
        jnp.concatenate([blocks[j] for j in sends[0]] + zeros, axis=1),
    )


class Sum:
    def __init__(self, held, sent, rhs, power, order, pad):
        self.held, self.sent, self.rhs = held, sent, rhs
        self.power = power
        self.order = order
        self.pad = pad
        self.rows = 2 * (sent.shape[1] - pad)
        self.total = None
        self.at = 0

    def prepare(self):
        self.rows //= 2
        if self.total is None:
            part = lax.dot_general(self.sent, self.rhs, TOKENS, preferred_element_type=f32)
        else:
            part = self.total[self.rows : 2 * self.rows + self.pad]
        self.payload = coded(part, self.power, self.rows)

    def send(self):
        self.got = exchanged(self.payload, "dp", 2 << self.order[self.at])
        self.at += 1
        if self.total is None:
            self.total = lax.dot_general(self.held, self.rhs, TOKENS, preferred_element_type=f32)

    def take(self, *earlier):
        got, self.power = decoded(after(self.got, earlier), self.power, self.rows)
        self.total = self.total[: self.rows + self.pad] + got

    def more(self):
        return self.at < len(self.order)

    def finish(self):
        while self.more():
            self.prepare()
            self.send()
            self.take()


class ShardSum:
    def __init__(self, sums):
        count, here = lax.axis_size("shard"), lax.axis_index("shard")
        self.rows = sums[0].rows // count
        self.total = jnp.concatenate([one.total for one in sums], axis=1) if len(sums) > 1 else sums[0].total
        self.power = jnp.concatenate([one.power for one in sums], axis=1) if len(sums) > 1 else sums[0].power
        taken = (self.rows + sums[0].pad, self.total.shape[1])
        self.payloads = [
            coded(lax.dynamic_slice(self.total, ((here ^ k) * self.rows, 0), taken), self.power, self.rows)
            for k in range(1, count)
        ]
        self.parts = [exchanged(part, "shard", k + 1) for k, part in enumerate(self.payloads)]

    def take(self, *earlier):
        here = lax.axis_index("shard")
        result = lax.dynamic_slice(self.total, (here * self.rows, 0), (self.rows, self.total.shape[1]))
        for part in self.parts:
            result = result + decoded(after(part, earlier), self.power, self.rows)[0][: self.rows]
        return result


class Everywhere:
    def __init__(self, value):
        self.value = value
        self.steps = []
        for axis in ("dp", "shard"):
            count, by = lax.axis_size(axis), 1
            while by < count:
                self.steps.append((axis, by))
                by *= 2

    def send(self):
        self.got = exchanged(self.value, *self.steps.pop(0))

    def take(self, *earlier):
        self.value = self.value + after(self.got, earlier)

    def finish(self):
        while self.steps:
            self.send()
            self.take()
        return self.value


def carried(state, half, factor, by):
    incoming = shifted(half, "shard", by)
    for _ in range(1, lax.axis_size("shard") - 1):
        passed = (state + factor * incoming.astype(f32)).astype(bf16)
        incoming = shifted(passed, "shard", by)
    return incoming


def both_with_most(rows):
    length = rows.shape[0] - PAD
    arrived = exchanged(rows, "dp", 1)
    most = jnp.maximum(rows[length : length + 1], arrived[length : length + 1]).astype(f32)
    return jnp.concatenate([rows[:length], arrived[:length]], axis=0), most


def mended(dx, edge, dtap, length):
    last = edge[HALO:] + shifted(edge[:HALO], "shard", -1)
    most = jnp.maximum(dtap[KW + 1 : KW + 2], jnp.max(jnp.abs(last), axis=0, keepdims=True)) * 1.01
    tail = jnp.concatenate([last, jnp.broadcast_to(most, (PAD, most.shape[1]))], axis=0).astype(bf16)
    return lax.dynamic_update_slice(dx, tail, (length - HALO, 0)), dtap


def rest_sums(both, bound, in_columns, orders):
    middle = both.shape[1] // 256 * 128
    power = exponent(bound)
    return [
        Sum(*in_columns[0], both[:, :middle], power[:, :middle], orders[0], PAD),
        Sum(*in_columns[1], both[:, middle:], power[:, middle:], orders[1], PAD),
    ]


def shards(
    hidden_in, cotangent, segment_ids,
    param_prenorm, param_inputs, param_kernel, param_offsets, param_timestep, param_decays,
    param_direct, param_gating, param_outputs,
    moment_prenorm, moment_inputs, moment_kernel, moment_offsets, moment_timestep, moment_decays,
    moment_direct, moment_gating, moment_outputs,
    square_prenorm, square_inputs, square_kernel, square_offsets, square_timestep, square_decays,
    square_direct, square_gating, square_outputs,
):
    length, width = hidden_in.shape
    own_inputs = param_inputs.astype(bf16)
    spare = -(param_inputs.shape[1] - DI) % 128
    upstream = cotangent.astype(bf16)
    own_rows = param_inputs.shape[0]
    most = jnp.broadcast_to((jnp.max(jnp.abs(cotangent)) * 1.01).astype(bf16), (own_rows, 1))
    rest_rows = shard_gathered(
        jnp.concatenate([own_inputs[:, DI:], most, jnp.zeros((own_rows, spare - 1), bf16)], axis=1),
    )
    rest_w = gathered(rest_rows)

    seg = segment_ids.astype(f32)
    ends = jnp.pad(seg[length - HALO :], (0, width - HALO))[None, :]
    halo = shifted(
        jnp.concatenate([hidden_in[length - HALO :], jnp.broadcast_to(ends, (HALO, width))], axis=0),
        "shard", 1,
    )
    rim_seg = jnp.where(lax.axis_index("shard") == 0, -1.0, halo[HALO, :HALO])
    rim = rim_seg[HALO - 1]
    all_segs = jnp.concatenate([rim_seg, seg])
    match = jnp.stack(
        [
            (all_segs[HALO - (KW - 1) + k : HALO - (KW - 1) + k + length] == seg).astype(f32)
            for k in range(KW - 1)
        ]
    )
    match = jnp.broadcast_to(match[:, :, None], (KW - 1, length, 128))
    chunks = seg.reshape(-1, Q)
    before = jnp.concatenate([rim[None], chunks[:-1, Q - 1]])
    mask = jnp.stack(
        [
            (chunks == before[:, None]).reshape(-1),
            (chunks == chunks[:, Q - 1 :]).reshape(-1),
            seg == rim,
            seg == seg[length - 1],
        ]
        + [seg < -1.0] * 4,
        axis=1,
    ).astype(f32)
    segc = jnp.broadcast_to(seg[:, None], (length, 8))
    segr = jnp.broadcast_to(seg[None, :], (8, length))

    taps = jnp.concatenate([param_kernel, param_offsets[None, :], jnp.zeros((8 - KW - 1, CH), f32)], axis=0)
    pars = jnp.concatenate([param_timestep[None, :], param_decays[None, :], jnp.zeros((6, HEADS), f32)], axis=0)
    dirx = jnp.broadcast_to(jnp.repeat(param_direct, HEAD_DIM)[None, :], (8, DI))
    gam = jnp.broadcast_to(param_gating[None, :], (8, DI))

    hidden = jnp.concatenate([halo[:HALO], hidden_in], axis=0)
    inv = lax.rsqrt(jnp.mean(hidden * hidden, axis=1, keepdims=True) + norm_eps)
    normed = (hidden * inv * param_prenorm).astype(bf16)
    own_normed = normed[HALO:]

    groups = lax.axis_size("shard")
    spots = [bit for bit in range(20) if (2 << bit) < lax.axis_size("dp")]
    orders = (spots, spots[::-1])
    in_block, out_block = groups * param_inputs.shape[0], groups * param_outputs.shape[0]
    up_both = both_cores(after(upstream, rest_rows))
    own_blocks, partner_blocks = own_and_partner(own_normed, in_block)
    arrived = exchanged(jnp.concatenate(partner_blocks, axis=1), "dp", 1)
    both_blocks = [
        jnp.concatenate([one, arrived[:, j * in_block : (j + 1) * in_block]], axis=0)
        for j, one in enumerate(own_blocks)
    ]
    in_columns = [columns_of(both_blocks, order, PAD) for order in orders]
    norm_bound = 2.02 * length * width**0.5 * jnp.max(jnp.abs(param_prenorm))
    early = (match, mask, segc, segr, taps, pars, dirx, gam, up_both, norm_bound, in_columns, normed)
    gate_rows = shard_gathered(after(own_inputs[:, :DI], rest_rows), early)
    gate_w = gathered(gate_rows)
    rest_w = after(rest_w, early)

    rest = jnp.dot(normed, rest_w, preferred_element_type=f32)
    delta, cum, cumt, tailc, taild, infd, keep, factor = prep(rest, pars, mask)
    v, kq, state, state_half = conv_state(rest, taps, match, taild)
    out_rows = shard_gathered(after(param_outputs.astype(bf16), gate_rows), v)
    out_w = gathered(out_rows)
    state = after(state, out_rows)
    incoming = carried(state, state_half, factor[0:1], 1)
    y = local_out(v, kq, delta, cum, cumt, mask, keep, segc, segr)
    gate_w = after(gate_w, y)
    z = jnp.dot(own_normed, gate_w, preferred_element_type=f32)
    out_w = after(out_w, z)
    back_gated = lax.dot_general(upstream, out_w, NT, preferred_element_type=f32)
    tokens = length * lax.axis_size("dp") * groups
    cotangent_most = jnp.max(rest_w[:, param_inputs.shape[1] - DI]).astype(f32)
    out_power = exponent(1.02 * tokens * DI**0.5 * jnp.max(jnp.abs(param_gating)) * cotangent_most)
    place = lax.axis_index("dp")
    block = out_block if out_block % 128 == 0 and len(spots) == 2 else 0
    at = jnp.stack([place // 2, place % 2]).astype(jnp.int32)
    gated, blocks, dy, dz, dinc, dinc_half, small = gate(
        block, at, y, v, z, back_gated, kq, incoming, infd, dirx, gam
    )

    outgoing = carried(dinc, dinc_half, factor[0:1], -1)
    if not block:
        own_blocks, partner_blocks = own_and_partner(gated, out_block)
        blocks = jnp.stack([*columns_of(own_blocks, spots, 0), *columns_of(partner_blocks, spots, 0)])
    arrived = exchanged(blocks[2:], "dp", 1)
    out_columns = [jnp.concatenate([blocks[i], arrived[i]], axis=0) for i in range(2)]
    dz_most = jnp.broadcast_to(small[2:3] * 1.01, (PAD, DI)).astype(bf16)
    dz = lax.dynamic_update_slice(dz, dz_most, (length, 0))
    dz_both, dz_bound = both_with_most(dz)
    block_out = hidden_in + jnp.dot(gated, out_w, preferred_element_type=f32)
    out_sum = Sum(*out_columns, up_both, out_power, spots, 0)
    gate_sum = Sum(*in_columns[1], dz_both, exponent(norm_bound * dz_bound), spots[::-1], PAD)
    first_sums = [out_sum, gate_sum]
    for one in first_sums:
        one.prepare()
        one.send()
    back_normed = lax.dot_general(dz, gate_w, NT, preferred_element_type=f32)
    outgoing = after(
        outgoing, out_sum.payload, gate_sum.payload, out_sum.total, gate_sum.total, back_normed, block_out
    )

    ssm = (kq, delta, cum, cumt, tailc, mask, keep, incoming)
    half = NG // 2
    dv1, *held1 = back_local(0, half, None, v, dy, *ssm, outgoing, dirx, segc, segr)
    for one in first_sums:
        one.take(dv1)
        if one.more():
            one.prepare()
            one.send()
    dv1 = after(dv1, *[one.payload for one in first_sums])
    drest1, dtap1 = mended(*unconv(0, rest, taps, match, dv1, None), length)
    both1, bound1 = both_with_most(drest1)
    sums1 = rest_sums(both1, norm_bound * bound1, in_columns, orders)
    for one in first_sums:
        one.take(dv1, both1)
        one.finish()
    shard_out, shard_gate = ShardSum([out_sum]), ShardSum([gate_sum])
    for one in sums1:
        one.prepare()
        one.send()
    dy = after(
        dy, [one.payload for one in sums1], [one.total for one in sums1], shard_out.payloads, shard_gate.payloads
    )
    dv2, *held2 = back_local(half, NG, held1[:2], v, dy, *ssm, outgoing, dirx, segc, segr)
    for one in sums1:
        one.take(dv2)
        if one.more():
            one.prepare()
            one.send()
    dv2 = after(dv2, *[one.payload for one in sums1])
    dstep, small_step = step_back(rest, pars, held1[2:], held2[2:])
    drest2, dtap2 = mended(*unconv(dv1.shape[1] // TILE, rest, taps, match, dv2, held2[0]), length)
    drest2 = jnp.concatenate([drest2, dstep], axis=1)
    both2, bound2 = both_with_most(drest2)
    sums2 = rest_sums(both2, norm_bound * bound2, in_columns, orders)
    for one in sums2:
        one.prepare()
        one.send()
    for one in sums1:
        one.take(dv2, dstep)
        one.finish()
    shard1 = ShardSum(sums1)
    drest1, drest2 = after((drest1, drest2), shard1.payloads, [two.payload for two in sums2])
    wide1 = drest1.shape[1]
    back_normed = back_normed + lax.dot_general(drest1, rest_w[:, :wide1], NT, preferred_element_type=f32)
    back_normed = back_normed + lax.dot_general(drest2, rest_w[:, wide1:], NT, preferred_element_type=f32)
    back_normed = back_normed[:length]
    own_inv = inv[HALO:]
    scaled = hidden_in * own_inv
    gained = back_normed * param_prenorm
    hidden_grad = cotangent + own_inv * (
        gained - scaled * jnp.mean(gained * scaled, axis=1, keepdims=True)
    )
    grad_prenorm = jnp.sum(back_normed * scaled, axis=0)

    dtap = jnp.concatenate([dtap1, dtap2], axis=1)
    pieces = [
        grad_prenorm,
        dtap[:KW].reshape(-1),
        dtap[KW],
        small_step[0],
        small_step[1],
        jnp.sum(small[1].reshape(HEADS, HEAD_DIM), axis=1),
        small[0],
    ]
    flat = jnp.concatenate(pieces)
    count = flat.shape[0]
    lines = -(-count // 1024) * 8
    everywhere = Everywhere(jnp.pad(flat, (0, lines * 128 - count)).reshape(lines, 128))
    everywhere.send()
    for one in sums2:
        one.take(back_normed)
        if one.more():
            one.prepare()
            one.send()
    sent = [one.payload for one in sums2]
    everywhere.take(sent)
    everywhere.send()
    for one in sums2:
        one.take(everywhere.value)
        one.finish()
    shard2 = ShardSum(sums2)
    sent = shard2.payloads
    everywhere.take(sent)
    total = everywhere.finish().reshape(-1)
    grad_outputs = shard_out.take(sent)
    grad_gate = shard_gate.take(sent)
    grad_rest = jnp.concatenate([shard1.take(sent), shard2.take()], axis=1)
    grad_inputs = jnp.concatenate([grad_gate, grad_rest[:, : param_inputs.shape[1] - DI]], axis=1)
    found, at = [], 0
    for piece in pieces:
        found.append(total[at : at + piece.shape[0]])
        at += piece.shape[0]
    grad_prenorm, grad_kernel, grad_offsets, grad_timestep, grad_decays, grad_direct, grad_gating = found
    grad_kernel = grad_kernel.reshape(KW, CH)

    params = (
        param_prenorm, param_inputs, param_kernel, param_offsets, param_timestep, param_decays,
        param_direct, param_gating, param_outputs,
    )
    moments = (
        moment_prenorm, moment_inputs, moment_kernel, moment_offsets, moment_timestep, moment_decays,
        moment_direct, moment_gating, moment_outputs,
    )
    squares = (
        square_prenorm, square_inputs, square_kernel, square_offsets, square_timestep, square_decays,
        square_direct, square_gating, square_outputs,
    )
    grads = (
        grad_prenorm, grad_inputs, grad_kernel, grad_offsets, grad_timestep, grad_decays,
        grad_direct, grad_gating, grad_outputs,
    )
    updated = [
        adamw(params[i], grads[i], moments[i], squares[i], rate_table[i], shrink_table[i])
        for i in range(9)
    ]
    return (
        (block_out, hidden_grad)
        + grads
        + tuple(u[0] for u in updated)
        + tuple(u[1] for u in updated)
        + tuple(u[2] for u in updated)
    )


def solution(mesh):
    rows = P(("dp", "shard"), None)
    member = (P(), rows, P(), P(), P(), P(), P(), P(), rows)

    return jax.shard_map(
        shards,
        mesh=mesh,
        in_specs=(rows, rows, P(("dp", "shard"))) + member * 3,
        out_specs=(rows, rows) + member * 4,
        check_vma=False,
    )
```

```python
import functools

import jax
import jax.numpy as jnp
from jax import lax
from jax.experimental import pallas as pl
from jax.experimental.pallas import tpu as pltpu
from jax.sharding import PartitionSpec as P


HEADS = 48
HEAD_DIM = 64
STATE = 128
KW = 4
ADAM_STEP = 10
DI = 3072
CH = 3328

Q = 128
GH = 8
GW = GH * HEAD_DIM
NG = HEADS // GH
HALO = 8
PAD = 16
TILE = 256

bf16 = jnp.bfloat16
f32 = jnp.float32
highest = lax.Precision.HIGHEST

norm_eps = 1e-05
beta_one = 0.9
beta_two = 0.95
adam_eps = 1e-08
rate_table = (0.2, 0.01, 0.2, 0.2, 0.2, 0.2, 0.2, 0.2, 0.01)
shrink_table = (0.0, 0.1, 0.1, 0.0, 0.0, 0.0, 0.0, 0.0, 0.1)

NN = (((1,), (0,)), ((), ()))
NT = (((1,), (1,)), ((), ()))


def halves(x):
    hi = x.astype(bf16)
    return hi, (x - hi.astype(f32)).astype(bf16)


def dot1(a, b, dims=NN):
    return lax.dot_general(a.astype(bf16), b.astype(bf16), dims, preferred_element_type=f32)


def dot3(a, b, dims=NN):
    ah, al = halves(a)
    bh, bl = halves(b)
    return dot1(ah, bh, dims) + (dot1(ah, bl, dims) + dot1(al, bh, dims))


def dot_halves(a, b, dims=NN):
    return dot1(a[0], b[0], dims) + (dot1(a[0], b[1], dims) + dot1(a[1], b[0], dims))


def dotf(a, b, dims=NN):
    return lax.dot_general(a, b, dims, precision=highest, preferred_element_type=f32)


def iota(shape, dim):
    return lax.broadcasted_iota(jnp.int32, shape, dim)


def sigmoid(x):
    return 0.5 * jnp.tanh(0.5 * x) + 0.5


def softplus(x):
    u = jnp.exp(-jnp.abs(x))
    series = u * (1.0 - u * (0.5 - u * (1.0 / 3.0 - u * (0.25 - u * 0.2))))
    return jnp.maximum(x, 0.0) + jnp.where(u < 0.03, series, jnp.log(1.0 + u))


def pair_lanes(cols, j):
    rows = cols.shape[0]
    low = iota((rows, 128), 1) < HEAD_DIM
    return jnp.where(low, cols[:, 2 * j : 2 * j + 1], cols[:, 2 * j + 1 : 2 * j + 2])


def group_lanes(cols):
    return jnp.concatenate([pair_lanes(cols, j) for j in range(cols.shape[1] // 2)], axis=1)


def head_onehot():
    return (iota((HEADS, DI), 1) // HEAD_DIM == iota((HEADS, DI), 0)).astype(f32)


def params(limit=60000, **kw):
    return pltpu.CompilerParams(vmem_limit_bytes=limit * 1024, **kw)


def prep_kernel(
    step_ref, par_ref, mask_ref, delta_ref, cum_ref, cumt_ref, tailc_ref,
    taild_ref, infd_ref, keep_ref, factor_ref,
):
    length = mask_ref.shape[0]
    count = length // Q
    tri = (iota((Q, Q), 0) >= iota((Q, Q), 1)).astype(f32)
    eye = (iota((HEADS, HEADS), 0) == iota((HEADS, HEADS), 1)).astype(f32)
    rate = jnp.exp(par_ref[1:2, :])
    base = jnp.zeros((1, HEADS), f32)
    held = []
    keeps = []
    for c in range(count):
        rows = slice(c * Q, (c + 1) * Q)
        delta = softplus(step_ref[pl.ds(HALO + c * Q, Q), :HEADS] + par_ref[0:1, :])
        cum = dotf(tri, -delta * rate)
        cumt_ref[:, rows] = dotf(eye, cum, NT)
        last = cum[Q - 1 : Q, :]
        tailc = jnp.exp(last - cum) * mask_ref[rows, 1:2] * delta
        for g in range(NG):
            part = slice(g * GH, (g + 1) * GH)
            delta_ref[g, rows, :] = delta[:, part]
            cum_ref[g, rows, :] = cum[:, part]
            tailc_ref[g, rows, :] = tailc[:, part]
        keeps.append(jnp.exp(last) * mask_ref[(c + 1) * Q - 1 : (c + 1) * Q, 0:1])
        whole = cum + base
        infd_ref[rows, :] = jnp.exp(whole) * mask_ref[rows, 2:3]
        held.append((whole, delta))
        base = base + last
    for c in range(count):
        rows = slice(c * Q, (c + 1) * Q)
        whole, delta = held[c]
        taild = jnp.exp(base - whole) * mask_ref[rows, 3:4] * delta
        for g in range(NG):
            taild_ref[g, rows, :] = taild[:, g * GH : (g + 1) * GH]
    factor = jnp.exp(base) * mask_ref[length - 1 : length, 2:3]
    spread = head_onehot()
    line = iota((8, HEADS), 0)
    table = jnp.zeros((8, HEADS), f32)
    for c in range(count):
        table = jnp.where(line == c, keeps[c], table)
    keep_ref[...] = dotf(table, spread)
    factor_ref[...] = dotf(jnp.where(line == 0, factor, 0.0), spread)


def whole(array):
    return pl.BlockSpec(array.shape, lambda i: (0,) * array.ndim)


def steps_of(rest):
    return pl.BlockSpec((rest.shape[0], 128), lambda i: (0, CH // 128))


def prep(rest, pars, mask):
    length = mask.shape[0]
    cols = jax.ShapeDtypeStruct((NG, length, GH), f32)
    wide = jax.ShapeDtypeStruct((8, DI), f32)
    shapes = (
        cols, cols, jax.ShapeDtypeStruct((HEADS, length), f32), cols, cols,
        jax.ShapeDtypeStruct((length, HEADS), f32), wide, wide,
    )
    return pl.pallas_call(
        prep_kernel,
        grid=(1,),
        in_specs=[steps_of(rest), whole(pars), whole(mask)],
        out_specs=tuple(whole(shape) for shape in shapes),
        out_shape=shapes,
        compiler_params=params(),
        cost_estimate=pl.CostEstimate(flops=10**7, bytes_accessed=10**7, transcendentals=10**5),
        name="prep",
    )(rest, pars, mask)


def conv_sum(x_ref, tap_ref, match_ref, start, rows, cols):
    total = tap_ref[KW : KW + 1, cols] + tap_ref[KW - 1 : KW, cols] * x_ref[
        pl.ds(HALO + start, rows), cols
    ]
    for k in range(KW - 1):
        taken = x_ref[pl.ds(HALO - (KW - 1) + k + start, rows), cols]
        total = total + tap_ref[k : k + 1, cols] * (taken * match_ref[k, pl.ds(start, rows), :])
    return total


def conv_kernel(
    xv_ref, xk_ref, tv_ref, tk_ref, match_ref, taild_ref, v_ref, kq_ref, state_ref, state_half_ref, kt_hi, kt_lo
):
    length = v_ref.shape[0]
    count = length // Q

    @pl.when(pl.program_id(0) == 0)
    def _():
        for c in range(count):
            for j in range(2):
                cols = slice(128 * j, 128 * (j + 1))
                s = conv_sum(xk_ref, tk_ref, match_ref, c * Q, Q, cols)
                m = s * sigmoid(s)
                kq_ref[c * Q : (c + 1) * Q, cols] = m
                if j == 0:
                    hi, lo = halves(m.T)
                    kt_hi[:, c * Q : (c + 1) * Q] = hi
                    kt_lo[:, c * Q : (c + 1) * Q] = lo

    total = jnp.zeros((STATE, GW), f32)
    for c in range(count):
        rows = slice(c * Q, (c + 1) * Q)
        tail = taild_ref[0, rows, :]
        parts = []
        for j in range(GW // 128):
            cols = slice(128 * j, 128 * (j + 1))
            s = conv_sum(xv_ref, tv_ref, match_ref, c * Q, Q, cols)
            m = s * sigmoid(s)
            v_ref[rows, cols] = m
            parts.append(m * pair_lanes(tail, j))
        hi, lo = halves(jnp.concatenate(parts, axis=1))
        kh, kl = kt_hi[:, rows], kt_lo[:, rows]
        total = total + (dot1(kh, hi) + (dot1(kh, lo) + dot1(kl, hi)))
    state_ref[...] = total
    state_half_ref[...] = total.astype(bf16)


def conv_state(rest, taps, match, taild):
    length = match.shape[1]
    high = length + HALO
    kq_at = DI // (2 * STATE)
    return pl.pallas_call(
        conv_kernel,
        grid=(NG,),
        in_specs=[
            pl.BlockSpec((high, GW), lambda g: (0, g)),
            pl.BlockSpec((high, 2 * STATE), lambda g: (0, kq_at)),
            pl.BlockSpec((8, GW), lambda g: (0, g)),
            pl.BlockSpec((8, 2 * STATE), lambda g: (0, kq_at)),
            pl.BlockSpec((KW - 1, length, 128), lambda g: (0, 0, 0)),
            pl.BlockSpec((1, length, GH), lambda g: (g, 0, 0)),
        ],
        out_specs=(
            pl.BlockSpec((length, GW), lambda g: (0, g)),
            pl.BlockSpec((length, 2 * STATE), lambda g: (0, 0)),
            pl.BlockSpec((STATE, GW), lambda g: (0, g)),
            pl.BlockSpec((STATE, GW), lambda g: (0, g)),
        ),
        out_shape=(
            jax.ShapeDtypeStruct((length, DI), f32),
            jax.ShapeDtypeStruct((length, 2 * STATE), f32),
            jax.ShapeDtypeStruct((STATE, DI), f32),
            jax.ShapeDtypeStruct((STATE, DI), bf16),
        ),
        scratch_shapes=[pltpu.VMEM((STATE, length), bf16), pltpu.VMEM((STATE, length), bf16)],
        compiler_params=params(),
        cost_estimate=pl.CostEstimate(flops=2 * 10**9, bytes_accessed=2 * 10**7, transcendentals=2 * 10**6),
        name="conv_state",
    )(rest, rest, taps, taps, match, taild)


def masks_of(segc_ref, segr_ref, rows):
    same = segc_ref[rows, 0:1] == segr_ref[0:1, rows]
    later = iota((Q, Q), 0) >= iota((Q, Q), 1)
    earlier = iota((Q, Q), 0) <= iota((Q, Q), 1)
    return jnp.where(same & later, 0.0, -1e30), jnp.where(same & earlier, 0.0, -1e30)


def local_kernel(
    v_ref, kq_ref, delta_ref, cum_ref, cumt_ref, mask_ref, keep_ref, segc_ref, segr_ref,
    y_ref, gram, bias, kt_hi, kt_lo,
):
    length = v_ref.shape[0]
    count = length // Q

    @pl.when(pl.program_id(0) == 0)
    def _():
        for c in range(count):
            rows = slice(c * Q, (c + 1) * Q)
            k, q = kq_ref[rows, :STATE], kq_ref[rows, STATE:]
            bias[rows, :] = masks_of(segc_ref, segr_ref, rows)[0]
            gram[rows, :] = dot3(q, k, NT)
            kt_hi[:, rows], kt_lo[:, rows] = halves(k.T)

    low = iota((Q, 128), 1) < HEAD_DIM
    state = None
    for c in range(count):
        rows = slice(c * Q, (c + 1) * Q)
        delta, cum = delta_ref[0, rows, :], cum_ref[0, rows, :]
        alive = jnp.broadcast_to(mask_ref[rows, 0:1], (Q, 128))
        ending = jnp.broadcast_to(mask_ref[rows, 1:2], (Q, 128))
        if c:
            carried = dot3(kq_ref[rows, STATE:], state)
        tails = []
        for j in range(GW // 128):
            cols = slice(128 * j, 128 * (j + 1))
            w = v_ref[rows, cols] * pair_lanes(delta, j)
            run = pair_lanes(cum, j)
            both = []
            for i in (2 * j, 2 * j + 1):
                fade = jnp.exp(cum[:, i : i + 1] - cumt_ref[i : i + 1, rows] + bias[rows, :])
                both.append(halves(gram[rows, :] * fade))
            parts = halves(w)
            zero = jnp.zeros_like(parts[0])
            stacked = tuple(
                jnp.concatenate([jnp.where(low, part, zero), jnp.where(low, zero, part)], axis=0)
                for part in parts
            )
            y = dot_halves(tuple(jnp.concatenate([both[0][i], both[1][i]], axis=1) for i in (0, 1)), stacked)
            if c:
                y = y + carried[:, cols] * (jnp.exp(run) * alive)
            y_ref[rows, cols] = y
            if c < count - 1:
                tails.append(halves(w * (jnp.exp(run[Q - 1 : Q, :] - run) * ending)))
        if c < count - 1:
            fresh = dot_halves(
                (kt_hi[:, rows], kt_lo[:, rows]),
                tuple(jnp.concatenate([part[i] for part in tails], axis=1) for i in (0, 1)),
            )
            state = fresh if state is None else state * keep_ref[c : c + 1, :] + fresh


def local_out(v, kq, delta, cum, cumt, mask, keep, segc, segr):
    length = v.shape[0]
    cols = pl.BlockSpec((1, length, GH), lambda g: (g, 0, 0))
    return pl.pallas_call(
        local_kernel,
        grid=(NG,),
        in_specs=[
            pl.BlockSpec((length, GW), lambda g: (0, g)),
            pl.BlockSpec((length, 2 * STATE), lambda g: (0, 0)),
            cols, cols,
            pl.BlockSpec((GH, length), lambda g: (g, 0)),
            pl.BlockSpec((length, 8), lambda g: (0, 0)),
            pl.BlockSpec((8, GW), lambda g: (0, g)),
            pl.BlockSpec((length, 8), lambda g: (0, 0)),
            pl.BlockSpec((8, length), lambda g: (0, 0)),
        ],
        out_specs=pl.BlockSpec((length, GW), lambda g: (0, g)),
        out_shape=jax.ShapeDtypeStruct((length, DI), f32),
        scratch_shapes=[
            pltpu.VMEM((length, Q), f32), pltpu.VMEM((length, Q), f32),
            pltpu.VMEM((STATE, length), bf16), pltpu.VMEM((STATE, length), bf16),
        ],
        compiler_params=params(),
        cost_estimate=pl.CostEstimate(flops=2 * 10**9, bytes_accessed=2 * 10**7, transcendentals=4 * 10**6),
        name="local_out",
    )(v, kq, delta, cum, cumt, mask, keep, segc, segr)


def gate_kernel(
    block, at_ref, y_ref, v_ref, z_ref, g_ref, kq_ref, inc_ref, infd_ref, dir_ref, gam_ref,
    out_ref, blocks_ref, dy_ref, dz_ref, dinc_ref, dinc_half_ref, small_ref, ybuf, rbuf,
):
    first = pl.program_id(0) == 0
    rows = y_ref.shape[0]
    q = kq_ref[:, STATE:]
    inflow = infd_ref[...]
    square = jnp.zeros((rows, 128), f32)
    cross = jnp.zeros((rows, 128), f32)
    for j in range(DI // 128):
        cols = slice(128 * j, 128 * (j + 1))
        carry = dot3(q, inc_ref[:, cols]) * pair_lanes(inflow, j)
        y = y_ref[:, cols] + carry + dir_ref[0:1, cols] * v_ref[:, cols]
        z = z_ref[:, cols]
        gated = y * (z * sigmoid(z))
        ybuf[:, cols] = y
        rbuf[:, cols] = gated
        square = square + gated * gated
        cross = cross + gated * (g_ref[:, cols] * gam_ref[0:1, cols])
    inv = lax.rsqrt(jnp.sum(square, axis=1, keepdims=True) * (1.0 / DI) + norm_eps)
    slope = inv * inv * inv * (jnp.sum(cross, axis=1, keepdims=True) * (1.0 / DI))
    qt = q.T

    @pl.when(first)
    def _():
        dinc_ref[...] = jnp.zeros_like(dinc_ref)
        small_ref[...] = jnp.zeros_like(small_ref)

    for j in range(DI // 128):
        cols = slice(128 * j, 128 * (j + 1))
        gated = rbuf[:, cols]
        scaled = gated * inv
        gam = gam_ref[0:1, cols]
        half = (scaled * gam).astype(bf16)
        out_ref[:, cols] = half
        if block:
            per = block // 128
            far = ((j // per) >> 1) ^ at_ref[0]
            which = 2 * (((j // per) & 1) ^ at_ref[1]) + (far & 1)
            place = pl.multiple_of((far >> 1) * block + (j % per) * 128, 128)
            blocks_ref[which, :, pl.ds(place, 128)] = half
        g = g_ref[:, cols]
        dgated = inv * (g * gam) - gated * slope
        z = z_ref[:, cols]
        s = sigmoid(z)
        dy = dgated * (z * s)
        dy_ref[:, cols] = dy
        dz = dgated * ybuf[:, cols] * (s * (1.0 + z * (1.0 - s)))
        dz_ref[:, cols] = dz.astype(bf16)
        small_ref[2:3, cols] = jnp.maximum(
            small_ref[2:3, cols], jnp.max(jnp.abs(dz), axis=0, keepdims=True)
        )
        small_ref[0:1, cols] += jnp.sum(g * scaled, axis=0, keepdims=True)
        small_ref[1:2, cols] += jnp.sum(dy * v_ref[:, cols], axis=0, keepdims=True)
        dinc_ref[:, cols] += dot3(qt, dy * pair_lanes(inflow, j))

    @pl.when(pl.program_id(0) == pl.num_programs(0) - 1)
    def _():
        dinc_half_ref[...] = dinc_ref[...].astype(bf16)


def gate(block, at, y, v, z, g, kq, inc, infd, dirx, gam):
    length = y.shape[0]
    tile = Q
    big = pl.BlockSpec((tile, DI), lambda i, at: (i, 0))
    fixed = lambda rows: pl.BlockSpec((rows, DI), lambda i, at: (0, 0))
    spare = 2 * block if block else 128
    return pl.pallas_call(
        functools.partial(gate_kernel, block),
        grid_spec=pltpu.PrefetchScalarGridSpec(
            num_scalar_prefetch=1,
            grid=(length // tile,),
            in_specs=[
                big, big, big, big,
                pl.BlockSpec((tile, 2 * STATE), lambda i, at: (i, 0)),
                fixed(STATE),
                pl.BlockSpec((tile, HEADS), lambda i, at: (i, 0)),
                fixed(8), fixed(8),
            ],
            out_specs=(
                big, pl.BlockSpec((4, tile, spare), lambda i, at: (0, i, 0)), big, big,
                fixed(STATE), fixed(STATE), fixed(8),
            ),
            scratch_shapes=[pltpu.VMEM((tile, DI), f32), pltpu.VMEM((tile, DI), f32)],
        ),
        out_shape=(
            jax.ShapeDtypeStruct((length, DI), bf16),
            jax.ShapeDtypeStruct((4, length, spare), bf16),
            jax.ShapeDtypeStruct((length, DI), f32),
            jax.ShapeDtypeStruct((length + PAD, DI), bf16),
            jax.ShapeDtypeStruct((STATE, DI), f32),
            jax.ShapeDtypeStruct((STATE, DI), bf16),
            jax.ShapeDtypeStruct((8, DI), f32),
        ),
        compiler_params=params(),
        cost_estimate=pl.CostEstimate(flops=10**9, bytes_accessed=4 * 10**7, transcendentals=4 * 10**6),
        name="gate",
    )(at, y, v, z, g, kq, inc, infd, dirx, gam)


def back_kernel(
    final, v_ref, dy_ref, kq_ref, delta_ref, cum_ref, cumt_ref, tailc_ref, mask_ref, keep_ref,
    inc_ref, dout_ref, dir_ref, segc_ref, segr_ref, dkq_in, dgram_in,
    dv_ref, dkq_ref, dgram, ddelta_ref, dcum_ref, drow_ref, flow_ref,
    gram, gramt, bias, biast, kt_hi, kt_lo, qt_hi, qt_lo, kq_hi, kq_lo, states,
):
    length = v_ref.shape[0]
    count = length // Q
    step = pl.program_id(0)

    @pl.when(step == 0)
    def _():
        for c in range(count):
            rows = slice(c * Q, (c + 1) * Q)
            k, q = kq_ref[rows, :STATE], kq_ref[rows, STATE:]
            b, bt = masks_of(segc_ref, segr_ref, rows)
            bias[rows, :] = b
            biast[rows, :] = bt
            scores = dot3(q, k, NT)
            gram[rows, :] = scores
            gramt[rows, :] = scores.T
            kt_hi[:, rows], kt_lo[:, rows] = halves(k.T)
            qt_hi[:, rows], qt_lo[:, rows] = halves(q.T)
            kq_hi[rows, :], kq_lo[rows, :] = halves(kq_ref[rows, :])
        dgram[...] = dgram_in[...]
        dkq_ref[...] = dkq_in[...]

    low = iota((Q, 128), 1) < HEAD_DIM
    lane = iota((Q, GH), 1)
    line = iota((8, GW), 0)

    states[0] = inc_ref[...].astype(f32)
    for c in range(count):
        rows = slice(c * Q, (c + 1) * Q)
        weighted = halves(v_ref[rows, :] * group_lanes(tailc_ref[0, rows, :]))
        states[c + 1] = states[c] * keep_ref[c : c + 1, :] + dot_halves(
            (kt_hi[:, rows], kt_lo[:, rows]), weighted
        )

    back = dout_ref[...].astype(f32)
    flows = jnp.zeros((8, GW), f32)
    for c in reversed(range(count)):
        rows = slice(c * Q, (c + 1) * Q)
        flows = jnp.where(line == c, jnp.sum(back * states[c + 1], axis=0, keepdims=True), flows)
        delta, cum = delta_ref[0, rows, :], cum_ref[0, rows, :]
        before = halves(states[c])
        after = halves(back)
        k, q = (kq_hi[rows, :STATE], kq_lo[rows, :STATE]), (kq_hi[rows, STATE:], kq_lo[rows, STATE:])
        y_in = dot_halves(q, before)
        w_in = dot_halves(k, after)
        alive = jnp.broadcast_to(mask_ref[rows, 0:1], (Q, 128))
        ending = jnp.broadcast_to(mask_ref[rows, 1:2], (Q, 128))
        ddelta = jnp.zeros((Q, GH), f32)
        dcum = jnp.zeros((Q, GH), f32)
        dys, ws = [], []
        for j in range(GW // 128):
            cols = slice(128 * j, 128 * (j + 1))
            dy, v = dy_ref[rows, cols], v_ref[rows, cols]
            spread = pair_lanes(delta, j)
            w = v * spread
            dy_hi, dy_lo = halves(dy)
            zero = jnp.zeros_like(dy_hi)
            stacked = tuple(
                jnp.concatenate([jnp.where(low, part, zero), jnp.where(low, zero, part)], axis=0)
                for part in (dy_hi, dy_lo)
            )
            inner = dot_halves(stacked, halves(w), NT)
            run = jnp.where(low, cum[:, 2 * j : 2 * j + 1], cum[:, 2 * j + 1 : 2 * j + 2])
            dflow = dy * (jnp.exp(run) * alive)
            tail = jnp.exp(run[Q - 1 : Q, :] - run) * ending
            dw_in = w_in[:, cols] * tail
            one = dflow * y_in[:, cols] - w * dw_in
            turned = []
            for i in (0, 1):
                h = 2 * j + i
                col, row = cum[:, h : h + 1], cumt_ref[h : h + 1, rows]
                turned.append(halves(gramt[rows, :] * jnp.exp(row - col + biast[rows, :])))
                weighed = inner[Q * i : Q * (i + 1), :] * jnp.exp(col - row + bias[rows, :])
                dgram[rows, :] += weighed
                full = weighed * gram[rows, :]
                drow_ref[h : h + 1, rows] = jnp.sum(full, axis=0, keepdims=True)
                keep = low if i == 0 else jnp.logical_not(low)
                full = full + jnp.where(keep, one, 0.0)
                dcum_ref[0, rows, h : h + 1] = jnp.sum(full, axis=1, keepdims=True)
            dw = dot_halves(
                tuple(jnp.concatenate([turned[0][i], turned[1][i]], axis=1) for i in (0, 1)), stacked
            ) + dw_in
            dv_ref[rows, cols] = spread * dw + dir_ref[0:1, cols] * dy
            two = v * dw
            for i in (0, 1):
                keep = low if i == 0 else jnp.logical_not(low)
                h = 2 * j + i
                ddelta_ref[0, rows, h : h + 1] = jnp.sum(jnp.where(keep, two, 0.0), axis=1, keepdims=True)
            dys.append(halves(dflow))
            ws.append(halves(w * tail))
        flowing = tuple(jnp.concatenate([part[i] for part in dys], axis=1) for i in (0, 1))
        leaving = tuple(jnp.concatenate([part[i] for part in ws], axis=1) for i in (0, 1))
        dkq_ref[rows, STATE:] += dot_halves(flowing, before, NT)
        dkq_ref[rows, :STATE] += dot_halves(leaving, after, NT)
        if c:
            back = back * keep_ref[c : c + 1, :] + dot_halves((qt_hi[:, rows], qt_lo[:, rows]), flowing)
    flow_ref[...] = flows

    @pl.when(jnp.logical_and(step == pl.num_programs(0) - 1, final))
    def _():
        for c in range(count):
            rows = slice(c * Q, (c + 1) * Q)
            k, q = kq_ref[rows, :STATE], kq_ref[rows, STATE:]
            dg = dgram[rows, :]
            dkq_ref[rows, STATE:] += dot3(dg, k)
            dkq_ref[rows, :STATE] += dot3(dg.T, q)


def back_local(
    first, last, held, v, dy, kq, delta, cum, cumt, tailc, mask, keep, inc, dout, dirx, segc, segr
):
    length = v.shape[0]
    count = length // Q
    groups = last - first
    if held is None:
        held = (jnp.zeros((length, 2 * STATE), f32), jnp.zeros((length, Q), f32))
    cols = pl.BlockSpec((1, length, GH), lambda g: (g + first, 0, 0))
    wide = pl.BlockSpec((length, GW), lambda g: (0, g + first))
    state = pl.BlockSpec((STATE, GW), lambda g: (0, g + first))
    lines = pl.BlockSpec((8, GW), lambda g: (0, g + first))
    turned = pl.BlockSpec((GH, length), lambda g: (g + first, 0))
    whole = pl.BlockSpec((length, 2 * STATE), lambda g: (0, 0))
    table = pl.BlockSpec((length, Q), lambda g: (0, 0))
    square = pltpu.VMEM((length, Q), f32)
    out_cols = pl.BlockSpec((1, length, GH), lambda g: (g, 0, 0))
    return pl.pallas_call(
        functools.partial(back_kernel, last == NG),
        grid=(groups,),
        in_specs=[
            wide, wide, whole, cols, cols, turned, cols, pl.BlockSpec((length, 8), lambda g: (0, 0)), lines,
            state, state, lines,
            pl.BlockSpec((length, 8), lambda g: (0, 0)),
            pl.BlockSpec((8, length), lambda g: (0, 0)),
            whole, table,
        ],
        out_specs=(
            pl.BlockSpec((length, GW), lambda g: (0, g)), whole, table, out_cols, out_cols,
            pl.BlockSpec((GH, length), lambda g: (g, 0)),
            pl.BlockSpec((8, GW), lambda g: (0, g)),
        ),
        out_shape=(
            jax.ShapeDtypeStruct((length, groups * GW), f32),
            jax.ShapeDtypeStruct((length, 2 * STATE), f32),
            jax.ShapeDtypeStruct((length, Q), f32),
            jax.ShapeDtypeStruct((groups, length, GH), f32),
            jax.ShapeDtypeStruct((groups, length, GH), f32),
            jax.ShapeDtypeStruct((groups * GH, length), f32),
            jax.ShapeDtypeStruct((8, groups * GW), f32),
        ),
        scratch_shapes=[
            square, square, square, square,
            *[pltpu.VMEM((STATE, length), bf16) for _ in range(4)],
            *[pltpu.VMEM((length, 2 * STATE), bf16) for _ in range(2)],
            pltpu.VMEM((count + 1, STATE, GW), f32),
        ],
        compiler_params=params(),
        cost_estimate=pl.CostEstimate(
            flops=groups * 5 * 10**9, bytes_accessed=groups * 5 * 10**6, transcendentals=groups * 10**6
        ),
        name="back_first" if first == 0 else "back_second",
    )(v, dy, kq, delta, cum, cumt, tailc, mask, keep, inc, dout, dirx, segc, segr, *held)


def step_kernel(
    step_ref, par_ref, ddelta_a, ddelta_b, dcum_a, dcum_b, drow_a, drow_b, flow_a, flow_b,
    dstep_ref, small_ref,
):
    length = ddelta_a.shape[1]
    half = ddelta_a.shape[0]
    upper = (iota((Q, Q), 0) <= iota((Q, Q), 1)).astype(f32)
    eye = (iota((Q, Q), 0) == iota((Q, Q), 1)).astype(f32)
    last = iota((Q, 1), 0) == Q - 1
    rate = jnp.exp(par_ref[1:2, :])
    spread = head_onehot()
    wide = half * GW
    flows = dotf(flow_a[...], spread[:, :wide], NT) + dotf(flow_b[...], spread[:, wide:], NT)
    times = jnp.zeros((1, HEADS), f32)
    decays = jnp.zeros((1, HEADS), f32)
    most = jnp.zeros((1, HEADS), f32)
    dstep_ref[...] = jnp.zeros_like(dstep_ref)
    for c in range(length // Q):
        rows = slice(c * Q, (c + 1) * Q)
        turned = jnp.concatenate([drow_a[:, rows], drow_b[:, rows]], axis=0)
        ddelta = jnp.concatenate([part[g, rows, :] for part in (ddelta_a, ddelta_b) for g in range(part.shape[0])], axis=1)
        dcum = jnp.concatenate([part[g, rows, :] for part in (dcum_a, dcum_b) for g in range(part.shape[0])], axis=1)
        dcum = dcum - dotf(eye, turned, NT)
        dcum = dcum + jnp.where(last, flows[c : c + 1, :], 0.0)
        x = step_ref[pl.ds(HALO + c * Q, Q), :HEADS] + par_ref[0:1, :]
        dlog = dotf(upper, dcum) * rate
        decays = decays - jnp.sum(dlog * softplus(x), axis=0, keepdims=True)
        dstep = (ddelta - dlog) * sigmoid(x)
        times = times + jnp.sum(dstep, axis=0, keepdims=True)
        most = jnp.maximum(most, jnp.max(jnp.abs(dstep), axis=0, keepdims=True))
        dstep_ref[rows, :HEADS] = dstep.astype(bf16)
    dstep_ref[pl.ds(length, PAD), :HEADS] = jnp.broadcast_to(most * 1.01, (PAD, HEADS)).astype(bf16)
    small_ref[...] = jnp.zeros_like(small_ref)
    small_ref[0:1, :] = times
    small_ref[1:2, :] = decays


def step_back(rest, pars, first, second):
    length = first[0].shape[1]
    arrays = [part for both in zip(first, second) for part in both]
    shapes = (
        jax.ShapeDtypeStruct((length + PAD, 128), bf16),
        jax.ShapeDtypeStruct((8, HEADS), f32),
    )
    return pl.pallas_call(
        step_kernel,
        grid=(1,),
        in_specs=[steps_of(rest), whole(pars)] + [whole(array) for array in arrays],
        out_specs=tuple(whole(shape) for shape in shapes),
        out_shape=shapes,
        compiler_params=params(),
        cost_estimate=pl.CostEstimate(flops=10**7, bytes_accessed=10**7, transcendentals=10**5),
        name="step_back",
    )(rest, pars, *arrays)


def unconv_kernel(mixed, x_ref, tap_ref, match_ref, dv_ref, dkq_ref, dx_ref, edge_ref, dtap_ref, *held):
    length = match_ref.shape[1]
    count = length // Q
    wide = pl.program_id(0) < mixed
    for buf in held:
        buf[0:HALO, :] = jnp.zeros((HALO, TILE), f32)
        buf[HALO + length :, :] = jnp.zeros((HALO, TILE), f32)
    for j in range(TILE // 128):
        cols = slice(128 * j, 128 * (j + 1))
        sums = [jnp.zeros((1, 128), f32) for _ in range(KW + 1)]
        for c in range(count):
            rows = slice(c * Q, (c + 1) * Q)
            s = conv_sum(x_ref, tap_ref, match_ref, c * Q, Q, cols)
            sig = sigmoid(s)
            dm = jnp.where(wide, dv_ref[rows, cols], dkq_ref[rows, cols])
            ds = dm * (sig * (1.0 + s * (1.0 - sig)))
            sums[KW] = sums[KW] + jnp.sum(ds, axis=0, keepdims=True)
            for k in range(KW):
                e = ds if k == KW - 1 else ds * match_ref[k, rows, :]
                held[k][HALO + c * Q : HALO + (c + 1) * Q, cols] = e
                taken = x_ref[pl.ds(HALO - (KW - 1) + k + c * Q, Q), cols]
                sums[k] = sums[k] + jnp.sum(e * taken, axis=0, keepdims=True)
        for k in range(KW + 1):
            dtap_ref[k : k + 1, cols] = sums[k]

        def placed(start, rows):
            total = None
            for k in range(KW):
                term = tap_ref[k : k + 1, cols] * held[k][pl.ds(start + KW - 1 - k, rows), cols]
                total = term if total is None else total + term
            return total

        edge_ref[0:HALO, cols] = placed(0, HALO)
        most = jnp.zeros((1, 128), f32)
        for c in range(count):
            dx = placed(HALO + c * Q, Q)
            most = jnp.maximum(most, jnp.max(jnp.abs(dx), axis=0, keepdims=True))
            dx_ref[c * Q : (c + 1) * Q, cols] = dx.astype(bf16)
            if c == count - 1:
                edge_ref[HALO:, cols] = dx[Q - HALO :, :]
        dtap_ref[KW + 1 : KW + 2, cols] = most
    dtap_ref[KW + 2 :, :] = jnp.zeros((8 - KW - 2, TILE), f32)


def unconv(first, rest, taps, match, dv, dkq):
    length = match.shape[1]
    high = length + HALO
    mixed = dv.shape[1] // TILE
    tiles = mixed if dkq is None else mixed + 1
    lone = dv if dkq is None else dkq
    return pl.pallas_call(
        functools.partial(unconv_kernel, mixed),
        grid=(tiles,),
        in_specs=[
            pl.BlockSpec((high, TILE), lambda j: (0, j + first)),
            pl.BlockSpec((8, TILE), lambda j: (0, j + first)),
            pl.BlockSpec((KW - 1, length, 128), lambda j: (0, 0, 0)),
            pl.BlockSpec((length, TILE), lambda j: (0, jnp.minimum(j, mixed - 1))),
            pl.BlockSpec((length, TILE), lambda j: (0, 0)),
        ],
        out_specs=(
            pl.BlockSpec((length, TILE), lambda j: (0, j)),
            pl.BlockSpec((2 * HALO, TILE), lambda j: (0, j)),
            pl.BlockSpec((8, TILE), lambda j: (0, j)),
        ),
        out_shape=(
            jax.ShapeDtypeStruct((length + PAD, tiles * TILE), bf16),
            jax.ShapeDtypeStruct((2 * HALO, tiles * TILE), f32),
            jax.ShapeDtypeStruct((8, tiles * TILE), f32),
        ),
        scratch_shapes=[pltpu.VMEM((length + 2 * HALO, TILE), f32) for _ in range(KW)],
        compiler_params=params(),
        cost_estimate=pl.CostEstimate(flops=10**8, bytes_accessed=10**7, transcendentals=10**6),
    )(rest, taps, match, dv, lone)


def adamw(param, grad, moment, square, rate, shrink):
    moment_new = beta_one * moment + (1.0 - beta_one) * grad
    square_new = beta_two * square + (1.0 - beta_two) * grad * grad
    first_corr = 1.0 - beta_one**ADAM_STEP
    second_corr = 1.0 - beta_two**ADAM_STEP
    update = moment_new / first_corr / (jnp.sqrt(square_new / second_corr) + adam_eps)
    return (param - rate * (update + shrink * param), moment_new, square_new)


def shifted(value, axis, by):
    count = lax.axis_size(axis)
    pairs = [(i, i + by) for i in range(count) if 0 <= i + by < count]
    return lax.ppermute(value, axis, pairs)


TOKENS = (((0,), (0,)), ((), ()))


def gathered(value):
    return lax.all_gather(value, "dp", axis=0, tiled=True)


def shard_gathered(value, *earlier):
    count, here = lax.axis_size("shard"), lax.axis_index("shard")
    rows, width = value.shape
    parts = [exchanged(value, "shard", k) for k in range(1, count)]
    held = jnp.zeros((count * rows, width), value.dtype)
    for k, part in enumerate([value] + parts):
        held = lax.dynamic_update_slice(held, after(part, earlier) if k else part, ((here ^ k) * rows, 0))
    return held


def exchanged(value, axis, by):
    return lax.ppermute(value, axis, [(i, i ^ by) for i in range(lax.axis_size(axis))])


def relative(value, block, core):
    base = lax.axis_index("dp") // 2
    length = value.shape[0]
    return [
        lax.dynamic_slice(value, (0, (((j ^ base) * 2) + core) * block), (length, block))
        for j in range(lax.axis_size("dp") // 2)
    ]


def both_cores(value):
    return jnp.concatenate([value, exchanged(value, "dp", 1)], axis=0)


def own_and_partner(value, block):
    core = lax.axis_index("dp") % 2
    return relative(value, block, core), relative(value, block, 1 - core)


def exponent(bound):
    return jnp.ceil(jnp.log2(jnp.maximum(bound, 1e-30)))


def coded(total, power, rows):
    scaled = total * jnp.exp2(15.0 - power)
    if total.shape[0] > rows:
        scaled = jnp.where(iota(total.shape, 0) < rows, scaled, power)
    return scaled.astype(jnp.float16)


def decoded(payload, power, rows):
    if payload.shape[0] == rows:
        return payload.astype(f32) * jnp.exp2(power - 15.0), power
    other = payload[rows : rows + 1].astype(f32)
    return payload.astype(f32) * jnp.exp2(other - 15.0), jnp.maximum(power, other) + 1.0


def after(value, *earlier):
    return lax.optimization_barrier((value, earlier))[0]


def split_plan(order):
    kept, sends = [0], []
    for bit in reversed(order):
        send = [j ^ (1 << bit) for j in kept]
        sends.insert(0, send)
        kept = kept + send
    return kept, sends


def columns_of(blocks, order, pad):
    kept, sends = split_plan(order)
    zeros = [jnp.zeros((blocks[0].shape[0], pad), bf16)] if pad else []
    return (
        jnp.concatenate([blocks[j] for j in kept[: len(sends[0])]] + zeros, axis=1),
        jnp.concatenate([blocks[j] for j in sends[0]] + zeros, axis=1),
    )


class Sum:
    def __init__(self, held, sent, rhs, power, order, pad):
        self.held, self.sent, self.rhs = held, sent, rhs
        self.power = power
        self.order = order
        self.pad = pad
        self.rows = 2 * (sent.shape[1] - pad)
        self.total = None
        self.at = 0

    def prepare(self):
        self.rows //= 2
        if self.total is None:
            part = lax.dot_general(self.sent, self.rhs, TOKENS, preferred_element_type=f32)
        else:
            part = self.total[self.rows : 2 * self.rows + self.pad]
        self.payload = coded(part, self.power, self.rows)

    def send(self):
        self.got = exchanged(self.payload, "dp", 2 << self.order[self.at])
        self.at += 1
        if self.total is None:
            rhs = after(self.rhs, self.payload)
            self.total = lax.dot_general(self.held, rhs, TOKENS, preferred_element_type=f32)

    def take(self, *earlier):
        got, self.power = decoded(after(self.got, earlier), self.power, self.rows)
        self.total = self.total[: self.rows + self.pad] + got

    def more(self):
        return self.at < len(self.order)

    def finish(self):
        while self.more():
            self.prepare()
            self.send()
            self.take()


class ShardSum:
    def __init__(self, sums):
        count, here = lax.axis_size("shard"), lax.axis_index("shard")
        self.rows = sums[0].rows // count
        self.total = jnp.concatenate([one.total for one in sums], axis=1) if len(sums) > 1 else sums[0].total
        self.power = jnp.concatenate([one.power for one in sums], axis=1) if len(sums) > 1 else sums[0].power
        taken = (self.rows + sums[0].pad, self.total.shape[1])
        self.payloads = [
            coded(lax.dynamic_slice(self.total, ((here ^ k) * self.rows, 0), taken), self.power, self.rows)
            for k in range(1, count)
        ]
        self.parts = [exchanged(part, "shard", k + 1) for k, part in enumerate(self.payloads)]

    def take(self, *earlier):
        here = lax.axis_index("shard")
        result = lax.dynamic_slice(self.total, (here * self.rows, 0), (self.rows, self.total.shape[1]))
        for part in self.parts:
            result = result + decoded(after(part, earlier), self.power, self.rows)[0][: self.rows]
        return result


class Everywhere:
    def __init__(self, value):
        self.value = value
        self.steps = []
        for axis in ("dp", "shard"):
            count, by = lax.axis_size(axis), 1
            while by < count:
                self.steps.append((axis, by))
                by *= 2

    def send(self):
        self.got = exchanged(self.value, *self.steps.pop(0))

    def take(self, *earlier):
        self.value = self.value + after(self.got, earlier)

    def finish(self):
        while self.steps:
            self.send()
            self.take()
        return self.value


def carried(state, half, factor, by):
    incoming = shifted(half, "shard", by)
    for _ in range(1, lax.axis_size("shard") - 1):
        passed = (state + factor * incoming.astype(f32)).astype(bf16)
        incoming = shifted(passed, "shard", by)
    return incoming


def both_with_most(rows):
    length = rows.shape[0] - PAD
    arrived = exchanged(rows, "dp", 1)
    most = jnp.maximum(rows[length : length + 1], arrived[length : length + 1]).astype(f32)
    return jnp.concatenate([rows[:length], arrived[:length]], axis=0), most


def mended(dx, edge, dtap, length):
    last = edge[HALO:] + shifted(edge[:HALO], "shard", -1)
    most = jnp.maximum(dtap[KW + 1 : KW + 2], jnp.max(jnp.abs(last), axis=0, keepdims=True)) * 1.01
    tail = jnp.concatenate([last, jnp.broadcast_to(most, (PAD, most.shape[1]))], axis=0).astype(bf16)
    return lax.dynamic_update_slice(dx, tail, (length - HALO, 0)), dtap


def rest_sums(both, bound, in_columns, orders):
    middle = both.shape[1] // 256 * 128
    power = exponent(bound)
    return [
        Sum(*in_columns[0], both[:, :middle], power[:, :middle], orders[0], PAD),
        Sum(*in_columns[1], both[:, middle:], power[:, middle:], orders[1], PAD),
    ]


def shards(
    hidden_in, cotangent, segment_ids,
    param_prenorm, param_inputs, param_kernel, param_offsets, param_timestep, param_decays,
    param_direct, param_gating, param_outputs,
    moment_prenorm, moment_inputs, moment_kernel, moment_offsets, moment_timestep, moment_decays,
    moment_direct, moment_gating, moment_outputs,
    square_prenorm, square_inputs, square_kernel, square_offsets, square_timestep, square_decays,
    square_direct, square_gating, square_outputs,
):
    length, width = hidden_in.shape
    own_inputs = param_inputs.astype(bf16)
    spare = -(param_inputs.shape[1] - DI) % 128
    upstream = cotangent.astype(bf16)
    own_rows = param_inputs.shape[0]
    most = jnp.broadcast_to((jnp.max(jnp.abs(cotangent)) * 1.01).astype(bf16), (own_rows, 1))
    rest_rows = shard_gathered(
        jnp.concatenate([own_inputs[:, DI:], most, jnp.zeros((own_rows, spare - 1), bf16)], axis=1),
    )
    rest_w = gathered(rest_rows)

    seg = segment_ids.astype(f32)
    ends = jnp.pad(seg[length - HALO :], (0, width - HALO))[None, :]
    halo = shifted(
        jnp.concatenate([hidden_in[length - HALO :], jnp.broadcast_to(ends, (HALO, width))], axis=0),
        "shard", 1,
    )
    rim_seg = jnp.where(lax.axis_index("shard") == 0, -1.0, halo[HALO, :HALO])
    rim = rim_seg[HALO - 1]
    all_segs = jnp.concatenate([rim_seg, seg])
    match = jnp.stack(
        [
            (all_segs[HALO - (KW - 1) + k : HALO - (KW - 1) + k + length] == seg).astype(f32)
            for k in range(KW - 1)
        ]
    )
    match = jnp.broadcast_to(match[:, :, None], (KW - 1, length, 128))
    chunks = seg.reshape(-1, Q)
    before = jnp.concatenate([rim[None], chunks[:-1, Q - 1]])
    mask = jnp.stack(
        [
            (chunks == before[:, None]).reshape(-1),
            (chunks == chunks[:, Q - 1 :]).reshape(-1),
            seg == rim,
            seg == seg[length - 1],
        ]
        + [seg < -1.0] * 4,
        axis=1,
    ).astype(f32)
    segc = jnp.broadcast_to(seg[:, None], (length, 8))
    segr = jnp.broadcast_to(seg[None, :], (8, length))

    taps = jnp.concatenate([param_kernel, param_offsets[None, :], jnp.zeros((8 - KW - 1, CH), f32)], axis=0)
    pars = jnp.concatenate([param_timestep[None, :], param_decays[None, :], jnp.zeros((6, HEADS), f32)], axis=0)
    dirx = jnp.broadcast_to(jnp.repeat(param_direct, HEAD_DIM)[None, :], (8, DI))
    gam = jnp.broadcast_to(param_gating[None, :], (8, DI))

    hidden = jnp.concatenate([halo[:HALO], hidden_in], axis=0)
    inv = lax.rsqrt(jnp.mean(hidden * hidden, axis=1, keepdims=True) + norm_eps)
    normed = (hidden * inv * param_prenorm).astype(bf16)
    own_normed = normed[HALO:]

    groups = lax.axis_size("shard")
    spots = [bit for bit in range(20) if (2 << bit) < lax.axis_size("dp")]
    orders = (spots, spots[::-1])
    in_block, out_block = groups * param_inputs.shape[0], groups * param_outputs.shape[0]
    up_both = both_cores(after(upstream, rest_rows))
    own_blocks, partner_blocks = own_and_partner(own_normed, in_block)
    arrived = exchanged(jnp.concatenate(partner_blocks, axis=1), "dp", 1)
    both_blocks = [
        jnp.concatenate([one, arrived[:, j * in_block : (j + 1) * in_block]], axis=0)
        for j, one in enumerate(own_blocks)
    ]
    in_columns = [columns_of(both_blocks, order, PAD) for order in orders]
    norm_bound = 2.02 * length * width**0.5 * jnp.max(jnp.abs(param_prenorm))
    early = (match, mask, segc, segr, taps, pars, dirx, gam, up_both, norm_bound, in_columns, normed)
    gate_rows = shard_gathered(after(own_inputs[:, :DI], rest_rows), early)
    gate_w = gathered(gate_rows)
    rest_w = after(rest_w, early)

    rest = jnp.dot(normed, rest_w, preferred_element_type=f32)
    delta, cum, cumt, tailc, taild, infd, keep, factor = prep(rest, pars, mask)
    v, kq, state, state_half = conv_state(rest, taps, match, taild)
    out_rows = shard_gathered(after(param_outputs.astype(bf16), gate_rows), v)
    out_w = gathered(out_rows)
    state = after(state, out_rows)
    incoming = carried(state, state_half, factor[0:1], 1)
    y = local_out(v, kq, delta, cum, cumt, mask, keep, segc, segr)
    gate_w = after(gate_w, y)
    z = jnp.dot(own_normed, gate_w, preferred_element_type=f32)
    out_w = after(out_w, z)
    back_gated = lax.dot_general(upstream, out_w, NT, preferred_element_type=f32)
    tokens = length * lax.axis_size("dp") * groups
    cotangent_most = jnp.max(rest_w[:, param_inputs.shape[1] - DI]).astype(f32)
    out_power = exponent(1.02 * tokens * DI**0.5 * jnp.max(jnp.abs(param_gating)) * cotangent_most)
    place = lax.axis_index("dp")
    block = out_block if out_block % 128 == 0 and len(spots) == 2 else 0
    at = jnp.stack([place // 2, place % 2]).astype(jnp.int32)
    gated, blocks, dy, dz, dinc, dinc_half, small = gate(
        block, at, y, v, z, back_gated, kq, incoming, infd, dirx, gam
    )

    outgoing = carried(dinc, dinc_half, factor[0:1], -1)
    if not block:
        own_blocks, partner_blocks = own_and_partner(gated, out_block)
        blocks = jnp.stack([*columns_of(own_blocks, spots, 0), *columns_of(partner_blocks, spots, 0)])
    arrived = exchanged(blocks[2:], "dp", 1)
    out_columns = [jnp.concatenate([blocks[i], arrived[i]], axis=0) for i in range(2)]
    dz_most = jnp.broadcast_to(small[2:3] * 1.01, (PAD, DI)).astype(bf16)
    dz = lax.dynamic_update_slice(dz, dz_most, (length, 0))
    dz_both, dz_bound = both_with_most(dz)
    block_out = hidden_in + jnp.dot(gated, out_w, preferred_element_type=f32)
    out_sum = Sum(*out_columns, up_both, out_power, spots, 0)
    gate_sum = Sum(*in_columns[1], dz_both, exponent(norm_bound * dz_bound), spots[::-1], PAD)
    first_sums = [out_sum, gate_sum]
    for one in first_sums:
        one.prepare()
        one.send()
    back_normed = lax.dot_general(dz, gate_w, NT, preferred_element_type=f32)
    outgoing = after(
        outgoing, out_sum.payload, gate_sum.payload, out_sum.total, gate_sum.total, back_normed, block_out
    )

    ssm = (kq, delta, cum, cumt, tailc, mask, keep, incoming)
    half = NG // 2
    dv1, *held1 = back_local(0, half, None, v, dy, *ssm, outgoing, dirx, segc, segr)
    for one in first_sums:
        one.take(dv1)
        if one.more():
            one.prepare()
            one.send()
    dv1 = after(dv1, *[one.payload for one in first_sums])
    drest1, dtap1 = mended(*unconv(0, rest, taps, match, dv1, None), length)
    both1, bound1 = both_with_most(drest1)
    sums1 = rest_sums(both1, norm_bound * bound1, in_columns, orders)
    for one in first_sums:
        one.take(dv1, both1)
        one.finish()
    shard_out, shard_gate = ShardSum([out_sum]), ShardSum([gate_sum])
    for one in sums1:
        one.prepare()
        one.send()
    dy = after(
        dy, [one.payload for one in sums1], [one.total for one in sums1], shard_out.payloads, shard_gate.payloads
    )
    dv2, *held2 = back_local(half, NG, held1[:2], v, dy, *ssm, outgoing, dirx, segc, segr)
    for one in sums1:
        one.take(dv2)
        if one.more():
            one.prepare()
            one.send()
    dv2 = after(dv2, *[one.payload for one in sums1])
    dstep, small_step = step_back(rest, pars, held1[2:], held2[2:])
    drest2, dtap2 = mended(*unconv(dv1.shape[1] // TILE, rest, taps, match, dv2, held2[0]), length)
    drest2 = jnp.concatenate([drest2, dstep], axis=1)
    both2, bound2 = both_with_most(drest2)
    sums2 = rest_sums(both2, norm_bound * bound2, in_columns, orders)
    for one in sums2:
        one.prepare()
        one.send()
    for one in sums1:
        one.take(dv2, dstep)
        one.finish()
    shard1 = ShardSum(sums1)
    drest1, drest2 = after((drest1, drest2), shard1.payloads, [two.payload for two in sums2])
    wide1 = drest1.shape[1]
    back_normed = back_normed + lax.dot_general(drest1, rest_w[:, :wide1], NT, preferred_element_type=f32)
    back_normed = back_normed + lax.dot_general(drest2, rest_w[:, wide1:], NT, preferred_element_type=f32)
    back_normed = back_normed[:length]
    own_inv = inv[HALO:]
    scaled = hidden_in * own_inv
    gained = back_normed * param_prenorm
    hidden_grad = cotangent + own_inv * (
        gained - scaled * jnp.mean(gained * scaled, axis=1, keepdims=True)
    )
    grad_prenorm = jnp.sum(back_normed * scaled, axis=0)

    dtap = jnp.concatenate([dtap1, dtap2], axis=1)
    pieces = [
        grad_prenorm,
        dtap[:KW].reshape(-1),
        dtap[KW],
        small_step[0],
        small_step[1],
        jnp.sum(small[1].reshape(HEADS, HEAD_DIM), axis=1),
        small[0],
    ]
    flat = jnp.concatenate(pieces)
    count = flat.shape[0]
    lines = -(-count // 1024) * 8
    everywhere = Everywhere(jnp.pad(flat, (0, lines * 128 - count)).reshape(lines, 128))
    everywhere.send()
    for one in sums2:
        one.take(back_normed)
        if one.more():
            one.prepare()
            one.send()
    sent = [one.payload for one in sums2]
    everywhere.take(sent)
    everywhere.send()
    for one in sums2:
        one.take(everywhere.value)
        one.finish()
    shard2 = ShardSum(sums2)
    sent = shard2.payloads
    everywhere.take(sent)
    total = everywhere.finish().reshape(-1)
    grad_outputs = shard_out.take(sent)
    grad_gate = shard_gate.take(sent)
    grad_rest = jnp.concatenate([shard1.take(sent), shard2.take()], axis=1)
    grad_inputs = jnp.concatenate([grad_gate, grad_rest[:, : param_inputs.shape[1] - DI]], axis=1)
    found, at = [], 0
    for piece in pieces:
        found.append(total[at : at + piece.shape[0]])
        at += piece.shape[0]
    grad_prenorm, grad_kernel, grad_offsets, grad_timestep, grad_decays, grad_direct, grad_gating = found
    grad_kernel = grad_kernel.reshape(KW, CH)

    params = (
        param_prenorm, param_inputs, param_kernel, param_offsets, param_timestep, param_decays,
        param_direct, param_gating, param_outputs,
    )
    moments = (
        moment_prenorm, moment_inputs, moment_kernel, moment_offsets, moment_timestep, moment_decays,
        moment_direct, moment_gating, moment_outputs,
    )
    squares = (
        square_prenorm, square_inputs, square_kernel, square_offsets, square_timestep, square_decays,
        square_direct, square_gating, square_outputs,
    )
    grads = (
        grad_prenorm, grad_inputs, grad_kernel, grad_offsets, grad_timestep, grad_decays,
        grad_direct, grad_gating, grad_outputs,
    )
    updated = [
        adamw(params[i], grads[i], moments[i], squares[i], rate_table[i], shrink_table[i])
        for i in range(9)
    ]
    return (
        (block_out, hidden_grad)
        + grads
        + tuple(u[0] for u in updated)
        + tuple(u[1] for u in updated)
        + tuple(u[2] for u in updated)
    )


def solution(mesh):
    rows = P(("dp", "shard"), None)
    member = (P(), rows, P(), P(), P(), P(), P(), P(), rows)

    return jax.shard_map(
        shards,
        mesh=mesh,
        in_specs=(rows, rows, P(("dp", "shard"))) + member * 3,
        out_specs=(rows, rows) + member * 4,
        check_vma=False,
    )
```
